32 devices in a mesh: space: 16 (over z, y, core), frame: 2 (over x).
Axes of the slice: x: 2, y: 2, z: 4, core: 2. Of those that a mesh axis runs over, the one named last changes fastest.
Arguments:
- raw_sequence: bfloat16 [4, 256, 512], P('frame', 'space'), may hold values from -12 to 12
- tile_shifts_grid: int32 [4, 2, 16, 32], P('frame', None, 'space'), may hold values from -16 to 16, as said below
- color_layer_kernel: bfloat16 [32, 36], replicated, may hold values from -1 to 1
- color_layer_offset: float32 [32], replicated, may hold values from -0.5 to 0.5
- log_variance_spectrum: float32 [256], replicated, may hold values from 4 to 8
- goal_features: bfloat16 [32, 128, 256], P(None, 'space', 'frame'), may hold values from -3 to 3
Outputs:
- merged: float32 [256, 512], P('space', 'frame')
- grad_weight: float32 [32, 36], replicated
- grad_bias: float32 [32], replicated
- grad_log_noise: float32 [256], replicated
The draws below stay inside these ranges and needn't reach their ends.
Inputs may be any that keep to these rules, and one draw needn't show every extreme that they name: tile_shifts_grid[0] (the reference frame) is zero; the other frames' displacements reach both ends of the range.
All inputs are finite; a program needn't handle non-finite values.
Results may differ from the reference program's by a relative error of at most 0.00033.
Values may be sent and summed in bfloat16 or wider, within the bound.
No kernel may reach another device: no remote copies, remote signals or barrier semaphores. Data moves between devices by JAX's collectives and lax.ppermute only.
A program may use at most 64 MiB of HBM per device.

```python
import math
import jax
import jax.numpy as jnp
from jax import lax

LARGEST_SHIFT = 16
CH = 32
FREQ = 256
FRAMES = 4
HEIGHT = 256
WIDTH = 512


def draw_raw_sequence(key, part):
    rows_pos = jnp.arange(HEIGHT, dtype=jnp.float32)
    rising = 1.0 + 2.0 * rows_pos / (HEIGHT - 1)
    values = jax.random.normal(key, (FRAMES, HEIGHT, WIDTH), jnp.float32) * rising[:, None]
    return jnp.clip(values, -12.0, 12.0).astype(jnp.bfloat16)


def draw_tile_shifts_grid(key, part):
    values = jax.random.randint(key, (FRAMES, 2, HEIGHT // 16, WIDTH // 16), -LARGEST_SHIFT, LARGEST_SHIFT + 1, dtype=jnp.int32)
    values = values.at[1, 0, 0, 0].set(LARGEST_SHIFT).at[1, 0, 1, 0].set(-LARGEST_SHIFT)
    values = values.at[1, 1, 0, 0].set(LARGEST_SHIFT).at[1, 1, 0, 1].set(-LARGEST_SHIFT)
    alternate = (jnp.arange(FRAMES, dtype=jnp.int32) > 0).astype(jnp.int32)
    return values * alternate[:, None, None, None]


def block_levels(rng, shape, shards, smallest, high):
    def one(axis_at, shards_of):
        heights = jax.random.uniform(jax.random.fold_in(jax.random.fold_in(rng, 6), axis_at), (shards_of,), jnp.float32, smallest / len(shards), high / len(shards))
        return jnp.repeat(jnp.exp(heights), shape[axis_at] // shards_of).reshape((-1,) + (1,) * (len(shape) - axis_at - 1))

    gain = one(*shards[0])
    for cut in shards[1:]:
        gain = gain * one(*cut)
    return gain


def scatter_about(key, dims, scale, limit, cuts=(), kind=jnp.bfloat16):
    entries = scale * jax.random.normal(key, dims, jnp.float32)
    if cuts:
        entries = entries * block_levels(key, dims, cuts, -0.22, 0.18)
    return jnp.clip(entries, -limit, limit).astype(kind)


def setup_inputs(seed: int = 0) -> dict:
    key_list = jax.random.split(jax.random.key(seed), 7)
    raw_sequence = draw_raw_sequence(jax.random.fold_in(key_list[6], 71), 0)
    tile_shifts_grid = draw_tile_shifts_grid(jax.random.fold_in(key_list[6], 71), 0)
    color_layer_kernel = scatter_about(key_list[2], (CH, 36), 36 ** -0.5, 1.0)
    color_layer_offset = jnp.clip(jax.random.uniform(key_list[3], (CH,), jnp.float32, -0.5, 0.5), -0.5, 0.5)
    log_variance_spectrum = jnp.clip(jax.random.uniform(key_list[4], (FREQ,), jnp.float32, 4.0, 8.0), 4.0, 8.0)
    goal_features = scatter_about(key_list[5], (CH, HEIGHT // 2, WIDTH // 2), 0.5, 3.0, ((1, 16), (2, 2)))
    return dict(raw_sequence=raw_sequence, tile_shifts_grid=tile_shifts_grid, color_layer_kernel=color_layer_kernel, color_layer_offset=color_layer_offset, log_variance_spectrum=log_variance_spectrum, goal_features=goal_features)


def build_table():
    freq = jnp.arange(256, dtype=jnp.int32)
    high = freq // 16
    low = freq % 16
    phase_int = (high[:, None] * high[None, :] + low[:, None] * low[None, :]) % 16
    phase_vals = phase_int.astype(jnp.float32) * (2.0 * math.pi / 16.0)
    return jnp.concatenate([jnp.cos(phase_vals), -jnp.sin(phase_vals)], axis=0)


def cut_patches(picture):
    leading = picture.shape[:-2]
    height = picture.shape[-2]
    breadth = picture.shape[-1]
    depth = len(leading)
    blocked = picture.reshape(leading + (height // 16, 16, breadth // 16, 16))
    order = tuple(range(depth)) + (depth + 1, depth + 3, depth, depth + 2)
    return jnp.transpose(blocked, order).reshape(leading + (256, height // 16, breadth // 16))


def from_tiles(tiled):
    tile_rows = tiled.shape[1]
    tile_cols = tiled.shape[2]
    blocked = tiled.reshape(16, 16, tile_rows, tile_cols)
    return jnp.transpose(blocked, (2, 0, 3, 1)).reshape(tile_rows * 16, tile_cols * 16)


def align_blocks(padded_frame, shifts, padding_halo_width):
    tile_rows = shifts.shape[1]
    tile_cols = shifts.shape[2]
    stride = padded_frame.shape[1]
    within = jnp.arange(16, dtype=jnp.int32)
    row_base = jnp.arange(tile_rows, dtype=jnp.int32) * 16
    col_base = jnp.arange(tile_cols, dtype=jnp.int32) * 16
    row_index = within[:, None, None, None] + row_base[None, None, :, None] + shifts[0][None, None] + padding_halo_width
    col_index = within[None, :, None, None] + col_base[None, None, None, :] + shifts[1][None, None] + padding_halo_width
    flat_index = (row_index * stride + col_index).reshape(256, tile_rows, tile_cols).astype(jnp.int32)
    return jnp.take(padded_frame.reshape(-1), flat_index, axis=0)


def wiener_frame(base_patches, blocks, fourier, noise_power):
    residual = base_patches - blocks
    spectrum = jnp.einsum('kp,prc->krc', fourier, residual, precision=lax.Precision.HIGHEST)
    real_part = spectrum[:256]
    imag_part = spectrum[256:]
    energy = real_part * real_part + imag_part * imag_part
    weight = energy / (energy + noise_power[:, None, None])
    shaped = jnp.concatenate([weight * real_part, weight * imag_part], axis=0)
    restored = jnp.einsum('kp,krc->prc', fourier, shaped, precision=lax.Precision.HIGHEST) / 256.0
    return blocks + restored, real_part, imag_part, weight


def noise_step(running, slope_spec, real_part, imag_part, weight):
    d_weight = (slope_spec[:256] * real_part + slope_spec[256:] * imag_part) / 256.0
    return running - jnp.sum(weight * (1.0 - weight) * d_weight, axis=(1, 2))


def pack_bayer(picture):
    height = picture.shape[0]
    breadth = picture.shape[1]
    blocked = picture.reshape(height // 2, 2, breadth // 2, 2)
    return jnp.transpose(blocked, (1, 3, 0, 2)).reshape(4, height // 2, breadth // 2)


def unpack_bayer(packed):
    height = packed.shape[1]
    breadth = packed.shape[2]
    blocked = packed.reshape(2, 2, height, breadth)
    return jnp.transpose(blocked, (2, 0, 3, 1)).reshape(2 * height, 2 * breadth)


def make_patches(framed, height, breadth):
    pieces = [framed[:, tap_row:tap_row + height, tap_col:tap_col + breadth] for tap_row in range(3) for tap_col in range(3)]
    return jnp.stack(pieces, axis=0).reshape(9 * framed.shape[0], height * breadth)


def demosaic_grads(framed, color_layer_kernel, color_layer_offset, goal_features, inv_pixels):
    height = framed.shape[1] - 2
    breadth = framed.shape[2] - 2
    patches = make_patches(framed, height, breadth)
    preact = jnp.dot(color_layer_kernel, patches, preferred_element_type=jnp.float32) + color_layer_offset[:, None]
    sigmoid_vals = jax.nn.sigmoid(preact)
    residual = preact * sigmoid_vals - goal_features.reshape(goal_features.shape[0], height * breadth).astype(jnp.float32)
    slope_vals = residual * inv_pixels * (sigmoid_vals * (1.0 + preact * (1.0 - sigmoid_vals)))
    grad_bias = jnp.sum(slope_vals, axis=1)
    slope_bf = slope_vals.astype(jnp.bfloat16)
    grad_weight = lax.dot_general(slope_bf, patches, (((1,), (1,)), ((), ())), preferred_element_type=jnp.float32)
    return grad_weight, grad_bias, slope_bf.reshape(slope_bf.shape[0], height, breadth)


def packed_slope(framed_slope, color_layer_kernel):
    height = framed_slope.shape[1] - 2
    breadth = framed_slope.shape[2] - 2
    flat_slope = framed_slope.reshape(framed_slope.shape[0], (height + 2) * (breadth + 2))
    grid_vals = jnp.dot(color_layer_kernel.T, flat_slope, preferred_element_type=jnp.float32)
    grid_vals = grid_vals.reshape(36, height + 2, breadth + 2)
    summed = jnp.zeros((4, height, breadth), jnp.float32)
    for tap_row in range(3):
        for tap_col in range(3):
            first = (tap_row * 3 + tap_col) * 4
            summed = summed + grid_vals[first:first + 4, 2 - tap_row:2 - tap_row + height, 2 - tap_col:2 - tap_col + breadth]
    return summed


def reference(raw_sequence, tile_shifts_grid, color_layer_kernel, color_layer_offset, log_variance_spectrum, goal_features):
    fourier = build_table()
    noise_power = jnp.exp(log_variance_spectrum)
    base_patches = cut_patches(raw_sequence[0]).astype(jnp.float32)
    padded_strip = jnp.pad(raw_sequence, ((0, 0), (LARGEST_SHIFT, LARGEST_SHIFT), (LARGEST_SHIFT, LARGEST_SHIFT)))

    def frame_pass(frame_pix, frame_shift):
        blocks = align_blocks(frame_pix, frame_shift, LARGEST_SHIFT).astype(jnp.float32)
        return wiener_frame(base_patches, blocks, fourier, noise_power)

    def forward_step(summed, inputs):
        outcome = frame_pass(inputs[0], inputs[1])
        return summed + outcome[0], None

    start_sum = jnp.zeros((256, HEIGHT // 16, WIDTH // 16), jnp.float32)
    summed, _ = lax.scan(forward_step, start_sum, (padded_strip, tile_shifts_grid))
    merged = from_tiles(summed / FRAMES)
    packed = pack_bayer(merged).astype(jnp.bfloat16)
    framed = jnp.pad(packed, ((0, 0), (1, 1), (1, 1)))
    grad_weight, grad_bias, slope_bf = demosaic_grads(framed, color_layer_kernel, color_layer_offset, goal_features, 1.0 / (HEIGHT * WIDTH // 4))
    framed_slope = jnp.pad(slope_bf, ((0, 0), (1, 1), (1, 1)))
    merged_slope = unpack_bayer(packed_slope(framed_slope, color_layer_kernel))
    slope_spec = jnp.einsum('kp,prc->krc', fourier, cut_patches(merged_slope) / FRAMES, precision=lax.Precision.HIGHEST)

    def backward_step(running, inputs):
        outcome = frame_pass(inputs[0], inputs[1])
        return noise_step(running, slope_spec, outcome[1], outcome[2], outcome[3]), None

    grad_log_noise, _ = lax.scan(backward_step, jnp.zeros((256,), jnp.float32), (padded_strip, tile_shifts_grid))
    return merged, grad_weight, grad_bias, grad_log_noise
```

```python
import functools
import math

import jax
import jax.numpy as jnp
import numpy as np
from jax import lax
from jax.experimental import pallas as pl
from jax.experimental.pallas import tpu as pltpu
from jax.sharding import PartitionSpec as P

TILE = 16
LANES = 128
HIGH = lax.Precision.HIGHEST


def dot(a, b, dims=((1,), (0,)), precision=None):
    return lax.dot_general(
        a, b, (dims, ((), ())), precision=precision, preferred_element_type=jnp.float32
    )


def tables():
    angle = 2.0 * math.pi / TILE * (np.outer(np.arange(TILE), np.arange(TILE)) % TILE)
    cos16, sin16 = np.cos(angle), np.sin(angle)
    eye8, eye16 = np.eye(8), np.eye(16)
    bc, bs = np.kron(eye8, cos16), np.kron(eye8, sin16)
    cols = np.concatenate([bc, bs], axis=1)
    back = np.concatenate([bc, bs], axis=0)
    rows = np.block([[bc, -bs], [-bs, -bc]])
    split = np.zeros((256, 256))
    for x in range(256):
        split[x, (x % 2) * 128 + x // 2] = 1.0
    wide = np.concatenate([np.kron(eye16, cos16), np.kron(eye16, sin16)], axis=1)
    f32 = np.float32
    return cols.astype(f32), back.astype(f32), rows.astype(f32), split, (split.T @ wide).astype(f32)


def tap_tables():
    place = np.zeros((36, 10, 144))
    back = np.zeros((96, 10, 36))
    pick = np.zeros((256, 128))
    for a in range(3):
        for b in range(3):
            for p in range(2):
                for q in range(2):
                    tap = (3 * a + b) * 4 + 2 * p + q
                    pick[(q * 3 + b) * 24 + 2 * a + p, tap] = 1.0
                    for sy in range(10):
                        r = 2 * (sy + a) + p
                        place[tap, sy, (q * 3 + b) * 24 + r] = 1.0
                        if 4 <= r < 20:
                            back[(q * 3 + b) * 16 + r - 4, sy, tap] = 1.0
    return place, back, pick.astype(np.float32)


def kernel(
    dims,
    y_ref,
    yc_ref,
    yf_ref,
    y2_ref,
    y3_ref,
    *refs,
):
    nf, fl, G, T, nsc, rs, n_space, inv_pixels = dims
    F = nf * fl
    W = G * LANES
    half = W // 2
    goal_refs = refs[:nf]
    (
        cols_ref,
        back_ref,
        rows_ref,
        split_ref,
        wide_ref,
        pick_ref,
        big_ref,
        bigt_ref,
        offs_ref,
        var_ref,
        merged_ref,
        out_ref,
        x_ref,
        goal_ref,
        sv_ref,
        sm_ref,
        sem,
        sa_ref,
        sb_ref,
        sk_ref,
        h_ref,
        mm_ref,
    ) = refs[nf:]
    s = lax.axis_index("space")
    fr = lax.axis_index("frame")
    odd = lax.rem(s, 2)
    odd2 = lax.rem(lax.div(s, 2), 2)
    raw_rows = F * G * TILE
    m_aux = 64 * nsc + rs
    used = rs

    for ref, band in ((y_ref, 1), (yc_ref, 2 - 2 * odd), (yf_ref, 2 * odd)):
        for j in range(nf):
            first = raw_rows + j * m_aux + 64 * nsc
            val = ref[first : first + used, :].astype(jnp.float32).astype(jnp.int32)
            at = (band * nf + lax.rem(fr + j, nf)) * used
            sv_ref[pl.ds(pl.multiple_of(at, 8), used), :] = val
    shift_copy = pltpu.make_async_copy(sv_ref, sm_ref, sem)
    shift_copy.start()

    slots = (
        (y_ref, 2),
        (yc_ref, 3 - 2 * odd),
        (yf_ref, 1 + 2 * odd),
        (y2_ref, 4 - 4 * odd2),
        (y3_ref, 4 * odd2),
    )

    def fill(k, carry):
        to = lax.rem(k + fr * (fl * G), F * G)
        for ref, slot in slots:
            block = ref[pl.ds(pl.multiple_of(k * TILE, TILE), TILE), :].astype(jnp.float32)
            x_ref[to, pl.ds(pl.multiple_of(slot * TILE, TILE), TILE), :] = block
        return carry

    lax.fori_loop(0, F * G, fill, 0, unroll=min(F * G, 16))

    for j in range(nf):
        at = pl.multiple_of(lax.rem(fr + j, nf) * (nsc * LANES), LANES)
        for r in range(8):
            goal_ref[r + 1, :, pl.ds(at, nsc * LANES)] = goal_refs[j][r].astype(jnp.float32)
        for ref, row, top in ((yc_ref, 9 - 9 * odd, odd), (yf_ref, 9 * odd, 1 - odd)):
            for c in range(nsc):
                first = raw_rows + j * m_aux + (top * nsc + c) * 32
                val = ref[pl.ds(pl.multiple_of(first, 16), 32), :].astype(jnp.float32)
                goal_ref[row, :, pl.ds(pl.multiple_of(at + c * LANES, LANES), LANES)] = val

    sa_ref[...] = jnp.zeros_like(sa_ref)
    sb_ref[...] = jnp.zeros_like(sb_ref)
    sk_ref[...] = jnp.zeros_like(sk_ref)
    h_ref[...] = jnp.zeros_like(h_ref)
    lane = lax.broadcasted_iota(jnp.int32, (TILE, LANES), 1)
    lane_tile = lane // TILE
    low = lane < 64
    var = var_ref[...]
    per = 16 // G
    chunks = F * G // 16
    shift_copy.wait()

    def forward(n, carry):
        b = lax.div(n, chunks)
        c = lax.rem(n, chunks)
        diffs = []
        for q in range(16):
            f = c * per + q // G
            g = q % G
            j = lax.div(f, fl)
            l = lax.rem(f, fl)
            row0 = (b * nf + j) * used
            blk = jnp.zeros((TILE, LANES), jnp.float32)
            for t in range(8):
                at = l * (2 * T) + 8 * g + t
                dy = sm_ref[row0 + lax.div(at, LANES), lax.rem(at, LANES)]
                at = at + T
                dx = sm_ref[row0 + lax.div(at, LANES), lax.rem(at, LANES)]
                start = TILE * (b + 1) + dy
                win = x_ref[f * G + g, pl.ds(start, TILE), :]
                if t == 0:
                    if g > 0:
                        other = x_ref[f * G + g - 1, pl.ds(start, TILE), :]
                    else:
                        other = jnp.zeros((TILE, LANES), jnp.float32)
                    win = jnp.where(low, win, other)
                if t == 7:
                    if g < G - 1:
                        other = x_ref[f * G + g + 1, pl.ds(start, TILE), :]
                    else:
                        other = jnp.zeros((TILE, LANES), jnp.float32)
                    win = jnp.where(low, other, win)
                win = pltpu.roll(win, (LANES - dx) & (LANES - 1), 1)
                blk = win if t == 0 else jnp.where(lane_tile == t, win, blk)
            at = pl.multiple_of((b * G + g) * TILE, TILE)
            sk_ref[pl.ds(at, TILE), :] += blk
            base = x_ref[g, pl.ds(pl.multiple_of(TILE * (b + 1), TILE), TILE), :]
            diffs.append(base - blk)
        pq = dot(jnp.concatenate(diffs, axis=0), cols_ref[...], precision=HIGH)
        top = jnp.concatenate([pq[:128, :128], pq[128:, :128]], axis=1)
        bottom = jnp.concatenate([pq[:128, 128:], pq[128:, 128:]], axis=1)
        ri = dot(rows_ref[...], jnp.concatenate([top, bottom], axis=0), precision=HIGH)
        for g in range(G):
            a_sum = jnp.zeros((TILE, LANES), jnp.float32)
            b_sum = jnp.zeros((TILE, LANES), jnp.float32)
            hr = jnp.zeros((TILE, LANES), jnp.float32)
            hi = jnp.zeros((TILE, LANES), jnp.float32)
            for u in range(per):
                q = u * G + g
                r0 = (q % 8) * TILE
                c0 = (q // 8) * LANES
                re = ri[r0 : r0 + TILE, c0 : c0 + LANES]
                im = ri[128 + r0 : 128 + r0 + TILE, c0 : c0 + LANES]
                energy = re * re + im * im
                weight = energy / (energy + var)
                wr = weight * re
                wi = weight * im
                rest = 1.0 - weight
                a_sum += wr
                b_sum += wi
                hr += wr * rest
                hi += wi * rest
            at = pl.multiple_of((b * G + g) * TILE, TILE)
            sa_ref[pl.ds(at, TILE), :] += a_sum
            sb_ref[pl.ds(at, TILE), :] += b_sum
            h_ref[b, 0, g * TILE : (g + 1) * TILE, :] += hr
            h_ref[b, 1, g * TILE : (g + 1) * TILE, :] += hi
        return carry

    lax.fori_loop(0, 3 * chunks, forward, 0)

    for st in range(-(-3 * G // 8)):
        lo = st * 128
        ab = jnp.concatenate([sa_ref[lo : lo + 128, :], sb_ref[lo : lo + 128, :]], axis=0)
        uv = dot(rows_ref[...], ab, precision=HIGH)
        uv = jnp.concatenate([uv[:128], uv[128:]], axis=1)
        pix = dot(uv, back_ref[...], precision=HIGH)
        val = (sk_ref[lo : lo + 128, :] + pix / 256.0) / F
        for q in range(8):
            b, g = divmod(st * 8 + q, G)
            if b > 2:
                break
            one = val[q * TILE : (q + 1) * TILE]
            if b == 0:
                one = jnp.where(s == 0, 0.0, one)
            if b == 2:
                one = jnp.where(s == n_space - 1, 0.0, one)
            mm_ref[g, b * TILE : (b + 1) * TILE, :] = one
    own = G // nf
    for k in range(own):
        merged_ref[:, k * LANES : (k + 1) * LANES] = mm_ref[fr * own + k, TILE : 2 * TILE, :]

    pairs = jnp.concatenate(
        [
            jnp.concatenate([mm_ref[2 * h, 12:36, :], mm_ref[2 * h + 1, 12:36, :]], axis=1)
            for h in range(G // 2)
        ],
        axis=0,
    )
    parted = dot(pairs.astype(jnp.bfloat16), split_ref[...])
    site = lax.broadcasted_iota(jnp.int32, (24, half), 1)
    pieces = []
    for q in range(2):
        plane = jnp.concatenate(
            [parted[24 * h : 24 * h + 24, q * 128 : (q + 1) * 128] for h in range(G // 2)], axis=1
        )
        pieces.append(jnp.where(site == 0, 0.0, pltpu.roll(plane, 1, 1)))
        pieces.append(plane)
        pieces.append(jnp.where(site == half - 1, 0.0, pltpu.roll(plane, half - 1, 1)))
    pieces.append(jnp.zeros((112, half), jnp.float32))
    taps = jnp.concatenate(pieces, axis=0).astype(jnp.bfloat16)

    preact = dot(big_ref[...], taps[:144])
    offs = offs_ref[...]
    bias = jnp.zeros((32, half), jnp.float32)
    slopes = []
    for sy in range(10):
        v = preact[sy * 32 : sy * 32 + 32] + offs
        sig = jax.nn.sigmoid(v)
        slope = (v * sig - goal_ref[sy]) * inv_pixels * (sig * (1.0 + v * (1.0 - sig)))
        if sy == 0:
            slope = jnp.where(s == 0, 0.0, slope)
        elif sy == 9:
            slope = jnp.where(s == n_space - 1, 0.0, slope)
        else:
            bias = bias + slope
        slopes.append(slope)
    slope_bf = jnp.concatenate(slopes, axis=0).astype(jnp.bfloat16)
    prod = dot(slope_bf[32:288], taps, ((1,), (1,)))
    gw = jnp.zeros((32, 256), jnp.float32)
    for sy in range(1, 9):
        gw = gw + pltpu.roll(prod[(sy - 1) * 32 : sy * 32], 256 - 2 * sy, 1)
    gw = dot(gw, pick_ref[...], precision=HIGH)
    bias = jnp.sum(bias, axis=1, keepdims=True)
    lane32 = lax.broadcasted_iota(jnp.int32, (32, LANES), 1)
    out_ref[0:32, :] = jnp.where(lane32 == 36, bias, gw)

    gt = dot(bigt_ref[...], slope_bf)
    site16 = lax.broadcasted_iota(jnp.int32, (TILE, half), 1)
    planes = []
    for q in range(2):
        left = gt[(q * 3) * 16 : (q * 3) * 16 + 16]
        mid = gt[(q * 3 + 1) * 16 : (q * 3 + 1) * 16 + 16]
        right = gt[(q * 3 + 2) * 16 : (q * 3 + 2) * 16 + 16]
        planes.append(
            mid
            + jnp.where(site16 == half - 1, 0.0, pltpu.roll(left, half - 1, 1))
            + jnp.where(site16 == 0, 0.0, pltpu.roll(right, 1, 1))
        )
    grad = jnp.concatenate(
        [
            jnp.concatenate([p[:, h * 128 : (h + 1) * 128] for p in planes], axis=1)
            for h in range(G // 2)
        ],
        axis=0,
    ) / F
    pq = dot(grad, wide_ref[...], precision=HIGH)
    noise = jnp.zeros((TILE, LANES), jnp.float32)
    for st in range(-(-G // 8)):
        groups = range(st * 8, min(G, st * 8 + 8))
        parts = []
        for first in (0, 256):
            for g in groups:
                r0 = (g // 2) * TILE
                c0 = first + (g % 2) * LANES
                parts.append(pq[r0 : r0 + TILE, c0 : c0 + LANES])
        m = len(groups) * TILE
        lhs = rows_ref[...]
        if m < 128:
            lhs = jnp.concatenate(
                [
                    jnp.concatenate([lhs[:m, :m], lhs[:m, 128 : 128 + m]], axis=1),
                    jnp.concatenate([lhs[128 : 128 + m, :m], lhs[128 : 128 + m, 128 : 128 + m]], axis=1),
                ],
                axis=0,
            )
        ri = dot(lhs, jnp.concatenate(parts, axis=0), precision=HIGH)
        for k, g in enumerate(groups):
            noise = noise - (
                ri[k * TILE : (k + 1) * TILE] * h_ref[1, 0, g * TILE : (g + 1) * TILE, :]
                + ri[m + k * TILE : m + (k + 1) * TILE] * h_ref[1, 1, g * TILE : (g + 1) * TILE, :]
            )
    noise = noise / 256.0
    for step in (64, 32, 16):
        noise = noise + pltpu.roll(noise, step, 1)
    out_ref[32:48, :] = noise


def involution(value, count, step, first):
    pairs = []
    for i in range(count):
        if i < first:
            continue
        j = ((i - first) ^ step) + first
        if 0 <= j < count:
            pairs.append((i, j))
    return lax.ppermute(value, "space", pairs)


def sum_space(value, count):
    bits = count.bit_length() - 1
    assert 1 << bits == count
    stages = []
    at = 0
    while at < bits:
        width = 2 if at == 1 and bits - at >= 2 else 1
        stages.append([m << at for m in range(1, 1 << width)])
        at += width
    for masks in stages:
        got = [
            lax.ppermute(value, "space", [(i, i ^ m) for i in range(count)]) for m in masks
        ]
        value = value + got[0]
        if len(got) == 3:
            value = value + (got[1] + got[2])
    return value


def shards(raw, shifts, weight, offset, log_var, goal):
    nf = lax.axis_size("frame")
    n_space = lax.axis_size("space")
    fl, band_rows, W = raw.shape
    T = shifts.shape[3]
    channels, site_rows, ws = goal.shape
    G = W // LANES
    F = nf * fl
    nsc = ws // LANES
    inv_pixels = 1.0 / (band_rows * n_space * W // 4)
    bf16 = jnp.bfloat16

    blocks = raw.reshape(fl, TILE, G, LANES).transpose(0, 2, 1, 3).reshape(fl * G * TILE, LANES)
    edge = jnp.stack([goal[:, 0], goal[:, site_rows - 1]], axis=0)
    edge = edge.reshape(2, channels, nsc, LANES).transpose(0, 2, 1, 3).reshape(-1, LANES)
    words = shifts.astype(bf16).reshape(-1)
    used = -(-words.shape[0] // LANES)
    rs = -(-used // 16) * 16
    words = jnp.pad(words, (0, rs * LANES - words.shape[0])).reshape(rs, LANES)
    aux = jnp.concatenate([edge, words], axis=0)
    packet = jnp.concatenate([blocks, aux], axis=0)
    goals = goal.transpose(1, 0, 2)

    def from_frame(value, j):
        return lax.ppermute(value, "frame", [(i, (i - j) % nf) for i in range(nf)])

    packets = [packet] + [from_frame(packet, j) for j in range(1, nf)]
    goal_parts = [goals] + [from_frame(goals, j) for j in range(1, nf)]
    cut = fl * G * TILE
    y = jnp.concatenate([p[:cut] for p in packets] + [p[cut:] for p in packets], axis=0)
    y_raw = y[: nf * cut]
    yc = involution(y, n_space, 1, 0)
    yf = involution(y, n_space, 1, 1)
    y2 = involution(y_raw, n_space, 2, 0)
    y3 = involution(y_raw, n_space, 2, 2)

    cols, back, rows, split, wide = tables()
    place, place_t, pick = tap_tables()
    big = jnp.dot(weight, jnp.asarray(place.reshape(36, -1), bf16), preferred_element_type=jnp.float32)
    big = big.reshape(channels, 10, 144).transpose(1, 0, 2).reshape(320, 144).astype(bf16)
    bigt = jnp.dot(
        jnp.asarray(place_t.reshape(-1, 36), bf16), weight.T, preferred_element_type=jnp.float32
    )
    bigt = bigt.reshape(96, 320).astype(bf16)
    offs = jnp.broadcast_to(offset[:, None], (channels, W // 2))
    var = jnp.tile(jnp.exp(log_var).reshape(TILE, TILE), (1, 8))

    dims = (nf, fl, G, T, nsc, rs, n_space, inv_pixels)
    f32 = jnp.float32
    pad_rows = -(-3 * G // 8) * 128
    sv_rows = 3 * nf * rs
    vm = pl.BlockSpec(memory_space=pltpu.VMEM)
    args = [y, yc, yf, y2, y3, *goal_parts, cols, back, rows, jnp.asarray(split, bf16), wide, pick]
    args += [big, bigt, offs, var]
    merged, part = pl.pallas_call(
        functools.partial(kernel, dims),
        out_shape=(
            jax.ShapeDtypeStruct((TILE, W // nf), f32),
            jax.ShapeDtypeStruct((48, LANES), f32),
        ),
        in_specs=[vm] * len(args),
        out_specs=(vm, vm),
        scratch_shapes=[
            pltpu.VMEM((F * G, 5 * TILE, LANES), f32),
            pltpu.VMEM((10, channels, W // 2), f32),
            pltpu.VMEM((sv_rows, LANES), jnp.int32),
            pltpu.SMEM((sv_rows, LANES), jnp.int32),
            pltpu.SemaphoreType.DMA,
            pltpu.VMEM((pad_rows, LANES), f32),
            pltpu.VMEM((pad_rows, LANES), f32),
            pltpu.VMEM((pad_rows, LANES), f32),
            pltpu.VMEM((3, 2, G * TILE, LANES), f32),
            pltpu.VMEM((G, 3 * TILE, LANES), f32),
        ],
        name="merge_step",
    )(*args)
    total = sum_space(part, n_space)
    return (
        merged,
        total[:32, :36],
        total[:32, 36],
        total[32:48, :16].reshape(256),
    )


def solution(mesh):
    placed = (
        P("frame", "space", None),
        P("frame", None, "space", None),
        P(),
        P(),
        P(),
        P(None, "space", "frame"),
    )
    return jax.shard_map(
        shards,
        mesh=mesh,
        in_specs=placed,
        out_specs=(P("space", "frame"), P(), P(), P()),
        check_vma=False,
    )
```

```python
import functools
import math

import jax
import jax.numpy as jnp
import numpy as np
from jax import lax
from jax.experimental import pallas as pl
from jax.experimental.pallas import tpu as pltpu
from jax.sharding import PartitionSpec as P

TILE = 16
LANES = 128
HIGH = lax.Precision.HIGHEST


def dot(a, b, dims=((1,), (0,)), precision=None):
    return lax.dot_general(
        a, b, (dims, ((), ())), precision=precision, preferred_element_type=jnp.float32
    )


def tables():
    angle = 2.0 * math.pi / TILE * (np.outer(np.arange(TILE), np.arange(TILE)) % TILE)
    cos16, sin16 = np.cos(angle), np.sin(angle)
    eye8, eye16 = np.eye(8), np.eye(16)
    bc, bs = np.kron(eye8, cos16), np.kron(eye8, sin16)
    cols = np.concatenate([bc, bs], axis=1)
    back = np.concatenate([bc, bs], axis=0)
    rows = np.block([[bc, -bs], [-bs, -bc]])
    split = np.zeros((256, 256))
    for x in range(256):
        split[x, (x % 2) * 128 + x // 2] = 1.0
    wide = np.concatenate([np.kron(eye16, cos16), np.kron(eye16, sin16)], axis=1)
    f32 = np.float32
    return cols.astype(f32), back.astype(f32), rows.astype(f32), split, (split.T @ wide).astype(f32)


def tap_tables():
    place = np.zeros((36, 10, 144))
    back = np.zeros((96, 10, 36))
    pick = np.zeros((256, 128))
    for a in range(3):
        for b in range(3):
            for p in range(2):
                for q in range(2):
                    tap = (3 * a + b) * 4 + 2 * p + q
                    pick[(q * 3 + b) * 24 + 2 * a + p, tap] = 1.0
                    for sy in range(10):
                        r = 2 * (sy + a) + p
                        place[tap, sy, (q * 3 + b) * 24 + r] = 1.0
                        if 4 <= r < 20:
                            back[(q * 3 + b) * 16 + r - 4, sy, tap] = 1.0
    return place, back, pick.astype(np.float32)


def kernel(
    dims,
    y_ref,
    yc_ref,
    yf_ref,
    y2_ref,
    y3_ref,
    *refs,
):
    nf, fl, G, T, nsc, rs, n_space, inv_pixels = dims
    F = nf * fl
    W = G * LANES
    half = W // 2
    goal_refs = refs[:nf]
    (
        cols_ref,
        back_ref,
        rows_ref,
        split_ref,
        wide_ref,
        pick_ref,
        big_ref,
        bigt_ref,
        offs_ref,
        var_ref,
        merged_ref,
        out_ref,
        x_ref,
        goal_ref,
        sv_ref,
        sm_ref,
        sem,
        sa_ref,
        sb_ref,
        sk_ref,
        h_ref,
        mm_ref,
    ) = refs[nf:]
    s = lax.axis_index("space")
    fr = lax.axis_index("frame")
    odd = lax.rem(s, 2)
    odd2 = lax.rem(lax.div(s, 2), 2)
    raw_rows = F * G * TILE
    m_aux = 64 * nsc + rs
    used = rs

    for ref, band in ((y_ref, 1), (yc_ref, 2 - 2 * odd), (yf_ref, 2 * odd)):
        for j in range(nf):
            first = raw_rows + j * m_aux + 64 * nsc
            val = ref[first : first + used, :].astype(jnp.float32).astype(jnp.int32)
            at = (band * nf + lax.rem(fr + j, nf)) * used
            sv_ref[pl.ds(pl.multiple_of(at, 8), used), :] = val
    shift_copy = pltpu.make_async_copy(sv_ref, sm_ref, sem)
    shift_copy.start()

    slots = (
        (y_ref, 2),
        (yc_ref, 3 - 2 * odd),
        (yf_ref, 1 + 2 * odd),
        (y2_ref, 4 - 4 * odd2),
        (y3_ref, 4 * odd2),
    )

    def fill(k, carry):
        to = lax.rem(k + fr * (fl * G), F * G)
        for ref, slot in slots:
            block = ref[pl.ds(pl.multiple_of(k * TILE, TILE), TILE), :].astype(jnp.float32)
            x_ref[to, pl.ds(pl.multiple_of(slot * TILE, TILE), TILE), :] = block
        return carry

    lax.fori_loop(0, F * G, fill, 0, unroll=min(F * G, 16))

    for j in range(nf):
        at = pl.multiple_of(lax.rem(fr + j, nf) * (nsc * LANES), LANES)
        for r in range(8):
            goal_ref[r + 1, :, pl.ds(at, nsc * LANES)] = goal_refs[j][r].astype(jnp.float32)
        for ref, row, top in ((yc_ref, 9 - 9 * odd, odd), (yf_ref, 9 * odd, 1 - odd)):
            for c in range(nsc):
                first = raw_rows + j * m_aux + (top * nsc + c) * 32
                val = ref[pl.ds(pl.multiple_of(first, 16), 32), :].astype(jnp.float32)
                goal_ref[row, :, pl.ds(pl.multiple_of(at + c * LANES, LANES), LANES)] = val

    sa_ref[...] = jnp.zeros_like(sa_ref)
    sb_ref[...] = jnp.zeros_like(sb_ref)
    sk_ref[...] = jnp.zeros_like(sk_ref)
    h_ref[...] = jnp.zeros_like(h_ref)
    lane = lax.broadcasted_iota(jnp.int32, (TILE, LANES), 1)
    lane_tile = lane // TILE
    low = lane < 64
    var = var_ref[...]
    per = 16 // G
    chunks = F * G // 16
    shift_copy.wait()

    def forward(n, carry):
        b = lax.div(n, chunks)
        c = lax.rem(n, chunks)
        diffs = []
        for q in range(16):
            f = c * per + q // G
            g = q % G
            j = lax.div(f, fl)
            l = lax.rem(f, fl)
            row0 = (b * nf + j) * used
            blk = jnp.zeros((TILE, LANES), jnp.float32)
            for t in range(8):
                at = l * (2 * T) + 8 * g + t
                dy = sm_ref[row0 + lax.div(at, LANES), lax.rem(at, LANES)]
                at = at + T
                dx = sm_ref[row0 + lax.div(at, LANES), lax.rem(at, LANES)]
                start = TILE * (b + 1) + dy
                win = x_ref[f * G + g, pl.ds(start, TILE), :]
                if t == 0:
                    if g > 0:
                        other = x_ref[f * G + g - 1, pl.ds(start, TILE), :]
                    else:
                        other = jnp.zeros((TILE, LANES), jnp.float32)
                    win = jnp.where(low, win, other)
                if t == 7:
                    if g < G - 1:
                        other = x_ref[f * G + g + 1, pl.ds(start, TILE), :]
                    else:
                        other = jnp.zeros((TILE, LANES), jnp.float32)
                    win = jnp.where(low, other, win)
                win = pltpu.roll(win, (LANES - dx) & (LANES - 1), 1)
                blk = win if t == 0 else jnp.where(lane_tile == t, win, blk)
            at = pl.multiple_of((b * G + g) * TILE, TILE)
            sk_ref[pl.ds(at, TILE), :] += blk
            base = x_ref[g, pl.ds(pl.multiple_of(TILE * (b + 1), TILE), TILE), :]
            diffs.append(base - blk)
        pq = dot(jnp.concatenate(diffs, axis=0), cols_ref[...], precision=HIGH)
        top = jnp.concatenate([pq[:128, :128], pq[128:, :128]], axis=1)
        bottom = jnp.concatenate([pq[:128, 128:], pq[128:, 128:]], axis=1)
        ri = dot(rows_ref[...], jnp.concatenate([top, bottom], axis=0), precision=HIGH)
        for g in range(G):
            a_sum = jnp.zeros((TILE, LANES), jnp.float32)
            b_sum = jnp.zeros((TILE, LANES), jnp.float32)
            hr = jnp.zeros((TILE, LANES), jnp.float32)
            hi = jnp.zeros((TILE, LANES), jnp.float32)
            for u in range(per):
                q = u * G + g
                r0 = (q % 8) * TILE
                c0 = (q // 8) * LANES
                re = ri[r0 : r0 + TILE, c0 : c0 + LANES]
                im = ri[128 + r0 : 128 + r0 + TILE, c0 : c0 + LANES]
                energy = re * re + im * im
                weight = energy / (energy + var)
                wr = weight * re
                wi = weight * im
                rest = 1.0 - weight
                a_sum += wr
                b_sum += wi
                hr += wr * rest
                hi += wi * rest
            at = pl.multiple_of((b * G + g) * TILE, TILE)
            sa_ref[pl.ds(at, TILE), :] += a_sum
            sb_ref[pl.ds(at, TILE), :] += b_sum
            h_ref[b, 0, g * TILE : (g + 1) * TILE, :] += hr
            h_ref[b, 1, g * TILE : (g + 1) * TILE, :] += hi
        return carry

    lax.fori_loop(0, 3 * chunks, forward, 0)

    for st in range(-(-3 * G // 8)):
        lo = st * 128
        ab = jnp.concatenate([sa_ref[lo : lo + 128, :], sb_ref[lo : lo + 128, :]], axis=0)
        uv = dot(rows_ref[...], ab, precision=HIGH)
        uv = jnp.concatenate([uv[:128], uv[128:]], axis=1)
        pix = dot(uv, back_ref[...], precision=HIGH)
        val = (sk_ref[lo : lo + 128, :] + pix / 256.0) / F
        for q in range(8):
            b, g = divmod(st * 8 + q, G)
            if b > 2:
                break
            one = val[q * TILE : (q + 1) * TILE]
            if b == 0:
                one = jnp.where(s == 0, 0.0, one)
            if b == 2:
                one = jnp.where(s == n_space - 1, 0.0, one)
            mm_ref[g, b * TILE : (b + 1) * TILE, :] = one
    own = G // nf
    for k in range(own):
        merged_ref[:, k * LANES : (k + 1) * LANES] = mm_ref[fr * own + k, TILE : 2 * TILE, :]

    pairs = jnp.concatenate(
        [
            jnp.concatenate([mm_ref[2 * h, 12:36, :], mm_ref[2 * h + 1, 12:36, :]], axis=1)
            for h in range(G // 2)
        ],
        axis=0,
    )
    parted = dot(pairs.astype(jnp.bfloat16), split_ref[...])
    site = lax.broadcasted_iota(jnp.int32, (24, half), 1)
    pieces = []
    for q in range(2):
        plane = jnp.concatenate(
            [parted[24 * h : 24 * h + 24, q * 128 : (q + 1) * 128] for h in range(G // 2)], axis=1
        )
        pieces.append(jnp.where(site == 0, 0.0, pltpu.roll(plane, 1, 1)))
        pieces.append(plane)
        pieces.append(jnp.where(site == half - 1, 0.0, pltpu.roll(plane, half - 1, 1)))
    pieces.append(jnp.zeros((112, half), jnp.float32))
    taps = jnp.concatenate(pieces, axis=0).astype(jnp.bfloat16)

    preact = dot(big_ref[...], taps[:144])
    offs = offs_ref[...]
    bias = jnp.zeros((32, half), jnp.float32)
    slopes = []
    for sy in range(10):
        v = preact[sy * 32 : sy * 32 + 32] + offs
        sig = jax.nn.sigmoid(v)
        slope = (v * sig - goal_ref[sy]) * inv_pixels * (sig * (1.0 + v * (1.0 - sig)))
        if sy == 0:
            slope = jnp.where(s == 0, 0.0, slope)
        elif sy == 9:
            slope = jnp.where(s == n_space - 1, 0.0, slope)
        else:
            bias = bias + slope
        slopes.append(slope)
    slope_bf = jnp.concatenate(slopes, axis=0).astype(jnp.bfloat16)
    prod = dot(slope_bf[32:288], taps, ((1,), (1,)))
    gw = jnp.zeros((32, 256), jnp.float32)
    for sy in range(1, 9):
        gw = gw + pltpu.roll(prod[(sy - 1) * 32 : sy * 32], 256 - 2 * sy, 1)
    gw = dot(gw, pick_ref[...], precision=HIGH)
    out_ref[0:32, :] = gw
    ones = jnp.ones((8, half), jnp.float32)
    bias = dot(ones, bias, ((1,), (1,)), precision=HIGH)[0:1]
    bias = jnp.concatenate([bias, jnp.zeros((1, LANES - 32), jnp.float32)], axis=1)

    gt = dot(bigt_ref[...], slope_bf)
    site16 = lax.broadcasted_iota(jnp.int32, (TILE, half), 1)
    planes = []
    for q in range(2):
        left = gt[(q * 3) * 16 : (q * 3) * 16 + 16]
        mid = gt[(q * 3 + 1) * 16 : (q * 3 + 1) * 16 + 16]
        right = gt[(q * 3 + 2) * 16 : (q * 3 + 2) * 16 + 16]
        planes.append(
            mid
            + jnp.where(site16 == half - 1, 0.0, pltpu.roll(left, half - 1, 1))
            + jnp.where(site16 == 0, 0.0, pltpu.roll(right, 1, 1))
        )
    grad = jnp.concatenate(
        [
            jnp.concatenate([p[:, h * 128 : (h + 1) * 128] for p in planes], axis=1)
            for h in range(G // 2)
        ],
        axis=0,
    ) / F
    pq = dot(grad, wide_ref[...], precision=HIGH)
    noise = jnp.zeros((TILE, LANES), jnp.float32)
    for st in range(-(-G // 8)):
        groups = range(st * 8, min(G, st * 8 + 8))
        parts = []
        for first in (0, 256):
            for g in groups:
                r0 = (g // 2) * TILE
                c0 = first + (g % 2) * LANES
                parts.append(pq[r0 : r0 + TILE, c0 : c0 + LANES])
        m = len(groups) * TILE
        lhs = rows_ref[...]
        if m < 128:
            lhs = jnp.concatenate(
                [
                    jnp.concatenate([lhs[:m, :m], lhs[:m, 128 : 128 + m]], axis=1),
                    jnp.concatenate([lhs[128 : 128 + m, :m], lhs[128 : 128 + m, 128 : 128 + m]], axis=1),
                ],
                axis=0,
            )
        ri = dot(lhs, jnp.concatenate(parts, axis=0), precision=HIGH)
        for k, g in enumerate(groups):
            noise = noise - (
                ri[k * TILE : (k + 1) * TILE] * h_ref[1, 0, g * TILE : (g + 1) * TILE, :]
                + ri[m + k * TILE : m + (k + 1) * TILE] * h_ref[1, 1, g * TILE : (g + 1) * TILE, :]
            )
    noise = noise / 256.0
    for step in (64, 32, 16):
        noise = noise + pltpu.roll(noise, step, 1)
    spot = lax.broadcasted_iota(jnp.int32, (TILE, LANES), 0) % 8
    noise = jnp.where(lane_tile == spot, noise, 0.0)
    upper = jnp.sum(noise[:8], axis=0, keepdims=True)
    lower = jnp.sum(noise[8:], axis=0, keepdims=True)
    row = lax.broadcasted_iota(jnp.int32, (8, LANES), 0)
    tail = jnp.where(row == 0, bias, jnp.where(row == 1, upper, jnp.where(row == 2, lower, 0.0)))
    out_ref[32:40, :] = tail


def last_sum(own_ref, got_ref, weight_ref, bias_ref, noise_ref):
    total = own_ref[...] + got_ref[...]
    weight_ref[...] = total[:32, :36]
    bias_ref[...] = total[32:33, :32]
    noise_ref[...] = total[33:35]


def involution(value, count, step, first):
    pairs = []
    for i in range(count):
        if i < first:
            continue
        j = ((i - first) ^ step) + first
        if 0 <= j < count:
            pairs.append((i, j))
    return lax.ppermute(value, "space", pairs)


def sum_space(value, count):
    bits = count.bit_length() - 1
    assert 1 << bits == count
    stages = []
    at = 0
    while at < bits:
        width = 2 if at == 1 and bits - at >= 3 else 1
        stages.append([m << at for m in range(1, 1 << width)])
        at += width
    for masks in stages[:-1]:
        got = [
            lax.ppermute(value, "space", [(i, i ^ m) for i in range(count)]) for m in masks
        ]
        value = value + got[0]
        if len(got) == 3:
            value = value + (got[1] + got[2])
    (mask,) = stages[-1]
    got = lax.ppermute(value, "space", [(i, i ^ mask) for i in range(count)])
    return value, got


def shards(raw, shifts, weight, offset, log_var, goal):
    nf = lax.axis_size("frame")
    n_space = lax.axis_size("space")
    fl, band_rows, W = raw.shape
    T = shifts.shape[3]
    channels, site_rows, ws = goal.shape
    G = W // LANES
    F = nf * fl
    nsc = ws // LANES
    inv_pixels = 1.0 / (band_rows * n_space * W // 4)
    bf16 = jnp.bfloat16

    used = -(-(fl * 2 * T) // LANES)
    rs = -(-used // 16) * 16

    def packet(raw, shifts, goal):
        blocks = raw.reshape(fl, TILE, G, LANES).transpose(0, 2, 1, 3).reshape(-1, LANES)
        edge = jnp.stack([goal[:, 0], goal[:, site_rows - 1]], axis=0)
        edge = edge.reshape(2, channels, nsc, LANES).transpose(0, 2, 1, 3).reshape(-1, LANES)
        words = shifts.astype(bf16).reshape(-1)
        words = jnp.pad(words, (0, rs * LANES - words.shape[0])).reshape(rs, LANES)
        return blocks, jnp.concatenate([edge, words], axis=0), goal.transpose(1, 0, 2)

    def from_frame(value, j):
        return lax.ppermute(value, "frame", [(i, (i - j) % nf) for i in range(nf)])

    packets = [packet(raw, shifts, goal)]
    for j in range(1, nf):
        packets.append(packet(*(from_frame(v, j) for v in (raw, shifts, goal))))
    goal_parts = [p[2] for p in packets]
    y = jnp.concatenate([p[0] for p in packets] + [p[1] for p in packets], axis=0)
    y_raw = y[: nf * fl * G * TILE]
    yc = involution(y, n_space, 1, 0)
    yf = involution(y, n_space, 1, 1)
    y2 = involution(y_raw, n_space, 2, 0)
    y3 = involution(y_raw, n_space, 2, 2)

    cols, back, rows, split, wide = tables()
    place, place_t, pick = tap_tables()
    big = jnp.dot(weight, jnp.asarray(place.reshape(36, -1), bf16), preferred_element_type=jnp.float32)
    big = big.reshape(channels, 10, 144).transpose(1, 0, 2).reshape(320, 144).astype(bf16)
    bigt = jnp.dot(
        jnp.asarray(place_t.reshape(-1, 36), bf16), weight.T, preferred_element_type=jnp.float32
    )
    bigt = bigt.reshape(96, 320).astype(bf16)
    offs = jnp.broadcast_to(offset[:, None], (channels, W // 2))
    var = jnp.tile(jnp.exp(log_var).reshape(TILE, TILE), (1, 8))

    dims = (nf, fl, G, T, nsc, rs, n_space, inv_pixels)
    f32 = jnp.float32
    pad_rows = -(-3 * G // 8) * 128
    sv_rows = 3 * nf * rs
    vm = pl.BlockSpec(memory_space=pltpu.VMEM)
    args = [y, yc, yf, y2, y3, *goal_parts, cols, back, rows, jnp.asarray(split, bf16), wide, pick]
    args += [big, bigt, offs, var]
    scratch = [
        pltpu.VMEM((F * G, 5 * TILE, LANES), f32),
        pltpu.VMEM((10, channels, W // 2), f32),
        pltpu.VMEM((sv_rows, LANES), jnp.int32),
        pltpu.SMEM((sv_rows, LANES), jnp.int32),
        pltpu.SemaphoreType.DMA,
        pltpu.VMEM((pad_rows, LANES), f32),
        pltpu.VMEM((pad_rows, LANES), f32),
        pltpu.VMEM((pad_rows, LANES), f32),
        pltpu.VMEM((3, 2, G * TILE, LANES), f32),
        pltpu.VMEM((G, 3 * TILE, LANES), f32),
    ]
    room = sum(int(np.prod(a.shape)) * a.dtype.itemsize for a in args)
    room += F * G * 5 * TILE * LANES * 4 + (14 << 20)
    merged, part = pl.pallas_call(
        functools.partial(kernel, dims),
        out_shape=(
            jax.ShapeDtypeStruct((TILE, W // nf), f32),
            jax.ShapeDtypeStruct((40, LANES), f32),
        ),
        in_specs=[vm] * len(args),
        out_specs=(vm, vm),
        scratch_shapes=scratch,
        compiler_params=pltpu.CompilerParams(vmem_limit_bytes=room),
        name="merge_step",
    )(*args)
    grad_weight, grad_bias, grad_noise = pl.pallas_call(
        last_sum,
        out_shape=(
            jax.ShapeDtypeStruct((channels, 36), f32),
            jax.ShapeDtypeStruct((1, channels), f32),
            jax.ShapeDtypeStruct((2, LANES), f32),
        ),
        in_specs=[vm, vm],
        out_specs=(vm, vm, vm),
        compiler_params=pltpu.CompilerParams(vmem_limit_bytes=1 << 20),
        name="last_sum",
    )(*sum_space(part, n_space))
    return merged, grad_weight, grad_bias.reshape(channels), grad_noise.reshape(256)


def solution(mesh):
    placed = (
        P("frame", "space", None),
        P("frame", None, "space", None),
        P(),
        P(),
        P(),
        P(None, "space", "frame"),
    )
    return jax.shard_map(
        shards,
        mesh=mesh,
        in_specs=placed,
        out_specs=(P("space", "frame"), P(), P(), P()),
        check_vma=False,
    )
```

```python
import functools
import math

import jax
import jax.numpy as jnp
import ml_dtypes
import numpy as np
from jax import lax
from jax.experimental import pallas as pl
from jax.experimental.pallas import tpu as pltpu
from jax.sharding import PartitionSpec as P

TILE = 16
LANES = 128
F32 = jnp.float32
BF16 = jnp.bfloat16


def dot(a, b, dims=((1,), (0,))):
    return lax.dot_general(a, b, (dims, ((), ())), preferred_element_type=F32)


def split(value, parts):
    terms = []
    for _ in range(parts):
        term = value.astype(BF16)
        terms.append(term)
        value = value - term.astype(F32)
    return terms


def split_table(value, parts):
    terms = []
    value = value.astype(np.float64)
    for _ in range(parts):
        term = value.astype(np.float32).astype(ml_dtypes.bfloat16)
        terms.append(term)
        value = value - term.astype(np.float64)
    return terms


def tables():
    angle = 2.0 * math.pi / TILE * (np.outer(np.arange(TILE), np.arange(TILE)) % TILE)
    cos16, sin16 = np.cos(angle), np.sin(angle)
    eye8, eye16 = np.eye(8), np.eye(16)
    bc, bs = np.kron(eye8, cos16), np.kron(eye8, sin16)
    fwd = split_table(np.concatenate([bc, bs], axis=1), 3)
    fwd_main = np.concatenate(fwd[:2], axis=0)
    inv = split_table(np.concatenate([bc, -bs], axis=0), 3)
    inv_main = np.concatenate(inv[:2], axis=1)
    part = np.zeros((256, 256))
    for x in range(256):
        part[x, (x % 2) * 128 + x // 2] = 1.0
    wide = np.concatenate([np.kron(eye16, cos16), np.kron(eye16, sin16)], axis=1)
    wide = split_table(part.T @ wide, 2)
    return fwd_main, fwd[2], inv_main, inv[2], part.astype(ml_dtypes.bfloat16), wide[0], wide[1]


def tap_tables():
    place = np.zeros((36, 10, 144))
    back = np.zeros((96, 10, 36))
    pick = np.zeros((256, 128))
    for a in range(3):
        for b in range(3):
            for p in range(2):
                for q in range(2):
                    tap = (3 * a + b) * 4 + 2 * p + q
                    pick[(q * 3 + b) * 24 + 2 * a + p, tap] = 1.0
                    for sy in range(10):
                        r = 2 * (sy + a) + p
                        place[tap, sy, (q * 3 + b) * 24 + r] = 1.0
                        if 4 <= r < 20:
                            back[(q * 3 + b) * 16 + r - 4, sy, tap] = 1.0
    return place, back, pick.astype(ml_dtypes.bfloat16)


def turn(re, im, k, n):
    if k == 0:
        return re, im
    if 4 * k == n:
        return im, -re
    if 8 * k == n:
        half = math.sqrt(0.5)
        return (re + im) * half, (im - re) * half
    if 8 * k == 3 * n:
        half = math.sqrt(0.5)
        return (im - re) * half, (re + im) * -half
    c, s = math.cos(2.0 * math.pi * k / n), math.sin(2.0 * math.pi * k / n)
    return re * c + im * s, im * c - re * s


def fft(re, im):
    n = len(re)
    if n == 1:
        return re, im
    er, ei = fft(re[0::2], im[0::2])
    our, oi = fft(re[1::2], im[1::2])
    half = n // 2
    xr, xi = [None] * n, [None] * n
    for k in range(half):
        tr, ti = turn(our[k], oi[k], k, n)
        xr[k], xi[k] = er[k] + tr, ei[k] + ti
        xr[k + half], xi[k + half] = er[k] - tr, ei[k] - ti
    return xr, xi


def add_lists(a, b):
    return b if a is None else [x + y for x, y in zip(a, b)]


def merge_kernel(dims, dy_ref, idx_ref, y_ref, yc_ref, yf_ref, *refs):
    nf, fl, G, T, nsc = dims
    F = nf * fl
    goal_refs = refs[:nf]
    fwd_ref, fwdl_ref, inv_ref, invl_ref, var_ref = refs[nf : nf + 5]
    merged_ref, pack_ref, pc_ref, pf_ref, h_ref = refs[nf + 5 : nf + 10]
    x_ref, p_ref, q_ref, xs_ref, mm_ref = refs[nf + 10 :]
    s = lax.axis_index("space")
    fr = lax.axis_index("frame")
    odd = lax.rem(s, 2)

    slots = ((y_ref, 1), (yc_ref, 2 - 2 * odd), (yf_ref, 2 * odd))

    def fill(k, carry):
        for ref, slot in slots:
            block = ref[pl.ds(pl.multiple_of(k * TILE, TILE), TILE), :].astype(F32)
            x_ref[k, pl.ds(pl.multiple_of(slot * TILE, TILE), TILE), :] = block
        return carry

    lax.fori_loop(0, F * G, fill, 0, unroll=min(F * G, 16))

    lead = G * 4
    for j in range(nf):
        for c in range(nsc):
            at = lead + (j * nsc + c) * 32
            cols = slice(c * LANES, (c + 1) * LANES)
            pc_ref[at : at + 32, :] = goal_refs[j][7 - 7 * odd, :, cols]
            pf_ref[at : at + 32, :] = goal_refs[j][7 * odd, :, cols]

    lane = lax.broadcasted_iota(jnp.int32, (TILE, LANES), 1)
    kind = (lane // TILE) % 4
    per = 16 // G
    chunks = F * G // 16
    rows_out = max(G, 8)
    fold = TILE // rows_out
    zero = jnp.zeros((TILE, LANES), F32)

    def place(f):
        j = lax.rem(f // fl + nf - fr, nf)
        return j * fl + f % fl

    def chunk_step(c, carry):
        sums = carry[0] if carry is not None else None
        blocks = []
        for q in range(16):
            g = q % G
            f = place(c * per + q // G)

            def load(t, group):
                if group < 0 or group >= G:
                    return zero
                start = dy_ref[f * T + 8 * g + t]
                return x_ref[f * G + group, pl.ds(start, TILE), :]

            idx = jnp.broadcast_to(idx_ref[pl.ds(f * G + g, 1), :], (TILE, LANES))
            mixes = (
                jnp.where(
                    lane < 40,
                    load(0, g),
                    jnp.where(lane < 104, load(4, g), load(0, g - 1)),
                ),
                jnp.where(lane < 56, load(1, g), load(5, g)),
                jnp.where(lane < 72, load(2, g), load(6, g)),
                jnp.where(
                    lane < 24,
                    load(7, g + 1),
                    jnp.where(lane < 88, load(3, g), load(7, g)),
                ),
            )
            moved = [jnp.take_along_axis(m, idx, axis=1) for m in mixes]
            blocks.append(
                jnp.where(
                    kind < 2,
                    jnp.where(kind == 0, moved[0], moved[1]),
                    jnp.where(kind == 2, moved[2], moved[3]),
                )
            )
        part = [functools.reduce(lambda a, b: a + b, blocks[g::G]) for g in range(G)]
        sums = add_lists(sums, part)
        first = place(0)
        base = [x_ref[first * G + g, TILE : 2 * TILE, :] for g in range(G)]
        both = jnp.concatenate(blocks + base, axis=0).astype(BF16)
        pq = dot(jnp.concatenate([both, both], axis=1), fwd_ref[...]) + dot(both, fwdl_ref[...])
        for q in range(16):
            rows = slice(q * TILE, (q + 1) * TILE)
            ref_rows = slice(256 + (q % G) * TILE, 256 + (q % G + 1) * TILE)
            diff = pq[ref_rows] - pq[rows]
            p_ref[rows, :] = diff[:, :LANES]
            q_ref[rows, :] = -diff[:, LANES:]
        re, im = fft(
            [p_ref[pl.ds(n, 16, stride=16), :] for n in range(16)],
            [q_ref[pl.ds(n, 16, stride=16), :] for n in range(16)],
        )
        out = [[], [], [], []]
        for k in range(16):
            var = jnp.broadcast_to(var_ref[k : k + 1, :], (TILE, LANES))
            energy = re[k] * re[k] + im[k] * im[k]
            weight = energy / (energy + var)
            wr = weight * re[k]
            wi = weight * im[k]
            rest = 1.0 - weight
            for store, val in zip(out, (wr, wi, wr * rest, wi * rest)):
                if fold == 2:
                    val = val[:8] + val[8:]
                store.append(val)
        flat = out[0] + out[1] + out[2] + out[3]
        return sums, add_lists(carry[1] if carry is not None else None, flat)

    carry = chunk_step(0, None)
    if chunks > 1:
        carry = lax.fori_loop(1, chunks, chunk_step, carry)
    sums, flat = carry
    for k in range(32):
        h_ref[k * rows_out : (k + 1) * rows_out, :] = flat[32 + k]

    vi, ur = fft(flat[16:32], flat[:16])
    uv = jnp.concatenate(
        [jnp.concatenate(ur, axis=0), jnp.concatenate(vi, axis=0)], axis=1
    )
    m = 16 * rows_out
    terms = split(uv, 3)
    wide = dot(jnp.concatenate(terms, axis=0), inv_ref[...])
    pix = wide[:m, :LANES] + (wide[m : 2 * m, :LANES] + wide[:m, LANES:])
    pix = pix + (wide[2 * m :, :LANES] + wide[m : 2 * m, LANES:] + dot(terms[0], invl_ref[...]))
    xs_ref[...] = pix
    for g in range(G):
        val = xs_ref[pl.ds(g, 16, stride=rows_out), :]
        for other in range(g + G, rows_out, G):
            val = val + xs_ref[pl.ds(other, 16, stride=rows_out), :]
        val = (sums[g] + val / 256.0) / F
        mm_ref[g] = val
        pack_ref[g] = val
    own = G // nf
    for k in range(own):
        merged_ref[:, k * LANES : (k + 1) * LANES] = mm_ref[fr * own + k]
    low = jnp.concatenate([mm_ref[g, 0:4, :] for g in range(G)], axis=0)
    high = jnp.concatenate([mm_ref[g, 12:16, :] for g in range(G)], axis=0)
    pc_ref[0:lead, :] = jnp.where(odd == 1, low, high).astype(BF16)
    pf_ref[0:lead, :] = jnp.where(odd == 1, high, low).astype(BF16)


def demosaic_kernel(dims, pack_ref, pc_ref, pf_ref, h_ref, *refs):
    nf, fl, G, nsc, n_space, inv_pixels = dims
    F = nf * fl
    W = G * LANES
    half = W // 2
    goal_refs = refs[:nf]
    part_ref, wideh_ref, widel_ref, pick_ref, big_ref, bigt_ref, offs_ref = refs[nf : nf + 7]
    out_ref, goal_ref, mm_ref, p_ref, q_ref, ns_ref = refs[nf + 7 :]
    s = lax.axis_index("space")
    fr = lax.axis_index("frame")
    odd = lax.rem(s, 2)
    rows_out = max(G, 8)

    lead = G * 4
    for j in range(nf):
        at = pl.multiple_of(lax.rem(fr + j, nf) * (nsc * LANES), LANES)
        for r in range(8):
            goal_ref[r + 1, :, pl.ds(at, nsc * LANES)] = goal_refs[j][r].astype(F32)
        for ref, row in ((pc_ref, 9 - 9 * odd), (pf_ref, 9 * odd)):
            for c in range(nsc):
                first = lead + (j * nsc + c) * 32
                val = ref[first : first + 32, :].astype(F32)
                goal_ref[row, :, pl.ds(pl.multiple_of(at + c * LANES, LANES), LANES)] = val

    near = pc_ref[0:lead, :].astype(F32)
    far = pf_ref[0:lead, :].astype(F32)
    low = jnp.where(odd == 1, near, far)
    high = jnp.where(odd == 1, far, near)
    for g in range(G):
        mm_ref[g, 0:4, :] = low[4 * g : 4 * g + 4]
        mm_ref[g, 4:20, :] = pack_ref[g]
        mm_ref[g, 20:24, :] = high[4 * g : 4 * g + 4]
    pairs = jnp.concatenate(
        [jnp.concatenate([mm_ref[2 * h], mm_ref[2 * h + 1]], axis=1) for h in range(G // 2)],
        axis=0,
    )
    parted = dot(pairs.astype(BF16), part_ref[...])
    site = lax.broadcasted_iota(jnp.int32, (24, half), 1)
    pieces = []
    for q in range(2):
        plane = jnp.concatenate(
            [parted[24 * h : 24 * h + 24, q * 128 : (q + 1) * 128] for h in range(G // 2)], axis=1
        )
        pieces.append(jnp.where(site == 0, 0.0, pltpu.roll(plane, 1, 1)))
        pieces.append(plane)
        pieces.append(jnp.where(site == half - 1, 0.0, pltpu.roll(plane, half - 1, 1)))
    pieces.append(jnp.zeros((112, half), F32))
    taps = jnp.concatenate(pieces, axis=0).astype(BF16)

    preact = dot(big_ref[...], taps[:144])
    offs = offs_ref[...]
    bias = jnp.zeros((32, half), F32)
    slopes = []
    for sy in range(10):
        v = preact[sy * 32 : sy * 32 + 32] + offs
        sig = jax.nn.sigmoid(v)
        slope = (v * sig - goal_ref[sy]) * inv_pixels * (sig * (1.0 + v * (1.0 - sig)))
        if sy == 0:
            slope = jnp.where(s == 0, 0.0, slope)
        elif sy == 9:
            slope = jnp.where(s == n_space - 1, 0.0, slope)
        else:
            bias = bias + slope
        slopes.append(slope)
    slope_bf = jnp.concatenate(slopes, axis=0).astype(BF16)

    gt = dot(bigt_ref[...], slope_bf)
    site16 = lax.broadcasted_iota(jnp.int32, (TILE, half), 1)
    planes = []
    for q in range(2):
        left, mid, right = (gt[(q * 3 + b) * 16 : (q * 3 + b) * 16 + 16] for b in range(3))
        planes.append(
            mid
            + jnp.where(site16 == half - 1, 0.0, pltpu.roll(left, half - 1, 1))
            + jnp.where(site16 == 0, 0.0, pltpu.roll(right, 1, 1))
        )
    grad = jnp.concatenate(
        [
            jnp.concatenate([p[:, h * 128 : (h + 1) * 128] for p in planes], axis=1)
            for h in range(G // 2)
        ],
        axis=0,
    )
    m = grad.shape[0]
    terms = split(grad, 2)
    pq = dot(jnp.concatenate(terms, axis=0), wideh_ref[...])
    pq = pq[:m] + (pq[m:] + dot(terms[0], widel_ref[...]))
    for r in range(rows_out):
        g = r % G
        rows = slice((g // 2) * TILE, (g // 2 + 1) * TILE)
        c0 = (g % 2) * LANES
        p_ref[r * TILE : (r + 1) * TILE, :] = pq[rows, c0 : c0 + LANES]
        q_ref[r * TILE : (r + 1) * TILE, :] = -pq[rows, 256 + c0 : 256 + c0 + LANES]
    gre, gim = fft(
        [p_ref[pl.ds(n, rows_out, stride=16), :] for n in range(16)],
        [q_ref[pl.ds(n, rows_out, stride=16), :] for n in range(16)],
    )
    for k in range(16):
        rows = slice(k * rows_out, (k + 1) * rows_out)
        rows_im = slice((16 + k) * rows_out, (17 + k) * rows_out)
        ns_ref[rows, :] = gre[k] * h_ref[rows, :] + gim[k] * h_ref[rows_im, :]
    noise = ns_ref[pl.ds(0, 16, stride=rows_out), :]
    for r in range(1, rows_out):
        noise = noise + ns_ref[pl.ds(r, 16, stride=rows_out), :]
    noise = noise * (-1.0 / (256.0 * F))
    for step in (64, 32, 16):
        noise = noise + pltpu.roll(noise, step, 1)
    lane_tile = lax.broadcasted_iota(jnp.int32, (TILE, LANES), 1) // TILE
    spot = lax.broadcasted_iota(jnp.int32, (TILE, LANES), 0) % 8
    noise = jnp.where(lane_tile == spot, noise, 0.0)
    upper = jnp.sum(noise[:8], axis=0, keepdims=True)
    lower = jnp.sum(noise[8:], axis=0, keepdims=True)

    prod = dot(slope_bf[32:288], taps, ((1,), (1,)))
    gw = jnp.zeros((32, 256), F32)
    for sy in range(1, 9):
        gw = gw + pltpu.roll(prod[(sy - 1) * 32 : sy * 32], 256 - 2 * sy, 1)
    picked = dot(jnp.concatenate(split(gw, 3), axis=0), pick_ref[...])
    out_ref[0:32, :] = picked[0:32] + (picked[32:64] + picked[64:96])
    bias = jnp.broadcast_to(jnp.sum(bias, axis=1, keepdims=True), (32, LANES))
    diag = lax.broadcasted_iota(jnp.int32, (32, LANES), 0) == lax.broadcasted_iota(
        jnp.int32, (32, LANES), 1
    )
    bias = jnp.sum(jnp.where(diag, bias, 0.0), axis=0, keepdims=True)
    row = lax.broadcasted_iota(jnp.int32, (8, LANES), 0)
    tail = jnp.where(row == 0, bias, jnp.where(row == 1, upper, jnp.where(row == 2, lower, 0.0)))
    out_ref[32:40, :] = tail


def last_sum(own_ref, got_ref, weight_ref, bias_ref, noise_ref):
    total = own_ref[...] + got_ref[...]
    weight_ref[...] = total[:32, :36]
    bias_ref[...] = total[32:33, :32]
    noise_ref[...] = total[33:35]


def involution(value, count, step, first):
    pairs = []
    for i in range(first, count):
        j = ((i - first) ^ step) + first
        if j < count:
            pairs.append((i, j))
    return lax.ppermute(value, "space", pairs)


def sum_space(value, count):
    bits = count.bit_length() - 1
    assert 1 << bits == count
    stages = []
    at = 0
    while at < bits:
        width = 2 if at == 1 and bits - at >= 3 else 1
        stages.append([m << at for m in range(1, 1 << width)])
        at += width
    for masks in stages[:-1]:
        got = [lax.ppermute(value, "space", [(i, i ^ m) for i in range(count)]) for m in masks]
        value = value + got[0]
        if len(got) == 3:
            value = value + (got[1] + got[2])
    (mask,) = stages[-1]
    got = lax.ppermute(value, "space", [(i, i ^ mask) for i in range(count)])
    return value, got


def call(body, args, smem, outs, scratch, name):
    vm = pl.BlockSpec(memory_space=pltpu.VMEM)
    sm = pl.BlockSpec(memory_space=pltpu.SMEM)
    sizes = [int(np.prod(a.shape)) * a.dtype.itemsize for a in list(args) + list(outs)]
    sizes += [int(np.prod(a.shape)) * 4 for a in scratch]
    return pl.pallas_call(
        body,
        out_shape=tuple(outs),
        in_specs=[sm] * smem + [vm] * (len(args) - smem),
        out_specs=(vm,) * len(outs),
        scratch_shapes=scratch,
        compiler_params=pltpu.CompilerParams(vmem_limit_bytes=sum(sizes) + (12 << 20)),
        name=name,
    )(*args)


def shards(raw, shifts, weight, offset, log_var, goal):
    nf = lax.axis_size("frame")
    n_space = lax.axis_size("space")
    fl, band_rows, W = raw.shape
    T = shifts.shape[3]
    channels, site_rows, ws = goal.shape
    G = W // LANES
    F = nf * fl
    nsc = ws // LANES
    inv_pixels = 1.0 / (band_rows * n_space * W // 4)
    rows_out = max(G, 8)

    def from_frame(value, j):
        return lax.ppermute(value, "frame", [(i, (i - j) % nf) for i in range(nf)])

    def pieces(value):
        return [value] + [from_frame(value, j) for j in range(1, nf)]

    raws = pieces(raw)
    shift_parts = pieces(shifts)
    goals = pieces(goal)

    y = jnp.concatenate(
        [r.reshape(fl, TILE, G, LANES).transpose(0, 2, 1, 3).reshape(-1, LANES) for r in raws],
        axis=0,
    )
    yc = involution(y, n_space, 1, 0)
    yf = involution(y, n_space, 1, 1)
    goals = [g.transpose(1, 0, 2) for g in goals]
    dy = jnp.concatenate([v[:, 0, 0].reshape(-1) for v in shift_parts]) + TILE
    dx = jnp.concatenate([v[:, 1, 0] for v in shift_parts], axis=0)
    dx = jnp.repeat(dx, TILE, axis=1).reshape(F * G, LANES)
    idx = (dx + jnp.arange(LANES, dtype=jnp.int32)) & (LANES - 1)

    fwd, fwd_low, inv, inv_low, part, wide, wide_low = (jnp.asarray(t) for t in tables())
    place, place_t, pick = tap_tables()
    big = dot(weight, jnp.asarray(place.reshape(36, -1), BF16))
    big = big.reshape(channels, 10, 144).transpose(1, 0, 2).reshape(320, 144).astype(BF16)
    bigt = dot(jnp.asarray(place_t.reshape(-1, 36), BF16), weight.T)
    bigt = bigt.reshape(96, 320).astype(BF16)
    offs = jnp.broadcast_to(offset[:, None], (channels, W // 2))
    var = jnp.tile(jnp.exp(log_var).reshape(TILE, TILE), (1, 8))

    side = 4 * G + nf * nsc * channels
    shape = jax.ShapeDtypeStruct
    merged, pack, pc, pf, moments = call(
        functools.partial(merge_kernel, (nf, fl, G, T, nsc)),
        [dy, idx, y, yc, yf, *goals, fwd, fwd_low, inv, inv_low, var],
        1,
        [
            shape((TILE, W // nf), F32),
            shape((G, TILE, LANES), F32),
            shape((side, LANES), BF16),
            shape((side, LANES), BF16),
            shape((32 * rows_out, LANES), F32),
        ],
        [
            pltpu.VMEM((F * G, 3 * TILE, LANES), F32),
            pltpu.VMEM((256, LANES), F32),
            pltpu.VMEM((256, LANES), F32),
            pltpu.VMEM((16 * rows_out, LANES), F32),
            pltpu.VMEM((G, TILE, LANES), F32),
        ],
        "merge",
    )
    pc = involution(pc, n_space, 1, 0)
    pf = involution(pf, n_space, 1, 1)
    (partial,) = call(
        functools.partial(demosaic_kernel, (nf, fl, G, nsc, n_space, inv_pixels)),
        [pack, pc, pf, moments, *goals, part, wide, wide_low, jnp.asarray(pick), big, bigt, offs],
        0,
        [shape((40, LANES), F32)],
        [
            pltpu.VMEM((10, channels, W // 2), F32),
            pltpu.VMEM((G, 24, LANES), F32),
            pltpu.VMEM((rows_out * TILE, LANES), F32),
            pltpu.VMEM((rows_out * TILE, LANES), F32),
            pltpu.VMEM((rows_out * TILE, LANES), F32),
        ],
        "demosaic",
    )
    grad_weight, grad_bias, grad_noise = call(
        last_sum,
        sum_space(partial, n_space),
        0,
        [shape((channels, 36), F32), shape((1, channels), F32), shape((2, LANES), F32)],
        [],
        "last_sum",
    )
    return merged, grad_weight, grad_bias.reshape(channels), grad_noise.reshape(256)


def solution(mesh):
    placed = (
        P("frame", "space", None),
        P("frame", None, "space", None),
        P(),
        P(),
        P(),
        P(None, "space", "frame"),
    )
    return jax.shard_map(
        shards,
        mesh=mesh,
        in_specs=placed,
        out_specs=(P("space", "frame"), P(), P(), P()),
        check_vma=False,
    )
```

```python
import functools
import math

import jax
import jax.numpy as jnp
import ml_dtypes
import numpy as np
from jax import lax
from jax.experimental import pallas as pl
from jax.experimental.pallas import tpu as pltpu
from jax.sharding import PartitionSpec as P


TILE = 16
LANES = 128
F32 = jnp.float32
BF16 = jnp.bfloat16


def dot(a, b, dims=((1,), (0,))):
    return lax.dot_general(a, b, (dims, ((), ())), preferred_element_type=F32)


def split(value, parts):
    terms = []
    for _ in range(parts):
        term = value.astype(BF16)
        terms.append(term)
        value = value - term.astype(F32)
    return terms


def split_table(value, parts):
    terms = []
    value = value.astype(np.float64)
    for _ in range(parts):
        term = value.astype(np.float32).astype(ml_dtypes.bfloat16)
        terms.append(term)
        value = value - term.astype(np.float64)
    return terms


def tables():
    angle = 2.0 * math.pi / TILE * (np.outer(np.arange(TILE), np.arange(TILE)) % TILE)
    cos16, sin16 = np.cos(angle), np.sin(angle)
    eye8, eye16 = np.eye(8), np.eye(16)
    bc, bs = np.kron(eye8, cos16), np.kron(eye8, sin16)
    fwd = split_table(np.concatenate([bc, bs], axis=1), 3)
    fwd_main = np.concatenate(fwd[:2], axis=0)
    inv = split_table(np.concatenate([bc, -bs], axis=0), 3)
    inv_main = np.concatenate(inv[:2], axis=1)
    part = np.zeros((256, 256))
    for x in range(256):
        part[x, (x % 2) * 128 + x // 2] = 1.0
    wide = np.concatenate([np.kron(eye16, cos16), np.kron(eye16, sin16)], axis=1)
    wide = split_table(part.T @ wide, 2)
    return fwd_main, fwd[2], inv_main, inv[2], part.astype(ml_dtypes.bfloat16), wide[0], wide[1]


def tap_tables():
    place = np.zeros((36, 10, 144))
    back = np.zeros((96, 10, 36))
    pick = np.zeros((256, 128))
    for a in range(3):
        for b in range(3):
            for p in range(2):
                for q in range(2):
                    tap = (3 * a + b) * 4 + 2 * p + q
                    pick[(q * 3 + b) * 24 + 2 * a + p, tap] = 1.0
                    for sy in range(10):
                        r = 2 * (sy + a) + p
                        place[tap, sy, (q * 3 + b) * 24 + r] = 1.0
                        if 4 <= r < 20:
                            back[(q * 3 + b) * 16 + r - 4, sy, tap] = 1.0
    return place, back, pick.astype(ml_dtypes.bfloat16)


def turn(re, im, k, n):
    if k == 0:
        return re, im
    if 4 * k == n:
        return im, -re
    if 8 * k == n:
        half = math.sqrt(0.5)
        return (re + im) * half, (im - re) * half
    if 8 * k == 3 * n:
        half = math.sqrt(0.5)
        return (im - re) * half, (re + im) * -half
    c, s = math.cos(2.0 * math.pi * k / n), math.sin(2.0 * math.pi * k / n)
    return re * c + im * s, im * c - re * s


def fft(re, im):
    n = len(re)
    if n == 1:
        return re, im
    er, ei = fft(re[0::2], im[0::2])
    our, oi = fft(re[1::2], im[1::2])
    half = n // 2
    xr, xi = [None] * n, [None] * n
    for k in range(half):
        tr, ti = turn(our[k], oi[k], k, n)
        xr[k], xi[k] = er[k] + tr, ei[k] + ti
        xr[k + half], xi[k + half] = er[k] - tr, ei[k] - ti
    return xr, xi


def tree(values):
    while len(values) > 1:
        half = len(values) // 2
        values = [a + b for a, b in zip(values[:half], values[half:])]
    return values[0]


def add_lists(a, b):
    return b if a is None else [x + y for x, y in zip(a, b)]


def merge_kernel(dims, *refs):
    nf, fl, G, T, nsc = dims
    F = nf * fl
    dy_refs, refs = refs[:nf], refs[nf:]
    dx_refs, refs = refs[:nf], refs[nf:]
    goal_refs, refs = refs[:nf], refs[nf:]
    y_ref, yc_ref, yf_ref, fwd_ref, fwdl_ref, inv_ref, invl_ref, var_ref = refs[:8]
    merged_ref, pack_ref, pc_ref, pf_ref, h_ref = refs[8:13]
    x_ref, idx_ref, p_ref, q_ref, xs_ref, mm_ref, goal_ref = refs[13:]
    s = lax.axis_index("space")
    fr = lax.axis_index("frame")
    odd = lax.rem(s, 2)

    slots = ((y_ref, 1), (yc_ref, 2 - 2 * odd), (yf_ref, 2 * odd))

    def fill(f, carry):
        for ref, slot in slots:
            rows = ref[f].astype(F32)
            for g in range(G):
                block = rows[:, g * LANES : (g + 1) * LANES]
                x_ref[f * G + g, pl.ds(pl.multiple_of(slot * TILE, TILE), TILE), :] = block
        return carry

    lax.fori_loop(0, F, fill, 0, unroll=min(F, 4))

    spot = lax.broadcasted_iota(jnp.int32, (8, LANES), 1)
    for j in range(nf):
        for l in range(fl):
            row = dx_refs[j][l, 1]
            if T < LANES:
                row = jnp.concatenate([row, jnp.zeros((1, LANES - T), jnp.int32)], axis=1)
            row = jnp.broadcast_to(row, (8, LANES))
            for g in range(G):
                moved = jnp.take_along_axis(row, 8 * g + spot // TILE, axis=1)
                idx_ref[(j * fl + l) * G + g] = (moved + (spot - TILE)) & (LANES - 1)

    lead = G * 4
    for j in range(nf):
        for c in range(nsc):
            cols = slice(c * LANES, (c + 1) * LANES)
            goal_ref[j * nsc + c] = goal_refs[j][:, :, cols].astype(F32).reshape(256, LANES)
    for k in range(nf * nsc):
        rows = slice(lead + k * 32, lead + k * 32 + 32)
        pc_ref[rows, :] = goal_ref[k, pl.ds(7 - 7 * odd, 32, stride=8), :].astype(BF16)
        pf_ref[rows, :] = goal_ref[k, pl.ds(7 * odd, 32, stride=8), :].astype(BF16)

    lane = lax.broadcasted_iota(jnp.int32, (TILE, LANES), 1)
    kind = (lane // TILE) % 4
    per = 16 // G
    chunks = F * G // 16
    rows_out = max(G, 8)
    fold = TILE // rows_out
    zero = jnp.zeros((TILE, LANES), F32)

    def place(f):
        if nf == 2:
            return f
        return lax.rem(f // fl + nf - fr, nf) * fl + f % fl

    def row_shift(f, t):
        if isinstance(f, int):
            return dy_refs[f // fl][f % fl, 0, 0, t]
        j = lax.div(f, fl)
        l = lax.rem(f, fl)
        value = dy_refs[0][l, 0, 0, t]
        for k in range(1, nf):
            value = jnp.where(j == k, dy_refs[k][l, 0, 0, t], value)
        return value

    first = lax.rem(nf - fr, nf) * fl
    log_var = var_ref[...]
    variances = []
    for k in range(16):
        row = jnp.broadcast_to(log_var[k // 8 : k // 8 + 1], (8, LANES))
        row = jnp.take_along_axis(row, (k % 8) * TILE + spot % TILE, axis=1)
        variances.append(jnp.concatenate([row, row], axis=0))

    def chunk_step(c, carry):
        sums = carry[0] if carry is not None else None
        blocks = []
        for q in range(16):
            g = q % G
            f = place(c * per + q // G)

            def load(t, group):
                if group < 0 or group >= G:
                    return zero
                start = row_shift(f, 8 * g + t)
                return x_ref[f * G + group, pl.ds(start, TILE), :]

            idx = idx_ref[f * G + g]
            idx = jnp.concatenate([idx, idx], axis=0)
            mixes = (
                jnp.where(
                    lane < 40,
                    load(0, g),
                    jnp.where(lane < 104, load(4, g), load(0, g - 1)),
                ),
                jnp.where(lane < 56, load(1, g), load(5, g)),
                jnp.where(lane < 72, load(2, g), load(6, g)),
                jnp.where(
                    lane < 24,
                    load(7, g + 1),
                    jnp.where(lane < 88, load(3, g), load(7, g)),
                ),
            )
            moved = [jnp.take_along_axis(m, idx, axis=1) for m in mixes]
            blocks.append(
                jnp.where(
                    kind < 2,
                    jnp.where(kind == 0, moved[0], moved[1]),
                    jnp.where(kind == 2, moved[2], moved[3]),
                )
            )
        part = [tree(blocks[g::G]) for g in range(G)]
        sums = add_lists(sums, part)
        base = [x_ref[first * G + g, TILE : 2 * TILE, :] for g in range(G)]
        both = jnp.concatenate(blocks + base, axis=0).astype(BF16)
        pq = dot(jnp.concatenate([both, both], axis=1), fwd_ref[...]) + dot(both, fwdl_ref[...])
        for q in range(16):
            rows = slice(q * TILE, (q + 1) * TILE)
            ref_rows = slice(256 + (q % G) * TILE, 256 + (q % G + 1) * TILE)
            diff = pq[ref_rows] - pq[rows]
            p_ref[rows, :] = diff[:, :LANES]
            q_ref[rows, :] = -diff[:, LANES:]
        re, im = fft(
            [p_ref[pl.ds(n, 16, stride=16), :] for n in range(16)],
            [q_ref[pl.ds(n, 16, stride=16), :] for n in range(16)],
        )
        out = [[], [], [], []]
        for k in range(16):
            energy = re[k] * re[k] + im[k] * im[k]
            weight = energy / (energy + variances[k])
            wr = weight * re[k]
            wi = weight * im[k]
            rest = 1.0 - weight
            for store, val in zip(out, (wr, wi, wr * rest, wi * rest)):
                if fold == 2:
                    val = val[:8] + val[8:]
                store.append(val)
        flat = out[0] + out[1] + out[2] + out[3]
        return sums, add_lists(carry[1] if carry is not None else None, flat)

    carry = chunk_step(0, None)
    if chunks > 1:
        carry = lax.fori_loop(1, chunks, chunk_step, carry)
    sums, flat = carry
    for k in range(32):
        h_ref[k * rows_out : (k + 1) * rows_out, :] = flat[32 + k]

    vi, ur = fft(flat[16:32], flat[:16])
    uv = jnp.concatenate(
        [jnp.concatenate(ur, axis=0), jnp.concatenate(vi, axis=0)], axis=1
    )
    m = 16 * rows_out
    terms = split(uv, 3)
    wide = dot(jnp.concatenate(terms, axis=0), inv_ref[...])
    pix = wide[:m, :LANES] + (wide[m : 2 * m, :LANES] + wide[:m, LANES:])
    pix = pix + (wide[2 * m :, :LANES] + wide[m : 2 * m, LANES:] + dot(terms[0], invl_ref[...]))
    xs_ref[...] = pix
    for g in range(G):
        val = xs_ref[pl.ds(g, 16, stride=rows_out), :]
        for other in range(g + G, rows_out, G):
            val = val + xs_ref[pl.ds(other, 16, stride=rows_out), :]
        val = (sums[g] + val / 256.0) / F
        mm_ref[g] = val
        pack_ref[g] = val
    own = G // nf
    for k in range(own):
        merged_ref[:, k * LANES : (k + 1) * LANES] = mm_ref[fr * own + k]
    low = jnp.concatenate([mm_ref[g, 0:4, :] for g in range(G)], axis=0)
    high = jnp.concatenate([mm_ref[g, 12:16, :] for g in range(G)], axis=0)
    pc_ref[0:lead, :] = jnp.where(odd == 1, low, high).astype(BF16)
    pf_ref[0:lead, :] = jnp.where(odd == 1, high, low).astype(BF16)


def demosaic_kernel(dims, pack_ref, pc_ref, pf_ref, h_ref, *refs):
    nf, fl, G, nsc, n_space, inv_pixels = dims
    F = nf * fl
    W = G * LANES
    half = W // 2
    goal_refs = refs[:nf]
    part_ref, wideh_ref, widel_ref, pick_ref, big_ref, bigt_ref, offs_ref = refs[nf : nf + 7]
    out_ref, goal_ref, raw_ref, mm_ref, p_ref, q_ref, ns_ref = refs[nf + 7 :]
    s = lax.axis_index("space")
    fr = lax.axis_index("frame")
    odd = lax.rem(s, 2)
    rows_out = max(G, 8)

    lead = G * 4
    for j in range(nf):
        at = pl.multiple_of(lax.rem(fr + j, nf) * (nsc * LANES), LANES)
        for c in range(nsc):
            cols = slice(c * LANES, (c + 1) * LANES)
            raw_ref[...] = goal_refs[j][:, :, cols].astype(F32).reshape(256, LANES)
            to = pl.ds(pl.multiple_of(at + c * LANES, LANES), LANES)
            for r in range(8):
                goal_ref[r + 1, :, to] = raw_ref[pl.ds(r, 32, stride=8), :]
        for ref, row in ((pc_ref, 9 - 9 * odd), (pf_ref, 9 * odd)):
            for c in range(nsc):
                first = lead + (j * nsc + c) * 32
                val = ref[first : first + 32, :].astype(F32)
                goal_ref[row, :, pl.ds(pl.multiple_of(at + c * LANES, LANES), LANES)] = val

    near = pc_ref[0:lead, :].astype(F32)
    far = pf_ref[0:lead, :].astype(F32)
    low = jnp.where(odd == 1, near, far)
    high = jnp.where(odd == 1, far, near)
    for g in range(G):
        mm_ref[g, 0:4, :] = low[4 * g : 4 * g + 4]
        mm_ref[g, 4:20, :] = pack_ref[g]
        mm_ref[g, 20:24, :] = high[4 * g : 4 * g + 4]
    pairs = jnp.concatenate(
        [jnp.concatenate([mm_ref[2 * h], mm_ref[2 * h + 1]], axis=1) for h in range(G // 2)],
        axis=0,
    )
    parted = dot(pairs.astype(BF16), part_ref[...])
    site = lax.broadcasted_iota(jnp.int32, (24, half), 1)
    pieces = []
    for q in range(2):
        plane = jnp.concatenate(
            [parted[24 * h : 24 * h + 24, q * 128 : (q + 1) * 128] for h in range(G // 2)], axis=1
        )
        pieces.append(jnp.where(site == 0, 0.0, pltpu.roll(plane, 1, 1)))
        pieces.append(plane)
        pieces.append(jnp.where(site == half - 1, 0.0, pltpu.roll(plane, half - 1, 1)))
    pieces.append(jnp.zeros((112, half), F32))
    taps = jnp.concatenate(pieces, axis=0).astype(BF16)

    preact = dot(big_ref[...], taps[:144])
    diag = lax.broadcasted_iota(jnp.int32, (32, LANES), 0) == lax.broadcasted_iota(
        jnp.int32, (32, LANES), 1
    )
    offs = jnp.concatenate([offs_ref[...], jnp.zeros((1, LANES - 32), F32)], axis=1)
    offs = jnp.where(diag, jnp.broadcast_to(offs, (32, LANES)), 0.0)
    offs = jnp.broadcast_to(jnp.sum(offs, axis=1, keepdims=True), (32, half))
    bias = jnp.zeros((32, half), F32)
    slopes = []
    for sy in range(10):
        v = preact[sy * 32 : sy * 32 + 32] + offs
        sig = jax.nn.sigmoid(v)
        slope = (v * sig - goal_ref[sy]) * inv_pixels * (sig * (1.0 + v * (1.0 - sig)))
        if sy == 0:
            slope = jnp.where(s == 0, 0.0, slope)
        elif sy == 9:
            slope = jnp.where(s == n_space - 1, 0.0, slope)
        else:
            bias = bias + slope
        slopes.append(slope)
    slope_bf = jnp.concatenate(slopes, axis=0).astype(BF16)

    gt = dot(bigt_ref[...], slope_bf)
    site16 = lax.broadcasted_iota(jnp.int32, (TILE, half), 1)
    planes = []
    for q in range(2):
        left, mid, right = (gt[(q * 3 + b) * 16 : (q * 3 + b) * 16 + 16] for b in range(3))
        planes.append(
            mid
            + jnp.where(site16 == half - 1, 0.0, pltpu.roll(left, half - 1, 1))
            + jnp.where(site16 == 0, 0.0, pltpu.roll(right, 1, 1))
        )
    grad = jnp.concatenate(
        [
            jnp.concatenate([p[:, h * 128 : (h + 1) * 128] for p in planes], axis=1)
            for h in range(G // 2)
        ],
        axis=0,
    )
    m = grad.shape[0]
    terms = split(grad, 2)
    pq = dot(jnp.concatenate(terms, axis=0), wideh_ref[...])
    pq = pq[:m] + (pq[m:] + dot(terms[0], widel_ref[...]))
    for r in range(rows_out):
        g = r % G
        rows = slice((g // 2) * TILE, (g // 2 + 1) * TILE)
        c0 = (g % 2) * LANES
        p_ref[r * TILE : (r + 1) * TILE, :] = pq[rows, c0 : c0 + LANES]
        q_ref[r * TILE : (r + 1) * TILE, :] = -pq[rows, 256 + c0 : 256 + c0 + LANES]
    gre, gim = fft(
        [p_ref[pl.ds(n, rows_out, stride=16), :] for n in range(16)],
        [q_ref[pl.ds(n, rows_out, stride=16), :] for n in range(16)],
    )
    for k in range(16):
        rows = slice(k * rows_out, (k + 1) * rows_out)
        rows_im = slice((16 + k) * rows_out, (17 + k) * rows_out)
        ns_ref[rows, :] = gre[k] * h_ref[rows, :] + gim[k] * h_ref[rows_im, :]
    noise = ns_ref[pl.ds(0, 16, stride=rows_out), :]
    for r in range(1, rows_out):
        noise = noise + ns_ref[pl.ds(r, 16, stride=rows_out), :]
    noise = noise * (-1.0 / (256.0 * F))
    for step in (64, 32, 16):
        noise = noise + pltpu.roll(noise, step, 1)
    lane_tile = lax.broadcasted_iota(jnp.int32, (TILE, LANES), 1) // TILE
    spot = lax.broadcasted_iota(jnp.int32, (TILE, LANES), 0) % 8
    noise = jnp.where(lane_tile == spot, noise, 0.0)
    upper = jnp.sum(noise[:8], axis=0, keepdims=True)
    lower = jnp.sum(noise[8:], axis=0, keepdims=True)

    prod = dot(slope_bf[32:288], taps, ((1,), (1,)))
    gw = jnp.zeros((32, 256), F32)
    for sy in range(1, 9):
        gw = gw + pltpu.roll(prod[(sy - 1) * 32 : sy * 32], 256 - 2 * sy, 1)
    picked = dot(jnp.concatenate(split(gw, 3), axis=0), pick_ref[...])
    out_ref[0:32, :] = picked[0:32] + (picked[32:64] + picked[64:96])
    bias = jnp.broadcast_to(jnp.sum(bias, axis=1, keepdims=True), (32, LANES))
    bias = jnp.sum(jnp.where(diag, bias, 0.0), axis=0, keepdims=True)
    row = lax.broadcasted_iota(jnp.int32, (8, LANES), 0)
    tail = jnp.where(row == 0, bias, jnp.where(row == 1, upper, jnp.where(row == 2, lower, 0.0)))
    out_ref[32:40, :] = tail


def last_sum(own_ref, got_ref, weight_ref, bias_ref, noise_ref):
    total = own_ref[...] + got_ref[...]
    weight_ref[...] = total[:32, :36]
    bias_ref[...] = total[32:33, :32]
    noise_ref[...] = total[33:35]


def involution(value, count, step, first):
    pairs = []
    for i in range(first, count):
        j = ((i - first) ^ step) + first
        if j < count:
            pairs.append((i, j))
    return lax.ppermute(value, "space", pairs)


def sum_space(value, count):
    bits = count.bit_length() - 1
    assert 1 << bits == count
    stages = []
    at = 0
    while at < bits:
        width = 2 if at == 1 and bits - at >= 3 else 1
        stages.append([m << at for m in range(1, 1 << width)])
        at += width
    for masks in stages[:-1]:
        got = [lax.ppermute(value, "space", [(i, i ^ m) for i in range(count)]) for m in masks]
        value = value + got[0]
        if len(got) == 3:
            value = value + (got[1] + got[2])
    (mask,) = stages[-1]
    got = lax.ppermute(value, "space", [(i, i ^ mask) for i in range(count)])
    return value, got


def call(body, args, smem, outs, scratch):
    vm = pl.BlockSpec(memory_space=pltpu.VMEM)
    sm = pl.BlockSpec(memory_space=pltpu.SMEM)
    sizes = [int(np.prod(a.shape)) * a.dtype.itemsize for a in list(args) + list(outs)]
    sizes += [int(np.prod(a.shape)) * 4 for a in scratch]
    return pl.pallas_call(
        body,
        out_shape=tuple(outs),
        in_specs=[sm] * smem + [vm] * (len(args) - smem),
        out_specs=(vm,) * len(outs),
        scratch_shapes=scratch,
        compiler_params=pltpu.CompilerParams(vmem_limit_bytes=sum(sizes) + (12 << 20)),
    )(*args)


def shards(raw, shifts, weight, offset, log_var, goal):
    nf = lax.axis_size("frame")
    n_space = lax.axis_size("space")
    fl, band_rows, W = raw.shape
    T = shifts.shape[3]
    channels, _, ws = goal.shape
    G = W // LANES
    F = nf * fl
    nsc = ws // LANES
    inv_pixels = 1.0 / (band_rows * n_space * W // 4)
    rows_out = max(G, 8)

    def from_frame(value, j):
        return lax.ppermute(value, "frame", [(i, (i - j) % nf) for i in range(nf)])

    def pieces(value):
        return [value] + [from_frame(value, j) for j in range(1, nf)]

    raws = pieces(raw)
    shift_parts = pieces(shifts)
    shift_parts = [v + TILE for v in shift_parts]
    y = jnp.concatenate(raws, axis=0)
    yf = involution(y, n_space, 1, 1)
    yc = involution(y, n_space, 1, 0)
    goals = pieces(goal)

    fwd, fwd_low, inv, inv_low, part, wide, wide_low = (jnp.asarray(t) for t in tables())
    place, place_t, pick = tap_tables()
    side = 4 * G + nf * nsc * channels
    shape = jax.ShapeDtypeStruct
    merged, pack, pc, pf, moments = call(
        functools.partial(merge_kernel, (nf, fl, G, T, nsc)),
        [*shift_parts, *shift_parts, *goals, y, yc, yf]
        + [fwd, fwd_low, inv, inv_low, jnp.exp(log_var).reshape(2, LANES)],
        nf,
        [
            shape((TILE, W // nf), F32),
            shape((G, TILE, LANES), F32),
            shape((side, LANES), BF16),
            shape((side, LANES), BF16),
            shape((32 * rows_out, LANES), F32),
        ],
        [
            pltpu.VMEM((F * G, 3 * TILE, LANES), F32),
            pltpu.VMEM((F * G, 8, LANES), jnp.int32),
            pltpu.VMEM((256, LANES), F32),
            pltpu.VMEM((256, LANES), F32),
            pltpu.VMEM((16 * rows_out, LANES), F32),
            pltpu.VMEM((G, TILE, LANES), F32),
            pltpu.VMEM((nf * nsc, 256, LANES), F32),
        ],
    )
    pc, pf, weight = lax.optimization_barrier((pc, pf, weight))
    pf = involution(pf, n_space, 1, 1)
    pc = involution(pc, n_space, 1, 0)
    big = dot(weight, jnp.asarray(place.reshape(36, -1), BF16))
    big = big.reshape(channels, 10, 144).transpose(1, 0, 2).reshape(320, 144).astype(BF16)
    bigt = dot(jnp.asarray(place_t.reshape(-1, 36), BF16), weight.T)
    bigt = bigt.reshape(96, 320).astype(BF16)
    (partial,) = call(
        functools.partial(demosaic_kernel, (nf, fl, G, nsc, n_space, inv_pixels)),
        [pack, pc, pf, moments, *goals, part, wide, wide_low, jnp.asarray(pick), big, bigt]
        + [offset.reshape(1, channels)],
        0,
        [shape((40, LANES), F32)],
        [
            pltpu.VMEM((10, channels, W // 2), F32),
            pltpu.VMEM((256, LANES), F32),
            pltpu.VMEM((G, 24, LANES), F32),
            pltpu.VMEM((rows_out * TILE, LANES), F32),
            pltpu.VMEM((rows_out * TILE, LANES), F32),
            pltpu.VMEM((rows_out * TILE, LANES), F32),
        ],
    )
    grad_weight, grad_bias, grad_noise = call(
        last_sum,
        sum_space(partial, n_space),
        0,
        [shape((channels, 36), F32), shape((1, channels), F32), shape((2, LANES), F32)],
        [],
    )
    return merged, grad_weight, grad_bias.reshape(channels), grad_noise.reshape(256)


def solution(mesh):
    placed = (
        P("frame", "space", None),
        P("frame", None, "space", None),
        P(),
        P(),
        P(),
        P(None, "space", "frame"),
    )

    return jax.shard_map(
        shards,
        mesh=mesh,
        in_specs=placed,
        out_specs=(P("space", "frame"), P(), P(), P()),
        check_vma=False,
    )
```

```python
import functools
import math

import jax
import jax.numpy as jnp
import ml_dtypes
import numpy as np
from jax import lax
from jax.experimental import pallas as pl
from jax.experimental.pallas import tpu as pltpu
from jax.sharding import PartitionSpec as P


TILE = 16
LANES = 128
F32 = jnp.float32
BF16 = jnp.bfloat16


def dot(a, b, dims=((1,), (0,))):
    return lax.dot_general(a, b, (dims, ((), ())), preferred_element_type=F32)


def split(value, parts):
    terms = []
    for _ in range(parts):
        term = value.astype(BF16)
        terms.append(term)
        value = value - term.astype(F32)
    return terms


def split_table(value, parts):
    terms = []
    value = value.astype(np.float64)
    for _ in range(parts):
        term = value.astype(np.float32).astype(ml_dtypes.bfloat16)
        terms.append(term)
        value = value - term.astype(np.float64)
    return terms


def tables():
    angle = 2.0 * math.pi / TILE * (np.outer(np.arange(TILE), np.arange(TILE)) % TILE)
    cos16, sin16 = np.cos(angle), np.sin(angle)
    eye8, eye16 = np.eye(8), np.eye(16)
    bc, bs = np.kron(eye8, cos16), np.kron(eye8, sin16)
    fwd = split_table(np.concatenate([bc, bs], axis=1), 3)
    fwd_main = np.concatenate(fwd[:2], axis=0)
    inv = split_table(np.concatenate([bc, -bs], axis=0), 3)
    inv_main = np.concatenate(inv[:2], axis=1)
    part = np.zeros((256, 256))
    for x in range(256):
        part[x, (x % 2) * 128 + x // 2] = 1.0
    wide = np.concatenate([np.kron(eye16, cos16), np.kron(eye16, sin16)], axis=1)
    wide = split_table(part.T @ wide, 2)
    return fwd_main, fwd[2], inv_main, inv[2], part.astype(ml_dtypes.bfloat16), wide[0], wide[1]


def tap_tables():
    place = np.zeros((36, 10, 144))
    back = np.zeros((96, 10, 36))
    pick = np.zeros((256, 128))
    for a in range(3):
        for b in range(3):
            for p in range(2):
                for q in range(2):
                    tap = (3 * a + b) * 4 + 2 * p + q
                    pick[(q * 3 + b) * 24 + 2 * a + p, tap] = 1.0
                    for sy in range(10):
                        r = 2 * (sy + a) + p
                        place[tap, sy, (q * 3 + b) * 24 + r] = 1.0
                        if 4 <= r < 20:
                            back[(q * 3 + b) * 16 + r - 4, sy, tap] = 1.0
    return place, back, pick.astype(ml_dtypes.bfloat16)


def turn(re, im, k, n):
    if k == 0:
        return re, im
    if 4 * k == n:
        return im, -re
    if 8 * k == n:
        half = math.sqrt(0.5)
        return (re + im) * half, (im - re) * half
    if 8 * k == 3 * n:
        half = math.sqrt(0.5)
        return (im - re) * half, (re + im) * -half
    c, s = math.cos(2.0 * math.pi * k / n), math.sin(2.0 * math.pi * k / n)
    return re * c + im * s, im * c - re * s


def fft(re, im):
    n = len(re)
    if n == 1:
        return re, im
    er, ei = fft(re[0::2], im[0::2])
    our, oi = fft(re[1::2], im[1::2])
    half = n // 2
    xr, xi = [None] * n, [None] * n
    for k in range(half):
        tr, ti = turn(our[k], oi[k], k, n)
        xr[k], xi[k] = er[k] + tr, ei[k] + ti
        xr[k + half], xi[k + half] = er[k] - tr, ei[k] - ti
    return xr, xi


def tree(values):
    while len(values) > 1:
        half = len(values) // 2
        values = [a + b for a, b in zip(values[:half], values[half:])]
    return values[0]


def add_lists(a, b):
    return b if a is None else [x + y for x, y in zip(a, b)]


def merge_kernel(dims, *refs):
    nf, fl, G, T, nsc = dims
    F = nf * fl
    dy_refs, refs = refs[:nf], refs[nf:]
    dx_refs, refs = refs[:nf], refs[nf:]
    goal_refs, refs = refs[:nf], refs[nf:]
    y_ref, yc_ref, yf_ref, fwd_ref, fwdl_ref, inv_ref, invl_ref, var_ref = refs[:8]
    merged_ref, pack_ref, pc_ref, pf_ref, h_ref = refs[8:13]
    x_ref, idx_ref, p_ref, q_ref, xs_ref, mm_ref, goal_ref = refs[13:20]
    held, sems = refs[20:24], refs[24]
    loads = [
        pltpu.make_async_copy(src, dst, sems.at[k])
        for k, (src, dst) in enumerate(zip((fwd_ref, fwdl_ref, inv_ref, invl_ref), held))
    ]
    for copy in loads:
        copy.start()
    fwd_ref, fwdl_ref, inv_ref, invl_ref = held
    s = lax.axis_index("space")
    fr = lax.axis_index("frame")
    odd = lax.rem(s, 2)

    slots = ((y_ref, 1), (yc_ref, 2 - 2 * odd), (yf_ref, 2 * odd))

    def fill(f, carry):
        for ref, slot in slots:
            rows = ref[f].astype(F32)
            for g in range(G):
                block = rows[:, g * LANES : (g + 1) * LANES]
                x_ref[f * G + g, pl.ds(pl.multiple_of(slot * TILE, TILE), TILE), :] = block
        return carry

    lax.fori_loop(0, F, fill, 0, unroll=min(F, 4))

    spot = lax.broadcasted_iota(jnp.int32, (8, LANES), 1)
    for j in range(nf):
        for l in range(fl):
            row = dx_refs[j][l, 1]
            if T < LANES:
                row = jnp.concatenate([row, jnp.zeros((1, LANES - T), jnp.int32)], axis=1)
            row = jnp.broadcast_to(row, (8, LANES))
            for g in range(G):
                moved = jnp.take_along_axis(row, 8 * g + spot // TILE, axis=1)
                idx_ref[(j * fl + l) * G + g] = (moved + (spot - TILE)) & (LANES - 1)

    lead = G * 4
    for j in range(nf):
        for c in range(nsc):
            cols = slice(c * LANES, (c + 1) * LANES)
            goal_ref[j * nsc + c] = goal_refs[j][:, :, cols].astype(F32).reshape(256, LANES)
    for k in range(nf * nsc):
        rows = slice(lead + k * 32, lead + k * 32 + 32)
        pc_ref[rows, :] = goal_ref[k, pl.ds(7 - 7 * odd, 32, stride=8), :].astype(BF16)
        pf_ref[rows, :] = goal_ref[k, pl.ds(7 * odd, 32, stride=8), :].astype(BF16)

    lane = lax.broadcasted_iota(jnp.int32, (TILE, LANES), 1)
    kind = (lane // TILE) % 4
    per = 16 // G
    chunks = F * G // 16
    rows_out = max(G, 8)
    fold = TILE // rows_out
    zero = jnp.zeros((TILE, LANES), F32)

    def place(f):
        if nf == 2:
            return f
        return lax.rem(f // fl + nf - fr, nf) * fl + f % fl

    def row_shift(f, t):
        if isinstance(f, int):
            return dy_refs[f // fl][f % fl, 0, 0, t]
        j = lax.div(f, fl)
        l = lax.rem(f, fl)
        value = dy_refs[0][l, 0, 0, t]
        for k in range(1, nf):
            value = jnp.where(j == k, dy_refs[k][l, 0, 0, t], value)
        return value

    first = lax.rem(nf - fr, nf) * fl
    log_var = var_ref[...]
    variances = []
    for k in range(16):
        row = jnp.broadcast_to(log_var[k // 8 : k // 8 + 1], (8, LANES))
        row = jnp.take_along_axis(row, (k % 8) * TILE + spot % TILE, axis=1)
        variances.append(jnp.concatenate([row, row], axis=0))

    def chunk_step(c, carry):
        sums = carry[0] if carry is not None else None
        blocks = []
        for q in range(16):
            g = q % G
            f = place(c * per + q // G)

            def load(t, group):
                if group < 0 or group >= G:
                    return zero
                start = row_shift(f, 8 * g + t)
                return x_ref[f * G + group, pl.ds(start, TILE), :]

            idx = idx_ref[f * G + g]
            idx = jnp.concatenate([idx, idx], axis=0)
            mixes = (
                jnp.where(
                    lane < 40,
                    load(0, g),
                    jnp.where(lane < 104, load(4, g), load(0, g - 1)),
                ),
                jnp.where(lane < 56, load(1, g), load(5, g)),
                jnp.where(lane < 72, load(2, g), load(6, g)),
                jnp.where(
                    lane < 24,
                    load(7, g + 1),
                    jnp.where(lane < 88, load(3, g), load(7, g)),
                ),
            )
            moved = [jnp.take_along_axis(m, idx, axis=1) for m in mixes]
            blocks.append(
                jnp.where(
                    kind < 2,
                    jnp.where(kind == 0, moved[0], moved[1]),
                    jnp.where(kind == 2, moved[2], moved[3]),
                )
            )
        part = [tree(blocks[g::G]) for g in range(G)]
        sums = add_lists(sums, part)
        base = [x_ref[first * G + g, TILE : 2 * TILE, :] for g in range(G)]
        both = jnp.concatenate(blocks + base, axis=0).astype(BF16)
        if carry is None:
            loads[0].wait()
            loads[1].wait()
        pq = dot(jnp.concatenate([both, both], axis=1), fwd_ref[...]) + dot(both, fwdl_ref[...])
        for q in range(16):
            rows = slice(q * TILE, (q + 1) * TILE)
            ref_rows = slice(256 + (q % G) * TILE, 256 + (q % G + 1) * TILE)
            diff = pq[ref_rows] - pq[rows]
            p_ref[rows, :] = diff[:, :LANES]
            q_ref[rows, :] = -diff[:, LANES:]
        re, im = fft(
            [p_ref[pl.ds(n, 16, stride=16), :] for n in range(16)],
            [q_ref[pl.ds(n, 16, stride=16), :] for n in range(16)],
        )
        out = [[], [], [], []]
        for k in range(16):
            energy = re[k] * re[k] + im[k] * im[k]
            weight = energy / (energy + variances[k])
            wr = weight * re[k]
            wi = weight * im[k]
            rest = 1.0 - weight
            for store, val in zip(out, (wr, wi, wr * rest, wi * rest)):
                if fold == 2:
                    val = val[:8] + val[8:]
                store.append(val)
        flat = out[0] + out[1] + out[2] + out[3]
        return sums, add_lists(carry[1] if carry is not None else None, flat)

    carry = chunk_step(0, None)
    if chunks > 1:
        carry = lax.fori_loop(1, chunks, chunk_step, carry)
    sums, flat = carry
    for k in range(32):
        h_ref[k * rows_out : (k + 1) * rows_out, :] = flat[32 + k]

    vi, ur = fft(flat[16:32], flat[:16])
    uv = jnp.concatenate(
        [jnp.concatenate(ur, axis=0), jnp.concatenate(vi, axis=0)], axis=1
    )
    m = 16 * rows_out
    terms = split(uv, 3)
    loads[2].wait()
    loads[3].wait()
    wide = dot(jnp.concatenate(terms, axis=0), inv_ref[...])
    pix = wide[:m, :LANES] + (wide[m : 2 * m, :LANES] + wide[:m, LANES:])
    pix = pix + (wide[2 * m :, :LANES] + wide[m : 2 * m, LANES:] + dot(terms[0], invl_ref[...]))
    xs_ref[...] = pix
    for g in range(G):
        val = xs_ref[pl.ds(g, 16, stride=rows_out), :]
        for other in range(g + G, rows_out, G):
            val = val + xs_ref[pl.ds(other, 16, stride=rows_out), :]
        val = (sums[g] + val / 256.0) / F
        mm_ref[g] = val
        pack_ref[g] = val
    own = G // nf
    for k in range(own):
        merged_ref[:, k * LANES : (k + 1) * LANES] = mm_ref[fr * own + k]
    low = jnp.concatenate([mm_ref[g, 0:4, :] for g in range(G)], axis=0)
    high = jnp.concatenate([mm_ref[g, 12:16, :] for g in range(G)], axis=0)
    pc_ref[0:lead, :] = jnp.where(odd == 1, low, high).astype(BF16)
    pf_ref[0:lead, :] = jnp.where(odd == 1, high, low).astype(BF16)


def demosaic_kernel(dims, pack_ref, pc_ref, pf_ref, h_ref, *refs):
    nf, fl, G, nsc, n_space, inv_pixels = dims
    F = nf * fl
    W = G * LANES
    half = W // 2
    goal_refs = refs[:nf]
    part_ref, wideh_ref, widel_ref, pick_ref, big_ref, bigt_ref, offs_ref = refs[nf : nf + 7]
    out_ref, goal_ref, raw_ref, mm_ref, p_ref, q_ref, ns_ref = refs[nf + 7 : nf + 14]
    held, sems = refs[nf + 14 : nf + 17], refs[nf + 17]
    loads = [
        pltpu.make_async_copy(src, dst, sems.at[k])
        for k, (src, dst) in enumerate(zip((wideh_ref, widel_ref, pick_ref), held))
    ]
    for copy in loads:
        copy.start()
    wideh_ref, widel_ref, pick_ref = held
    s = lax.axis_index("space")
    fr = lax.axis_index("frame")
    odd = lax.rem(s, 2)
    rows_out = max(G, 8)

    lead = G * 4
    for j in range(nf):
        at = pl.multiple_of(lax.rem(fr + j, nf) * (nsc * LANES), LANES)
        for c in range(nsc):
            cols = slice(c * LANES, (c + 1) * LANES)
            raw_ref[...] = goal_refs[j][:, :, cols].astype(F32).reshape(256, LANES)
            to = pl.ds(pl.multiple_of(at + c * LANES, LANES), LANES)
            for r in range(8):
                goal_ref[r + 1, :, to] = raw_ref[pl.ds(r, 32, stride=8), :]
        for ref, row in ((pc_ref, 9 - 9 * odd), (pf_ref, 9 * odd)):
            for c in range(nsc):
                first = lead + (j * nsc + c) * 32
                val = ref[first : first + 32, :].astype(F32)
                goal_ref[row, :, pl.ds(pl.multiple_of(at + c * LANES, LANES), LANES)] = val

    near = pc_ref[0:lead, :].astype(F32)
    far = pf_ref[0:lead, :].astype(F32)
    low = jnp.where(odd == 1, near, far)
    high = jnp.where(odd == 1, far, near)
    for g in range(G):
        mm_ref[g, 0:4, :] = low[4 * g : 4 * g + 4]
        mm_ref[g, 4:20, :] = pack_ref[g]
        mm_ref[g, 20:24, :] = high[4 * g : 4 * g + 4]
    pairs = jnp.concatenate(
        [jnp.concatenate([mm_ref[2 * h], mm_ref[2 * h + 1]], axis=1) for h in range(G // 2)],
        axis=0,
    )
    parted = dot(pairs.astype(BF16), part_ref[...])
    site = lax.broadcasted_iota(jnp.int32, (24, half), 1)
    pieces = []
    for q in range(2):
        plane = jnp.concatenate(
            [parted[24 * h : 24 * h + 24, q * 128 : (q + 1) * 128] for h in range(G // 2)], axis=1
        )
        pieces.append(jnp.where(site == 0, 0.0, pltpu.roll(plane, 1, 1)))
        pieces.append(plane)
        pieces.append(jnp.where(site == half - 1, 0.0, pltpu.roll(plane, half - 1, 1)))
    pieces.append(jnp.zeros((112, half), F32))
    taps = jnp.concatenate(pieces, axis=0).astype(BF16)

    preact = dot(big_ref[...], taps[:144])
    diag = lax.broadcasted_iota(jnp.int32, (32, LANES), 0) == lax.broadcasted_iota(
        jnp.int32, (32, LANES), 1
    )
    offs = jnp.concatenate([offs_ref[...], jnp.zeros((1, LANES - 32), F32)], axis=1)
    offs = jnp.where(diag, jnp.broadcast_to(offs, (32, LANES)), 0.0)
    offs = jnp.broadcast_to(jnp.sum(offs, axis=1, keepdims=True), (32, half))
    bias = jnp.zeros((32, half), F32)
    slopes = []
    for sy in range(10):
        v = preact[sy * 32 : sy * 32 + 32] + offs
        sig = jax.nn.sigmoid(v)
        slope = (v * sig - goal_ref[sy]) * inv_pixels * (sig * (1.0 + v * (1.0 - sig)))
        if sy == 0:
            slope = jnp.where(s == 0, 0.0, slope)
        elif sy == 9:
            slope = jnp.where(s == n_space - 1, 0.0, slope)
        else:
            bias = bias + slope
        slopes.append(slope)
    slope_bf = jnp.concatenate(slopes, axis=0).astype(BF16)

    gt = dot(bigt_ref[...], slope_bf)
    site16 = lax.broadcasted_iota(jnp.int32, (TILE, half), 1)
    planes = []
    for q in range(2):
        left, mid, right = (gt[(q * 3 + b) * 16 : (q * 3 + b) * 16 + 16] for b in range(3))
        planes.append(
            mid
            + jnp.where(site16 == half - 1, 0.0, pltpu.roll(left, half - 1, 1))
            + jnp.where(site16 == 0, 0.0, pltpu.roll(right, 1, 1))
        )
    grad = jnp.concatenate(
        [
            jnp.concatenate([p[:, h * 128 : (h + 1) * 128] for p in planes], axis=1)
            for h in range(G // 2)
        ],
        axis=0,
    )
    m = grad.shape[0]
    terms = split(grad, 2)
    for copy in loads:
        copy.wait()
    pq = dot(jnp.concatenate(terms, axis=0), wideh_ref[...])
    pq = pq[:m] + (pq[m:] + dot(terms[0], widel_ref[...]))
    for r in range(rows_out):
        g = r % G
        rows = slice((g // 2) * TILE, (g // 2 + 1) * TILE)
        c0 = (g % 2) * LANES
        p_ref[r * TILE : (r + 1) * TILE, :] = pq[rows, c0 : c0 + LANES]
        q_ref[r * TILE : (r + 1) * TILE, :] = -pq[rows, 256 + c0 : 256 + c0 + LANES]
    gre, gim = fft(
        [p_ref[pl.ds(n, rows_out, stride=16), :] for n in range(16)],
        [q_ref[pl.ds(n, rows_out, stride=16), :] for n in range(16)],
    )
    for k in range(16):
        rows = slice(k * rows_out, (k + 1) * rows_out)
        rows_im = slice((16 + k) * rows_out, (17 + k) * rows_out)
        ns_ref[rows, :] = gre[k] * h_ref[rows, :] + gim[k] * h_ref[rows_im, :]
    noise = ns_ref[pl.ds(0, 16, stride=rows_out), :]
    for r in range(1, rows_out):
        noise = noise + ns_ref[pl.ds(r, 16, stride=rows_out), :]
    noise = noise * (-1.0 / (256.0 * F))
    for step in (64, 32, 16):
        noise = noise + pltpu.roll(noise, step, 1)
    lane_tile = lax.broadcasted_iota(jnp.int32, (TILE, LANES), 1) // TILE
    spot = lax.broadcasted_iota(jnp.int32, (TILE, LANES), 0) % 8
    noise = jnp.where(lane_tile == spot, noise, 0.0)
    upper = jnp.sum(noise[:8], axis=0, keepdims=True)
    lower = jnp.sum(noise[8:], axis=0, keepdims=True)

    prod = dot(slope_bf[32:288], taps, ((1,), (1,)))
    gw = jnp.zeros((32, 256), F32)
    for sy in range(1, 9):
        gw = gw + pltpu.roll(prod[(sy - 1) * 32 : sy * 32], 256 - 2 * sy, 1)
    picked = dot(jnp.concatenate(split(gw, 3), axis=0), pick_ref[...])
    out_ref[0:32, :] = picked[0:32] + (picked[32:64] + picked[64:96])
    bias = jnp.broadcast_to(jnp.sum(bias, axis=1, keepdims=True), (32, LANES))
    bias = jnp.sum(jnp.where(diag, bias, 0.0), axis=0, keepdims=True)
    row = lax.broadcasted_iota(jnp.int32, (8, LANES), 0)
    tail = jnp.where(row == 0, bias, jnp.where(row == 1, upper, jnp.where(row == 2, lower, 0.0)))
    out_ref[32:40, :] = tail


def last_sum(own_ref, got_ref, weight_ref, bias_ref, noise_ref):
    total = own_ref[...] + got_ref[...]
    weight_ref[...] = total[:32, :36]
    bias_ref[...] = total[32:33, :32]
    noise_ref[...] = total[33:35]


def involution(value, count, step, first):
    pairs = []
    for i in range(first, count):
        j = ((i - first) ^ step) + first
        if j < count:
            pairs.append((i, j))
    return lax.ppermute(value, "space", pairs)


def sum_space(value, count):
    bits = count.bit_length() - 1
    assert 1 << bits == count
    stages = []
    at = 0
    while at < bits:
        width = 2 if at == 1 and bits - at >= 3 else 1
        stages.append([m << at for m in range(1, 1 << width)])
        at += width
    for masks in stages[:-1]:
        got = []
        for m in masks:
            got.append(lax.ppermute(value, "space", [(i, i ^ m) for i in range(count)]))
        value = value + got[0]
        if len(got) == 3:
            value = value + (got[1] + got[2])
    (mask,) = stages[-1]
    got = lax.ppermute(value, "space", [(i, i ^ mask) for i in range(count)])
    return value, got


def call(body, args, smem, outs, scratch, far=()):
    vm = pl.BlockSpec(memory_space=pltpu.VMEM)
    sm = pl.BlockSpec(memory_space=pltpu.SMEM)
    sizes = [int(np.prod(a.shape)) * a.dtype.itemsize for a in list(args) + list(outs)]
    sizes += [int(np.prod(a.shape)) * 4 for a in scratch]
    hbm = pl.BlockSpec(memory_space=pltpu.HBM)
    specs = [sm if k < smem else hbm if k in far else vm for k in range(len(args))]
    args = [
        pltpu.with_memory_space_constraint(a, pltpu.HBM) if k in far else a
        for k, a in enumerate(args)
    ]
    return pl.pallas_call(
        body,
        out_shape=tuple(outs),
        in_specs=specs,
        out_specs=(vm,) * len(outs),
        scratch_shapes=scratch,
        compiler_params=pltpu.CompilerParams(vmem_limit_bytes=sum(sizes) + (12 << 20)),
    )(*args)


def shards(raw, shifts, weight, offset, log_var, goal):
    nf = lax.axis_size("frame")
    n_space = lax.axis_size("space")
    fl, band_rows, W = raw.shape
    T = shifts.shape[3]
    channels, _, ws = goal.shape
    G = W // LANES
    F = nf * fl
    nsc = ws // LANES
    inv_pixels = 1.0 / (band_rows * n_space * W // 4)
    rows_out = max(G, 8)

    def from_frame(value, j):
        return lax.ppermute(value, "frame", [(i, (i - j) % nf) for i in range(nf)])

    def pieces(value):
        return [value] + [from_frame(value, j) for j in range(1, nf)]

    raws = pieces(raw)
    goals = pieces(goal)
    shift_parts = pieces(shifts)
    y = jnp.pad(raw, ((0, F - fl), (0, 0), (0, 0)))
    y = lax.optimization_barrier(y)
    for j in range(1, nf):
        y = lax.dynamic_update_slice(y, raws[j], (j * fl, 0, 0))
    y, shifts, log_var = lax.optimization_barrier((y, shifts, log_var))
    shift_parts = [v + TILE for v in [shifts] + shift_parts[1:]]
    yf = involution(y, n_space, 1, 1)
    yc = involution(y, n_space, 1, 0)
    fwd, fwd_low, inv, inv_low, part, wide, wide_low = (jnp.asarray(t) for t in tables())
    place, place_t, pick = tap_tables()
    side = 4 * G + nf * nsc * channels
    shape = jax.ShapeDtypeStruct
    merged, pack, pc, pf, moments = call(
        functools.partial(merge_kernel, (nf, fl, G, T, nsc)),
        [*shift_parts, *shift_parts, *goals, y, yc, yf]
        + [fwd, fwd_low, inv, inv_low, jnp.exp(log_var).reshape(2, LANES)],
        nf,
        [
            shape((TILE, W // nf), F32),
            shape((G, TILE, LANES), F32),
            shape((side, LANES), BF16),
            shape((side, LANES), BF16),
            shape((32 * rows_out, LANES), F32),
        ],
        [
            pltpu.VMEM((F * G, 3 * TILE, LANES), F32),
            pltpu.VMEM((F * G, 8, LANES), jnp.int32),
            pltpu.VMEM((256, LANES), F32),
            pltpu.VMEM((256, LANES), F32),
            pltpu.VMEM((16 * rows_out, LANES), F32),
            pltpu.VMEM((G, TILE, LANES), F32),
            pltpu.VMEM((nf * nsc, 256, LANES), F32),
            *[pltpu.VMEM(t.shape, BF16) for t in (fwd, fwd_low, inv, inv_low)],
            pltpu.SemaphoreType.DMA((4,)),
        ],
        {3 * nf + 3, 3 * nf + 4, 3 * nf + 5, 3 * nf + 6},
    )
    pc, pf, weight = lax.optimization_barrier((pc, pf, weight))
    pf = involution(pf, n_space, 1, 1)
    pc = involution(pc, n_space, 1, 0)
    big = dot(weight, jnp.asarray(place.reshape(36, -1), BF16))
    big = big.reshape(channels, 10, 144).transpose(1, 0, 2).reshape(320, 144).astype(BF16)
    bigt = dot(jnp.asarray(place_t.reshape(-1, 36), BF16), weight.T)
    bigt = bigt.reshape(96, 320).astype(BF16)
    (partial,) = call(
        functools.partial(demosaic_kernel, (nf, fl, G, nsc, n_space, inv_pixels)),
        [pack, pc, pf, moments, *goals, part, wide, wide_low, jnp.asarray(pick), big, bigt]
        + [offset.reshape(1, channels)],
        0,
        [shape((40, LANES), F32)],
        [
            pltpu.VMEM((10, channels, W // 2), F32),
            pltpu.VMEM((256, LANES), F32),
            pltpu.VMEM((G, 24, LANES), F32),
            pltpu.VMEM((rows_out * TILE, LANES), F32),
            pltpu.VMEM((rows_out * TILE, LANES), F32),
            pltpu.VMEM((rows_out * TILE, LANES), F32),
            *[pltpu.VMEM(t.shape, BF16) for t in (wide, wide_low, pick)],
            pltpu.SemaphoreType.DMA((3,)),
        ],
        {5 + nf, 6 + nf, 7 + nf},
    )
    grad_weight, grad_bias, grad_noise = call(
        last_sum,
        sum_space(partial, n_space),
        0,
        [shape((channels, 36), F32), shape((1, channels), F32), shape((2, LANES), F32)],
        [],
    )
    return merged, grad_weight, grad_bias.reshape(channels), grad_noise.reshape(256)


def solution(mesh):
    placed = (
        P("frame", "space", None),
        P("frame", None, "space", None),
        P(),
        P(),
        P(),
        P(None, "space", "frame"),
    )

    return jax.shard_map(
        shards,
        mesh=mesh,
        in_specs=placed,
        out_specs=(P("space", "frame"), P(), P(), P()),
        check_vma=False,
    )
```

```python
import functools
import math

import jax
import jax.numpy as jnp
import ml_dtypes
import numpy as np
from jax import lax
from jax.experimental import pallas as pl
from jax.experimental.pallas import tpu as pltpu
from jax.sharding import PartitionSpec as P


TILE = 16
LANES = 128
F32 = jnp.float32
BF16 = jnp.bfloat16


def dot(a, b, dims=((1,), (0,))):
    return lax.dot_general(a, b, (dims, ((), ())), preferred_element_type=F32)


def split(value, parts):
    terms = []
    for _ in range(parts):
        term = value.astype(BF16)
        terms.append(term)
        value = value - term.astype(F32)
    return terms


def split_table(value, parts):
    terms = []
    for _ in range(parts):
        term = float(np.float32(value).astype(ml_dtypes.bfloat16))
        terms.append(term)
        value = value - term
    return terms


def wave(phase, parts):
    near = jnp.minimum(phase, 16 - phase)
    step = jnp.minimum(near, 8 - near)
    flip = near > 4
    steps = [split_table(math.cos(2.0 * math.pi * k / 16.0), parts) for k in range(4)]
    terms = []
    for p in range(parts):
        value = jnp.zeros(phase.shape, F32)
        for k in range(4):
            value = jnp.where(step == k, float(steps[k][p]), value)
        terms.append(jnp.where(flip, -value, value))
    return terms


def waves(phase, parts):
    phase = phase & 15
    return wave(phase, parts), wave((phase + 12) & 15, parts)


def tap_tables():
    place = np.zeros((36, 10, 144))
    back = np.zeros((96, 10, 36))
    for a in range(3):
        for b in range(3):
            for p in range(2):
                for q in range(2):
                    tap = (3 * a + b) * 4 + 2 * p + q
                    for sy in range(10):
                        r = 2 * (sy + a) + p
                        place[tap, sy, (q * 3 + b) * 24 + r] = 1.0
                        if 4 <= r < 20:
                            back[(q * 3 + b) * 16 + r - 4, sy, tap] = 1.0
    return place, back


def turn(re, im, k, n):
    if k == 0:
        return re, im
    if 4 * k == n:
        return im, -re
    if 8 * k == n:
        half = math.sqrt(0.5)
        return (re + im) * half, (im - re) * half
    if 8 * k == 3 * n:
        half = math.sqrt(0.5)
        return (im - re) * half, (re + im) * -half
    c, s = math.cos(2.0 * math.pi * k / n), math.sin(2.0 * math.pi * k / n)
    return re * c + im * s, im * c - re * s


def fft(re, im):
    n = len(re)
    if n == 1:
        return re, im
    er, ei = fft(re[0::2], im[0::2])
    our, oi = fft(re[1::2], im[1::2])
    half = n // 2
    xr, xi = [None] * n, [None] * n
    for k in range(half):
        tr, ti = turn(our[k], oi[k], k, n)
        xr[k], xi[k] = er[k] + tr, ei[k] + ti
        xr[k + half], xi[k + half] = er[k] - tr, ei[k] - ti
    return xr, xi


def tree(values):
    while len(values) > 1:
        half = len(values) // 2
        values = [a + b for a, b in zip(values[:half], values[half:])]
    return values[0]


def add_lists(a, b):
    return b if a is None else [x + y for x, y in zip(a, b)]


def merge_kernel(dims, *refs):
    nf, fl, G, T, nsc = dims
    F = nf * fl
    dy_refs, refs = refs[:nf], refs[nf:]
    dx_refs, refs = refs[:nf], refs[nf:]
    goal_refs, refs = refs[:nf], refs[nf:]
    y_ref, yc_ref, yf_ref, var_ref = refs[:4]
    merged_ref, pack_ref, pc_ref, pf_ref, h_ref = refs[4:9]
    x_ref, idx_ref, p_ref, q_ref, xs_ref, mm_ref, goal_ref = refs[9:16]
    fwd_ref, fwdl_ref, inv_ref, invl_ref = refs[16:20]
    s = lax.axis_index("space")
    fr = lax.axis_index("frame")
    odd = lax.rem(s, 2)

    slots = ((y_ref, 1), (yc_ref, 2 - 2 * odd), (yf_ref, 2 * odd))

    def fill(f, carry):
        for ref, slot in slots:
            rows = ref[f].astype(F32)
            for g in range(G):
                block = rows[:, g * LANES : (g + 1) * LANES]
                x_ref[f * G + g, pl.ds(pl.multiple_of(slot * TILE, TILE), TILE), :] = block
        return carry

    lax.fori_loop(0, F, fill, 0, unroll=min(F, 4))

    spot = lax.broadcasted_iota(jnp.int32, (8, LANES), 1)
    for j in range(nf):
        for l in range(fl):
            row = dx_refs[j][l, 1]
            if T < LANES:
                row = jnp.concatenate([row, jnp.zeros((1, LANES - T), jnp.int32)], axis=1)
            row = jnp.broadcast_to(row, (8, LANES))
            for g in range(G):
                moved = jnp.take_along_axis(row, 8 * g + spot // TILE, axis=1)
                idx_ref[(j * fl + l) * G + g] = (moved + (spot - TILE)) & (LANES - 1)

    lead = G * 4
    for j in range(nf):
        for c in range(nsc):
            cols = slice(c * LANES, (c + 1) * LANES)
            goal_ref[j * nsc + c] = goal_refs[j][:, :, cols].astype(F32).reshape(256, LANES)
    for k in range(nf * nsc):
        rows = slice(lead + k * 32, lead + k * 32 + 32)
        pc_ref[rows, :] = goal_ref[k, pl.ds(7 - 7 * odd, 32, stride=8), :].astype(BF16)
        pf_ref[rows, :] = goal_ref[k, pl.ds(7 * odd, 32, stride=8), :].astype(BF16)

    lane = lax.broadcasted_iota(jnp.int32, (TILE, LANES), 1)
    kind = (lane // TILE) % 4

    line = lax.broadcasted_iota(jnp.int32, (TILE, LANES), 0)
    cos, sin = waves(line * (lane & 15), 3)
    for k in range(8):
        at = slice(k * TILE, (k + 1) * TILE)
        mid = slice(128 + k * TILE, 128 + (k + 1) * TILE)
        here = (lane // TILE) == k
        c = [jnp.where(here, v, 0.0).astype(BF16) for v in cos]
        d = [jnp.where(here, v, 0.0).astype(BF16) for v in sin]
        fwd_ref[at, :] = jnp.concatenate([c[0], d[0]], axis=1)
        fwd_ref[mid, :] = jnp.concatenate([c[1], d[1]], axis=1)
        fwdl_ref[at, :] = jnp.concatenate([c[2], d[2]], axis=1)
        inv_ref[at, :] = jnp.concatenate([c[0], c[1]], axis=1)
        inv_ref[mid, :] = jnp.concatenate([-d[0], -d[1]], axis=1)
        invl_ref[at, :] = c[2]
        invl_ref[mid, :] = -d[2]
    per = 16 // G
    chunks = F * G // 16
    rows_out = max(G, 8)
    fold = TILE // rows_out
    zero = jnp.zeros((TILE, LANES), F32)

    def place(f):
        if nf == 2:
            return f
        return lax.rem(f // fl + nf - fr, nf) * fl + f % fl

    def row_shift(f, t):
        if isinstance(f, int):
            return dy_refs[f // fl][f % fl, 0, 0, t]
        j = lax.div(f, fl)
        l = lax.rem(f, fl)
        value = dy_refs[0][l, 0, 0, t]
        for k in range(1, nf):
            value = jnp.where(j == k, dy_refs[k][l, 0, 0, t], value)
        return value

    first = lax.rem(nf - fr, nf) * fl
    log_var = var_ref[...]
    variances = []
    for k in range(16):
        row = jnp.broadcast_to(log_var[k // 8 : k // 8 + 1], (8, LANES))
        row = jnp.take_along_axis(row, (k % 8) * TILE + spot % TILE, axis=1)
        variances.append(jnp.concatenate([row, row], axis=0))

    def chunk_step(c, carry):
        sums = carry[0] if carry is not None else None
        blocks = []
        for q in range(16):
            g = q % G
            f = place(c * per + q // G)

            def load(t, group):
                if group < 0 or group >= G:
                    return zero
                start = row_shift(f, 8 * g + t)
                return x_ref[f * G + group, pl.ds(start, TILE), :]

            idx = idx_ref[f * G + g]
            idx = jnp.concatenate([idx, idx], axis=0)
            mixes = (
                jnp.where(
                    lane < 40,
                    load(0, g),
                    jnp.where(lane < 104, load(4, g), load(0, g - 1)),
                ),
                jnp.where(lane < 56, load(1, g), load(5, g)),
                jnp.where(lane < 72, load(2, g), load(6, g)),
                jnp.where(
                    lane < 24,
                    load(7, g + 1),
                    jnp.where(lane < 88, load(3, g), load(7, g)),
                ),
            )
            moved = [jnp.take_along_axis(m, idx, axis=1) for m in mixes]
            blocks.append(
                jnp.where(
                    kind < 2,
                    jnp.where(kind == 0, moved[0], moved[1]),
                    jnp.where(kind == 2, moved[2], moved[3]),
                )
            )
        part = [tree(blocks[g::G]) for g in range(G)]
        sums = add_lists(sums, part)
        base = [x_ref[first * G + g, TILE : 2 * TILE, :] for g in range(G)]
        both = jnp.concatenate(blocks + base, axis=0).astype(BF16)
        pq = dot(jnp.concatenate([both, both], axis=1), fwd_ref[...]) + dot(both, fwdl_ref[...])
        for q in range(16):
            rows = slice(q * TILE, (q + 1) * TILE)
            ref_rows = slice(256 + (q % G) * TILE, 256 + (q % G + 1) * TILE)
            diff = pq[ref_rows] - pq[rows]
            p_ref[rows, :] = diff[:, :LANES]
            q_ref[rows, :] = -diff[:, LANES:]
        re, im = fft(
            [p_ref[pl.ds(n, 16, stride=16), :] for n in range(16)],
            [q_ref[pl.ds(n, 16, stride=16), :] for n in range(16)],
        )
        out = [[], [], [], []]
        for k in range(16):
            energy = re[k] * re[k] + im[k] * im[k]
            weight = energy / (energy + variances[k])
            wr = weight * re[k]
            wi = weight * im[k]
            rest = 1.0 - weight
            for store, val in zip(out, (wr, wi, wr * rest, wi * rest)):
                if fold == 2:
                    val = val[:8] + val[8:]
                store.append(val)
        flat = out[0] + out[1] + out[2] + out[3]
        return sums, add_lists(carry[1] if carry is not None else None, flat)

    carry = chunk_step(0, None)
    if chunks > 1:
        carry = lax.fori_loop(1, chunks, chunk_step, carry)
    sums, flat = carry
    for k in range(32):
        h_ref[k * rows_out : (k + 1) * rows_out, :] = flat[32 + k]

    vi, ur = fft(flat[16:32], flat[:16])
    uv = jnp.concatenate(
        [jnp.concatenate(ur, axis=0), jnp.concatenate(vi, axis=0)], axis=1
    )
    m = 16 * rows_out
    terms = split(uv, 3)
    wide = dot(jnp.concatenate(terms, axis=0), inv_ref[...])
    pix = wide[:m, :LANES] + (wide[m : 2 * m, :LANES] + wide[:m, LANES:])
    pix = pix + (wide[2 * m :, :LANES] + wide[m : 2 * m, LANES:] + dot(terms[0], invl_ref[...]))
    xs_ref[...] = pix
    for g in range(G):
        val = xs_ref[pl.ds(g, 16, stride=rows_out), :]
        for other in range(g + G, rows_out, G):
            val = val + xs_ref[pl.ds(other, 16, stride=rows_out), :]
        val = (sums[g] + val / 256.0) / F
        mm_ref[g] = val
        pack_ref[g] = val
    own = G // nf
    for k in range(own):
        merged_ref[:, k * LANES : (k + 1) * LANES] = mm_ref[fr * own + k]
    low = jnp.concatenate([mm_ref[g, 0:4, :] for g in range(G)], axis=0)
    high = jnp.concatenate([mm_ref[g, 12:16, :] for g in range(G)], axis=0)
    pc_ref[0:lead, :] = jnp.where(odd == 1, low, high).astype(BF16)
    pf_ref[0:lead, :] = jnp.where(odd == 1, high, low).astype(BF16)


def demosaic_kernel(dims, pack_ref, pc_ref, pf_ref, h_ref, *refs):
    nf, fl, G, nsc, n_space, inv_pixels = dims
    F = nf * fl
    W = G * LANES
    half = W // 2
    goal_refs = refs[:nf]
    big_ref, bigt_ref, offs_ref = refs[nf : nf + 3]
    out_ref, goal_ref, raw_ref, mm_ref, p_ref, q_ref, ns_ref = refs[nf + 3 : nf + 10]
    part_ref, wideh_ref, widel_ref = refs[nf + 10 :]
    s = lax.axis_index("space")
    fr = lax.axis_index("frame")
    odd = lax.rem(s, 2)
    rows_out = max(G, 8)

    lead = G * 4
    for j in range(nf):
        at = pl.multiple_of(lax.rem(fr + j, nf) * (nsc * LANES), LANES)
        for c in range(nsc):
            cols = slice(c * LANES, (c + 1) * LANES)
            raw_ref[...] = goal_refs[j][:, :, cols].astype(F32).reshape(256, LANES)
            to = pl.ds(pl.multiple_of(at + c * LANES, LANES), LANES)
            for r in range(8):
                goal_ref[r + 1, :, to] = raw_ref[pl.ds(r, 32, stride=8), :]
        for ref, row in ((pc_ref, 9 - 9 * odd), (pf_ref, 9 * odd)):
            for c in range(nsc):
                first = lead + (j * nsc + c) * 32
                val = ref[first : first + 32, :].astype(F32)
                goal_ref[row, :, pl.ds(pl.multiple_of(at + c * LANES, LANES), LANES)] = val

    line = lax.broadcasted_iota(jnp.int32, (256, 256), 0)
    column = lax.broadcasted_iota(jnp.int32, (256, 256), 1)
    source = 2 * (column & 127) + (column >> 7)
    part_ref[...] = jnp.where(line == source, 1.0, 0.0).astype(BF16)
    lane8 = lax.broadcasted_iota(jnp.int32, (8, LANES), 1)
    line8 = lax.broadcasted_iota(jnp.int32, (8, LANES), 0)
    empty = jnp.zeros((8, LANES), F32)
    for q in range(2):
        cos, sin = waves((2 * line8 + q) * (lane8 & 15), 2)
        for t in range(0, 16, 2):
            for ref, c, d in ((wideh_ref, cos[0], sin[0]), (widel_ref, cos[1], sin[1])):
                rows = []
                for u in (t, t + 1):
                    here = lane8 // TILE == u % 8
                    row = []
                    for v in (c, d):
                        v = jnp.where(here, v, 0.0)
                        row += [v, empty] if u < 8 else [empty, v]
                    rows.append(jnp.concatenate(row, axis=1))
                at = q * 128 + t * 8
                ref[at : at + 16, :] = jnp.concatenate(rows, axis=0).astype(BF16)

    near = pc_ref[0:lead, :].astype(F32)
    far = pf_ref[0:lead, :].astype(F32)
    low = jnp.where(odd == 1, near, far)
    high = jnp.where(odd == 1, far, near)
    for g in range(G):
        mm_ref[g, 0:4, :] = low[4 * g : 4 * g + 4]
        mm_ref[g, 4:20, :] = pack_ref[g]
        mm_ref[g, 20:24, :] = high[4 * g : 4 * g + 4]
    pairs = jnp.concatenate(
        [jnp.concatenate([mm_ref[2 * h], mm_ref[2 * h + 1]], axis=1) for h in range(G // 2)],
        axis=0,
    )
    parted = dot(pairs.astype(BF16), part_ref[...])
    site = lax.broadcasted_iota(jnp.int32, (24, half), 1)
    pieces = []
    for q in range(2):
        plane = jnp.concatenate(
            [parted[24 * h : 24 * h + 24, q * 128 : (q + 1) * 128] for h in range(G // 2)], axis=1
        )
        pieces.append(jnp.where(site == 0, 0.0, pltpu.roll(plane, 1, 1)))
        pieces.append(plane)
        pieces.append(jnp.where(site == half - 1, 0.0, pltpu.roll(plane, half - 1, 1)))
    pieces.append(jnp.zeros((112, half), F32))
    taps = jnp.concatenate(pieces, axis=0).astype(BF16)

    preact = dot(big_ref[...], taps[:144])
    diag = lax.broadcasted_iota(jnp.int32, (32, LANES), 0) == lax.broadcasted_iota(
        jnp.int32, (32, LANES), 1
    )
    offs = jnp.where(diag, jnp.broadcast_to(offs_ref[2:3, :], (32, LANES)), 0.0)
    offs = jnp.broadcast_to(jnp.sum(offs, axis=1, keepdims=True), (32, half))
    bias = jnp.zeros((32, half), F32)
    slopes = []
    for sy in range(10):
        v = preact[sy * 32 : sy * 32 + 32] + offs
        sig = jax.nn.sigmoid(v)
        slope = (v * sig - goal_ref[sy]) * inv_pixels * (sig * (1.0 + v * (1.0 - sig)))
        if sy == 0:
            slope = jnp.where(s == 0, 0.0, slope)
        elif sy == 9:
            slope = jnp.where(s == n_space - 1, 0.0, slope)
        else:
            bias = bias + slope
        slopes.append(slope)
    slope_bf = jnp.concatenate(slopes, axis=0).astype(BF16)

    gt = dot(bigt_ref[...], slope_bf)
    site16 = lax.broadcasted_iota(jnp.int32, (TILE, half), 1)
    planes = []
    for q in range(2):
        left, mid, right = (gt[(q * 3 + b) * 16 : (q * 3 + b) * 16 + 16] for b in range(3))
        planes.append(
            mid
            + jnp.where(site16 == half - 1, 0.0, pltpu.roll(left, half - 1, 1))
            + jnp.where(site16 == 0, 0.0, pltpu.roll(right, 1, 1))
        )
    grad = jnp.concatenate(
        [
            jnp.concatenate([p[:, h * 128 : (h + 1) * 128] for p in planes], axis=1)
            for h in range(G // 2)
        ],
        axis=0,
    )
    m = grad.shape[0]
    terms = split(grad, 2)
    pq = dot(jnp.concatenate(terms, axis=0), wideh_ref[...])
    pq = pq[:m] + (pq[m:] + dot(terms[0], widel_ref[...]))
    for r in range(rows_out):
        g = r % G
        rows = slice((g // 2) * TILE, (g // 2 + 1) * TILE)
        c0 = (g % 2) * LANES
        p_ref[r * TILE : (r + 1) * TILE, :] = pq[rows, c0 : c0 + LANES]
        q_ref[r * TILE : (r + 1) * TILE, :] = -pq[rows, 256 + c0 : 256 + c0 + LANES]
    gre, gim = fft(
        [p_ref[pl.ds(n, rows_out, stride=16), :] for n in range(16)],
        [q_ref[pl.ds(n, rows_out, stride=16), :] for n in range(16)],
    )
    for k in range(16):
        rows = slice(k * rows_out, (k + 1) * rows_out)
        rows_im = slice((16 + k) * rows_out, (17 + k) * rows_out)
        ns_ref[rows, :] = gre[k] * h_ref[rows, :] + gim[k] * h_ref[rows_im, :]
    noise = ns_ref[pl.ds(0, 16, stride=rows_out), :]
    for r in range(1, rows_out):
        noise = noise + ns_ref[pl.ds(r, 16, stride=rows_out), :]
    noise = noise * (-1.0 / (256.0 * F))
    for step in (64, 32, 16):
        noise = noise + pltpu.roll(noise, step, 1)
    lane_tile = lax.broadcasted_iota(jnp.int32, (TILE, LANES), 1) // TILE
    spot = lax.broadcasted_iota(jnp.int32, (TILE, LANES), 0) % 8
    noise = jnp.where(lane_tile == spot, noise, 0.0)
    upper = jnp.sum(noise[:8], axis=0, keepdims=True)
    lower = jnp.sum(noise[8:], axis=0, keepdims=True)

    prod = dot(slope_bf[32:288], taps, ((1,), (1,)))
    gw = jnp.zeros((32, 256), F32)
    for sy in range(1, 9):
        gw = gw + pltpu.roll(prod[(sy - 1) * 32 : sy * 32], 256 - 2 * sy, 1)
    tap = lax.broadcasted_iota(jnp.int32, (32, LANES), 1)
    pair = tap >> 2
    a = (pair * 11) >> 5
    source = ((tap & 1) * 3 + pair - 3 * a) * 24 + 2 * a + ((tap >> 1) & 1)
    source = jnp.where(tap < 36, source, 0)
    lower_part = jnp.take_along_axis(gw[:, :LANES], source & 127, axis=1)
    upper_part = jnp.take_along_axis(gw[:, LANES:], source & 127, axis=1)
    out_ref[0:32, :] = jnp.where(source < LANES, lower_part, upper_part)
    bias = jnp.broadcast_to(jnp.sum(bias, axis=1, keepdims=True), (32, LANES))
    bias = jnp.sum(jnp.where(diag, bias, 0.0), axis=0, keepdims=True)
    row = lax.broadcasted_iota(jnp.int32, (8, LANES), 0)
    tail = jnp.where(row == 0, bias, jnp.where(row == 1, upper, jnp.where(row == 2, lower, 0.0)))
    out_ref[32:40, :] = tail


def last_sum(own_ref, got_ref, weight_ref, bias_ref, noise_ref):
    total = own_ref[...] + got_ref[...]
    weight_ref[...] = total[:32, :36]
    bias_ref[...] = total[32:33, :32]
    noise_ref[...] = total[33:35]


def involution(value, count, step, first):
    pairs = []
    for i in range(first, count):
        j = ((i - first) ^ step) + first
        if j < count:
            pairs.append((i, j))
    return lax.ppermute(value, "space", pairs)


def sum_space(value, count):
    bits = count.bit_length() - 1
    assert 1 << bits == count
    stages = []
    at = 0
    while at < bits:
        width = 2 if at == 1 and bits - at >= 3 else 1
        stages.append([m << at for m in range(1, 1 << width)])
        at += width
    for masks in stages[:-1]:
        got = []
        for m in masks:
            got.append(lax.ppermute(value, "space", [(i, i ^ m) for i in range(count)]))
        value = value + got[0]
        if len(got) == 3:
            value = value + (got[1] + got[2])
    (mask,) = stages[-1]
    got = lax.ppermute(value, "space", [(i, i ^ mask) for i in range(count)])
    return value, got


def call(body, args, smem, outs, scratch):
    vm = pl.BlockSpec(memory_space=pltpu.VMEM)
    sm = pl.BlockSpec(memory_space=pltpu.SMEM)
    sizes = [int(np.prod(a.shape)) * a.dtype.itemsize for a in list(args) + list(outs)]
    sizes += [int(np.prod(a.shape)) * 4 for a in scratch]
    return pl.pallas_call(
        body,
        out_shape=tuple(outs),
        in_specs=[sm] * smem + [vm] * (len(args) - smem),
        out_specs=(vm,) * len(outs),
        scratch_shapes=scratch,
        compiler_params=pltpu.CompilerParams(vmem_limit_bytes=sum(sizes) + (12 << 20)),
    )(*args)


def shards(raw, shifts, weight, offset, log_var, goal):
    nf = lax.axis_size("frame")
    n_space = lax.axis_size("space")
    fl, band_rows, W = raw.shape
    T = shifts.shape[3]
    channels, _, ws = goal.shape
    G = W // LANES
    F = nf * fl
    nsc = ws // LANES
    inv_pixels = 1.0 / (band_rows * n_space * W // 4)
    rows_out = max(G, 8)

    def from_frame(value, j):
        return lax.ppermute(value, "frame", [(i, (i - j) % nf) for i in range(nf)])

    def pieces(value):
        return [value] + [from_frame(value, j) for j in range(1, nf)]

    raws = pieces(raw)
    goals = pieces(goal)
    shift_parts = pieces(shifts)
    y = jnp.pad(raw, ((0, F - fl), (0, 0), (0, 0)))
    y = lax.optimization_barrier(y)
    for j in range(1, nf):
        y = lax.dynamic_update_slice(y, raws[j], (j * fl, 0, 0))
    shift_parts = [v + TILE for v in shift_parts]
    small = jnp.concatenate(
        [jnp.exp(log_var), offset, jnp.zeros((6 * LANES - channels,), F32)]
    ).reshape(8, LANES)
    yf = involution(y, n_space, 1, 1)
    yc = involution(y, n_space, 1, 0)
    place, place_t = tap_tables()
    side = 4 * G + nf * nsc * channels
    shape = jax.ShapeDtypeStruct
    merged, pack, pc, pf, moments = call(
        functools.partial(merge_kernel, (nf, fl, G, T, nsc)),
        [*shift_parts, *shift_parts, *goals, y, yc, yf, small],
        nf,
        [
            shape((TILE, W // nf), F32),
            shape((G, TILE, LANES), F32),
            shape((side, LANES), BF16),
            shape((side, LANES), BF16),
            shape((32 * rows_out, LANES), F32),
        ],
        [
            pltpu.VMEM((F * G, 3 * TILE, LANES), F32),
            pltpu.VMEM((F * G, 8, LANES), jnp.int32),
            pltpu.VMEM((256, LANES), F32),
            pltpu.VMEM((256, LANES), F32),
            pltpu.VMEM((16 * rows_out, LANES), F32),
            pltpu.VMEM((G, TILE, LANES), F32),
            pltpu.VMEM((nf * nsc, 256, LANES), F32),
            pltpu.VMEM((256, 256), BF16),
            pltpu.VMEM((128, 256), BF16),
            pltpu.VMEM((256, 256), BF16),
            pltpu.VMEM((256, 128), BF16),
        ],
    )
    pc, pf, weight = lax.optimization_barrier((pc, pf, weight))
    pf = involution(pf, n_space, 1, 1)
    pc = involution(pc, n_space, 1, 0)
    big = dot(weight, jnp.asarray(place.reshape(36, -1), BF16))
    big = big.reshape(channels, 10, 144).transpose(1, 0, 2).reshape(320, 144).astype(BF16)
    bigt = dot(jnp.asarray(place_t.reshape(-1, 36), BF16), weight.T)
    bigt = bigt.reshape(96, 320).astype(BF16)
    (partial,) = call(
        functools.partial(demosaic_kernel, (nf, fl, G, nsc, n_space, inv_pixels)),
        [pack, pc, pf, moments, *goals, big, bigt, small],
        0,
        [shape((40, LANES), F32)],
        [
            pltpu.VMEM((10, channels, W // 2), F32),
            pltpu.VMEM((256, LANES), F32),
            pltpu.VMEM((G, 24, LANES), F32),
            pltpu.VMEM((rows_out * TILE, LANES), F32),
            pltpu.VMEM((rows_out * TILE, LANES), F32),
            pltpu.VMEM((rows_out * TILE, LANES), F32),
            pltpu.VMEM((256, 256), BF16),
            pltpu.VMEM((256, 512), BF16),
            pltpu.VMEM((256, 512), BF16),
        ],
    )
    grad_weight, grad_bias, grad_noise = call(
        last_sum,
        sum_space(partial, n_space),
        0,
        [shape((channels, 36), F32), shape((1, channels), F32), shape((2, LANES), F32)],
        [],
    )
    return merged, grad_weight, grad_bias.reshape(channels), grad_noise.reshape(256)


def solution(mesh):
    placed = (
        P("frame", "space", None),
        P("frame", None, "space", None),
        P(),
        P(),
        P(),
        P(None, "space", "frame"),
    )

    return jax.shard_map(
        shards,
        mesh=mesh,
        in_specs=placed,
        out_specs=(P("space", "frame"), P(), P(), P()),
        check_vma=False,
    )
```

```python
import functools
import math

import jax
import jax.numpy as jnp
import ml_dtypes
import numpy as np
from jax import lax
from jax.experimental import pallas as pl
from jax.experimental.pallas import tpu as pltpu
from jax.sharding import PartitionSpec as P


TILE = 16
LANES = 128
F32 = jnp.float32
BF16 = jnp.bfloat16


def dot(a, b, dims=((1,), (0,))):
    return lax.dot_general(a, b, (dims, ((), ())), preferred_element_type=F32)


def split(value, parts):
    terms = []
    for _ in range(parts):
        term = value.astype(BF16)
        terms.append(term)
        value = value - term.astype(F32)
    return terms


def split_table(value, parts):
    terms = []
    for _ in range(parts):
        term = float(np.float32(value).astype(ml_dtypes.bfloat16))
        terms.append(term)
        value = value - term
    return terms


def wave(phase, parts):
    near = jnp.minimum(phase, 16 - phase)
    step = jnp.minimum(near, 8 - near)
    flip = near > 4
    steps = [split_table(math.cos(2.0 * math.pi * k / 16.0), parts) for k in range(4)]
    terms = []
    for p in range(parts):
        value = jnp.zeros(phase.shape, F32)
        for k in range(4):
            value = jnp.where(step == k, float(steps[k][p]), value)
        terms.append(jnp.where(flip, -value, value))
    return terms


def waves(phase, parts):
    phase = phase & 15
    return wave(phase, parts), wave((phase + 12) & 15, parts)


def tap_tables():
    place = np.zeros((36, 10, 144))
    back = np.zeros((96, 10, 36))
    for a in range(3):
        for b in range(3):
            for p in range(2):
                for q in range(2):
                    tap = (3 * a + b) * 4 + 2 * p + q
                    for sy in range(10):
                        r = 2 * (sy + a) + p
                        place[tap, sy, (q * 3 + b) * 24 + r] = 1.0
                        if 4 <= r < 20:
                            back[(q * 3 + b) * 16 + r - 4, sy, tap] = 1.0
    return place, back


def turn(re, im, k, n):
    if k == 0:
        return re, im
    if 4 * k == n:
        return im, -re
    if 8 * k == n:
        half = math.sqrt(0.5)
        return (re + im) * half, (im - re) * half
    if 8 * k == 3 * n:
        half = math.sqrt(0.5)
        return (im - re) * half, (re + im) * -half
    c, s = math.cos(2.0 * math.pi * k / n), math.sin(2.0 * math.pi * k / n)
    return re * c + im * s, im * c - re * s


def fft(re, im):
    n = len(re)
    if n == 1:
        return re, im
    er, ei = fft(re[0::2], im[0::2])
    our, oi = fft(re[1::2], im[1::2])
    half = n // 2
    xr, xi = [None] * n, [None] * n
    for k in range(half):
        tr, ti = turn(our[k], oi[k], k, n)
        xr[k], xi[k] = er[k] + tr, ei[k] + ti
        xr[k + half], xi[k + half] = er[k] - tr, ei[k] - ti
    return xr, xi


def tree(values):
    while len(values) > 1:
        half = len(values) // 2
        values = [a + b for a, b in zip(values[:half], values[half:])]
    return values[0]


def add_lists(a, b):
    return b if a is None else [x + y for x, y in zip(a, b)]


def merge_kernel(dims, *refs):
    nf, fl, G, T, nsc = dims
    F = nf * fl
    dx_refs, refs = refs[:nf], refs[nf:]
    goal_refs, refs = refs[:nf], refs[nf:]
    y_ref, yc_ref, yf_ref, var_ref = refs[:4]
    pack_ref, pc_ref, pf_ref, h_ref = refs[4:8]
    x_ref, idx_ref, p_ref, q_ref, xs_ref, goal_ref = refs[8:14]
    fwd_ref, fwdl_ref, inv_ref, invl_ref = refs[14:18]
    dy_refs, sems = refs[18 : 18 + nf], refs[18 + nf]
    moves = [
        pltpu.make_async_copy(src, dst, sems.at[j])
        for j, (src, dst) in enumerate(zip(dx_refs, dy_refs))
    ]
    for move in moves:
        move.start()
    s = lax.axis_index("space")
    fr = lax.axis_index("frame")
    odd = lax.rem(s, 2)

    slots = ((y_ref, 1), (yc_ref, 2 - 2 * odd), (yf_ref, 2 * odd))

    def fill(f, carry):
        for ref, slot in slots:
            rows = ref[f].astype(F32)
            for g in range(G):
                block = rows[:, g * LANES : (g + 1) * LANES]
                x_ref[f * G + g, pl.ds(pl.multiple_of(slot * TILE, TILE), TILE), :] = block
        return carry

    lax.fori_loop(0, F, fill, 0, unroll=min(F, 4))

    spot = lax.broadcasted_iota(jnp.int32, (8, LANES), 1)
    for j in range(nf):
        for l in range(fl):
            row = dx_refs[j][l, 1]
            if T < LANES:
                row = jnp.concatenate([row, jnp.zeros((1, LANES - T), jnp.int32)], axis=1)
            row = jnp.broadcast_to(row, (8, LANES))
            for g in range(G):
                moved = jnp.take_along_axis(row, 8 * g + spot // TILE, axis=1)
                idx_ref[(j * fl + l) * G + g] = (moved + (spot - TILE)) & (LANES - 1)

    lead = G * 4
    for j in range(nf):
        for c in range(nsc):
            cols = slice(c * LANES, (c + 1) * LANES)
            goal_ref[j * nsc + c] = goal_refs[j][:, :, cols].astype(F32).reshape(256, LANES)
    for k in range(nf * nsc):
        rows = slice(lead + k * 32, lead + k * 32 + 32)
        pc_ref[rows, :] = goal_ref[k, pl.ds(7 - 7 * odd, 32, stride=8), :].astype(BF16)
        pf_ref[rows, :] = goal_ref[k, pl.ds(7 * odd, 32, stride=8), :].astype(BF16)

    lane = lax.broadcasted_iota(jnp.int32, (TILE, LANES), 1)
    kind = (lane // TILE) % 4

    line = lax.broadcasted_iota(jnp.int32, (TILE, LANES), 0)
    cos, sin = waves(line * (lane & 15), 3)
    for k in range(8):
        at = slice(k * TILE, (k + 1) * TILE)
        mid = slice(128 + k * TILE, 128 + (k + 1) * TILE)
        here = (lane // TILE) == k
        c = [jnp.where(here, v, 0.0).astype(BF16) for v in cos]
        d = [jnp.where(here, v, 0.0).astype(BF16) for v in sin]
        fwd_ref[at, :] = jnp.concatenate([c[0], d[0]], axis=1)
        fwd_ref[mid, :] = jnp.concatenate([c[1], d[1]], axis=1)
        fwdl_ref[at, :] = jnp.concatenate([c[2], d[2]], axis=1)
        inv_ref[at, :] = jnp.concatenate([c[0], c[1]], axis=1)
        inv_ref[mid, :] = jnp.concatenate([-d[0], -d[1]], axis=1)
        invl_ref[at, :] = c[2]
        invl_ref[mid, :] = -d[2]
    per = 16 // G
    chunks = F * G // 16
    rows_out = max(G, 8)
    fold = TILE // rows_out
    zero = jnp.zeros((TILE, LANES), F32)

    def place(f):
        if nf == 2:
            return f
        return lax.rem(f // fl + nf - fr, nf) * fl + f % fl

    def row_shift(f, t):
        if isinstance(f, int):
            return dy_refs[f // fl][f % fl, 0, 0, t]
        j = lax.div(f, fl)
        l = lax.rem(f, fl)
        value = dy_refs[0][l, 0, 0, t]
        for k in range(1, nf):
            value = jnp.where(j == k, dy_refs[k][l, 0, 0, t], value)
        return value

    first = lax.rem(nf - fr, nf) * fl
    log_var = var_ref[...]
    variances = []
    for k in range(16):
        row = jnp.broadcast_to(log_var[k // 8 : k // 8 + 1], (8, LANES))
        row = jnp.take_along_axis(row, (k % 8) * TILE + spot % TILE, axis=1)
        variances.append(jnp.concatenate([row, row], axis=0))

    def chunk_step(c, carry):
        sums = carry[0] if carry is not None else None
        blocks = []
        for q in range(16):
            g = q % G
            f = place(c * per + q // G)

            def load(t, group):
                if group < 0 or group >= G:
                    return zero
                start = row_shift(f, 8 * g + t)
                return x_ref[f * G + group, pl.ds(start, TILE), :]

            idx = idx_ref[f * G + g]
            idx = jnp.concatenate([idx, idx], axis=0)
            mixes = (
                jnp.where(
                    lane < 40,
                    load(0, g),
                    jnp.where(lane < 104, load(4, g), load(0, g - 1)),
                ),
                jnp.where(lane < 56, load(1, g), load(5, g)),
                jnp.where(lane < 72, load(2, g), load(6, g)),
                jnp.where(
                    lane < 24,
                    load(7, g + 1),
                    jnp.where(lane < 88, load(3, g), load(7, g)),
                ),
            )
            moved = [jnp.take_along_axis(m, idx, axis=1) for m in mixes]
            blocks.append(
                jnp.where(
                    kind < 2,
                    jnp.where(kind == 0, moved[0], moved[1]),
                    jnp.where(kind == 2, moved[2], moved[3]),
                )
            )
        part = [tree(blocks[g::G]) for g in range(G)]
        sums = add_lists(sums, part)
        base = [x_ref[first * G + g, TILE : 2 * TILE, :] for g in range(G)]
        both = jnp.concatenate(blocks + base, axis=0).astype(BF16)
        pq = dot(jnp.concatenate([both, both], axis=1), fwd_ref[...]) + dot(both, fwdl_ref[...])
        for q in range(16):
            rows = slice(q * TILE, (q + 1) * TILE)
            ref_rows = slice(256 + (q % G) * TILE, 256 + (q % G + 1) * TILE)
            diff = pq[ref_rows] - pq[rows]
            p_ref[rows, :] = diff[:, :LANES]
            q_ref[rows, :] = -diff[:, LANES:]
        re, im = fft(
            [p_ref[pl.ds(n, 16, stride=16), :] for n in range(16)],
            [q_ref[pl.ds(n, 16, stride=16), :] for n in range(16)],
        )
        out = [[], [], [], []]
        for k in range(16):
            energy = re[k] * re[k] + im[k] * im[k]
            weight = energy / (energy + variances[k])
            wr = weight * re[k]
            wi = weight * im[k]
            rest = 1.0 - weight
            for store, val in zip(out, (wr, wi, wr * rest, wi * rest)):
                if fold == 2:
                    val = val[:8] + val[8:]
                store.append(val)
        flat = out[0] + out[1] + out[2] + out[3]
        return sums, add_lists(carry[1] if carry is not None else None, flat)

    for move in moves:
        move.wait()
    carry = chunk_step(0, None)
    if chunks > 1:
        carry = lax.fori_loop(1, chunks, chunk_step, carry)
    sums, flat = carry
    for k in range(32):
        h_ref[k * rows_out : (k + 1) * rows_out, :] = flat[32 + k]

    vi, ur = fft(flat[16:32], flat[:16])
    uv = jnp.concatenate(
        [jnp.concatenate(ur, axis=0), jnp.concatenate(vi, axis=0)], axis=1
    )
    m = 16 * rows_out
    terms = split(uv, 3)
    wide = dot(jnp.concatenate(terms, axis=0), inv_ref[...])
    pix = wide[:m, :LANES] + (wide[m : 2 * m, :LANES] + wide[:m, LANES:])
    pix = pix + (wide[2 * m :, :LANES] + wide[m : 2 * m, LANES:] + dot(terms[0], invl_ref[...]))
    xs_ref[...] = pix
    for g in range(G):
        val = xs_ref[pl.ds(g, 16, stride=rows_out), :]
        for other in range(g + G, rows_out, G):
            val = val + xs_ref[pl.ds(other, 16, stride=rows_out), :]
        val = (sums[g] + val / 256.0) / F
        pack_ref[g] = val
    low = jnp.concatenate([pack_ref[g, 0:4, :] for g in range(G)], axis=0)
    high = jnp.concatenate([pack_ref[g, 12:16, :] for g in range(G)], axis=0)
    pc_ref[0:lead, :] = jnp.where(odd == 1, low, high).astype(BF16)
    pf_ref[0:lead, :] = jnp.where(odd == 1, high, low).astype(BF16)


def demosaic_kernel(dims, pack_ref, pc_ref, pf_ref, h_ref, *refs):
    nf, fl, G, nsc, n_space, inv_pixels = dims
    F = nf * fl
    W = G * LANES
    half = W // 2
    goal_refs = refs[:nf]
    big_ref, bigt_ref, offs_ref = refs[nf : nf + 3]
    out_ref, goal_ref, raw_ref, mm_ref, p_ref, q_ref, ns_ref = refs[nf + 3 : nf + 10]
    part_ref, wideh_ref, widel_ref = refs[nf + 10 :]
    s = lax.axis_index("space")
    fr = lax.axis_index("frame")
    odd = lax.rem(s, 2)
    rows_out = max(G, 8)

    lead = G * 4
    for j in range(nf):
        at = pl.multiple_of(lax.rem(fr + j, nf) * (nsc * LANES), LANES)
        for c in range(nsc):
            cols = slice(c * LANES, (c + 1) * LANES)
            raw_ref[...] = goal_refs[j][:, :, cols].astype(F32).reshape(256, LANES)
            to = pl.ds(pl.multiple_of(at + c * LANES, LANES), LANES)
            for r in range(8):
                goal_ref[r + 1, :, to] = raw_ref[pl.ds(r, 32, stride=8), :]
        for ref, row in ((pc_ref, 9 - 9 * odd), (pf_ref, 9 * odd)):
            for c in range(nsc):
                first = lead + (j * nsc + c) * 32
                val = ref[first : first + 32, :].astype(F32)
                goal_ref[row, :, pl.ds(pl.multiple_of(at + c * LANES, LANES), LANES)] = val

    line = lax.broadcasted_iota(jnp.int32, (256, 256), 0)
    column = lax.broadcasted_iota(jnp.int32, (256, 256), 1)
    source = 2 * (column & 127) + (column >> 7)
    part_ref[...] = jnp.where(line == source, 1.0, 0.0).astype(BF16)
    lane8 = lax.broadcasted_iota(jnp.int32, (8, LANES), 1)
    line8 = lax.broadcasted_iota(jnp.int32, (8, LANES), 0)
    empty = jnp.zeros((8, LANES), F32)
    for q in range(2):
        cos, sin = waves((2 * line8 + q) * (lane8 & 15), 2)
        for t in range(0, 16, 2):
            for ref, c, d in ((wideh_ref, cos[0], sin[0]), (widel_ref, cos[1], sin[1])):
                rows = []
                for u in (t, t + 1):
                    here = lane8 // TILE == u % 8
                    row = []
                    for v in (c, d):
                        v = jnp.where(here, v, 0.0)
                        row += [v, empty] if u < 8 else [empty, v]
                    rows.append(jnp.concatenate(row, axis=1))
                at = q * 128 + t * 8
                ref[at : at + 16, :] = jnp.concatenate(rows, axis=0).astype(BF16)

    near = pc_ref[0:lead, :].astype(F32)
    far = pf_ref[0:lead, :].astype(F32)
    low = jnp.where(odd == 1, near, far)
    high = jnp.where(odd == 1, far, near)
    for g in range(G):
        mm_ref[g, 0:4, :] = low[4 * g : 4 * g + 4]
        mm_ref[g, 4:20, :] = pack_ref[g]
        mm_ref[g, 20:24, :] = high[4 * g : 4 * g + 4]
    pairs = jnp.concatenate(
        [jnp.concatenate([mm_ref[2 * h], mm_ref[2 * h + 1]], axis=1) for h in range(G // 2)],
        axis=0,
    )
    parted = dot(pairs.astype(BF16), part_ref[...])
    site = lax.broadcasted_iota(jnp.int32, (24, half), 1)
    pieces = []
    for q in range(2):
        plane = jnp.concatenate(
            [parted[24 * h : 24 * h + 24, q * 128 : (q + 1) * 128] for h in range(G // 2)], axis=1
        )
        pieces.append(jnp.where(site == 0, 0.0, pltpu.roll(plane, 1, 1)))
        pieces.append(plane)
        pieces.append(jnp.where(site == half - 1, 0.0, pltpu.roll(plane, half - 1, 1)))
    pieces.append(jnp.zeros((112, half), F32))
    taps = jnp.concatenate(pieces, axis=0).astype(BF16)

    preact = dot(big_ref[...], taps[:144])
    diag = lax.broadcasted_iota(jnp.int32, (32, LANES), 0) == lax.broadcasted_iota(
        jnp.int32, (32, LANES), 1
    )
    offs = jnp.where(diag, jnp.broadcast_to(offs_ref[2:3, :], (32, LANES)), 0.0)
    offs = jnp.broadcast_to(jnp.sum(offs, axis=1, keepdims=True), (32, half))
    bias = jnp.zeros((32, half), F32)
    slopes = []
    for sy in range(10):
        v = preact[sy * 32 : sy * 32 + 32] + offs
        sig = jax.nn.sigmoid(v)
        slope = (v * sig - goal_ref[sy]) * inv_pixels * (sig * (1.0 + v * (1.0 - sig)))
        if sy == 0:
            slope = jnp.where(s == 0, 0.0, slope)
        elif sy == 9:
            slope = jnp.where(s == n_space - 1, 0.0, slope)
        else:
            bias = bias + slope
        slopes.append(slope)
    slope_bf = jnp.concatenate(slopes, axis=0).astype(BF16)

    gt = dot(bigt_ref[...], slope_bf)
    site16 = lax.broadcasted_iota(jnp.int32, (TILE, half), 1)
    planes = []
    for q in range(2):
        left, mid, right = (gt[(q * 3 + b) * 16 : (q * 3 + b) * 16 + 16] for b in range(3))
        planes.append(
            mid
            + jnp.where(site16 == half - 1, 0.0, pltpu.roll(left, half - 1, 1))
            + jnp.where(site16 == 0, 0.0, pltpu.roll(right, 1, 1))
        )
    grad = jnp.concatenate(
        [
            jnp.concatenate([p[:, h * 128 : (h + 1) * 128] for p in planes], axis=1)
            for h in range(G // 2)
        ],
        axis=0,
    )
    m = grad.shape[0]
    terms = split(grad, 2)
    pq = dot(jnp.concatenate(terms, axis=0), wideh_ref[...])
    pq = pq[:m] + (pq[m:] + dot(terms[0], widel_ref[...]))
    for r in range(rows_out):
        g = r % G
        rows = slice((g // 2) * TILE, (g // 2 + 1) * TILE)
        c0 = (g % 2) * LANES
        p_ref[r * TILE : (r + 1) * TILE, :] = pq[rows, c0 : c0 + LANES]
        q_ref[r * TILE : (r + 1) * TILE, :] = -pq[rows, 256 + c0 : 256 + c0 + LANES]
    gre, gim = fft(
        [p_ref[pl.ds(n, rows_out, stride=16), :] for n in range(16)],
        [q_ref[pl.ds(n, rows_out, stride=16), :] for n in range(16)],
    )
    for k in range(16):
        rows = slice(k * rows_out, (k + 1) * rows_out)
        rows_im = slice((16 + k) * rows_out, (17 + k) * rows_out)
        ns_ref[rows, :] = gre[k] * h_ref[rows, :] + gim[k] * h_ref[rows_im, :]
    noise = ns_ref[pl.ds(0, 16, stride=rows_out), :]
    for r in range(1, rows_out):
        noise = noise + ns_ref[pl.ds(r, 16, stride=rows_out), :]
    noise = noise * (-1.0 / (256.0 * F))
    for step in (64, 32, 16):
        noise = noise + pltpu.roll(noise, step, 1)

    prod = dot(slope_bf[32:288], taps, ((1,), (1,)))
    gw = jnp.zeros((32, 256), F32)
    for sy in range(1, 9):
        gw = gw + pltpu.roll(prod[(sy - 1) * 32 : sy * 32], 256 - 2 * sy, 1)
    tap = lax.broadcasted_iota(jnp.int32, (32, LANES), 1)
    pair = tap >> 2
    a = (pair * 11) >> 5
    source = ((tap & 1) * 3 + pair - 3 * a) * 24 + 2 * a + ((tap >> 1) & 1)
    source = jnp.where(tap < 36, source, 0)
    lower_part = jnp.take_along_axis(gw[:, :LANES], source & 127, axis=1)
    upper_part = jnp.take_along_axis(gw[:, LANES:], source & 127, axis=1)
    gw = jnp.where(source < LANES, lower_part, upper_part)
    gw = jnp.where(tap == 36, jnp.sum(bias, axis=1, keepdims=True), gw)
    gw = jnp.where(tap < 37, gw, 0.0)
    first = gw[0:8] + (pltpu.roll(gw[8:16], 37, 1) + pltpu.roll(gw[16:24], 74, 1))
    group = lane8 // TILE
    second = jnp.where(group == 5, noise[:8], jnp.where(group == 6, noise[8:], gw[24:32]))
    out_ref[...] = jnp.concatenate([first, second], axis=0)


def last_sum(nf, pack_ref, own_ref, got_ref, merged_ref, weight_ref, bias_ref, noise_ref):
    own = pack_ref.shape[0] // nf
    fr = lax.axis_index("frame")
    for k in range(own):
        merged_ref[:, k * LANES : (k + 1) * LANES] = pack_ref[fr * own + k]
    total = own_ref[...] + got_ref[...]
    first, second = total[:8], total[8:]
    gw = jnp.concatenate(
        [first, pltpu.roll(first, LANES - 37, 1), pltpu.roll(first, LANES - 74, 1), second], axis=0
    )
    weight_ref[...] = gw[:, :36]
    line = lax.broadcasted_iota(jnp.int32, (32, LANES), 0)
    lane = lax.broadcasted_iota(jnp.int32, (32, LANES), 1)
    bias = jnp.where(line == lane, jnp.broadcast_to(gw[:, 36:37], (32, LANES)), 0.0)
    bias_ref[...] = jnp.sum(bias, axis=0, keepdims=True)[:, :32]
    group = lane[:8] // TILE
    for k in range(2):
        part = jnp.where(group == 5 + k, second, 0.0)
        for step in (16, 32, 64):
            part = part + pltpu.roll(part, step, 1)
        part = jnp.where(group == line[:8], part, 0.0)
        noise_ref[k : k + 1, :] = jnp.sum(part, axis=0, keepdims=True)


def involution(value, count, step, first):
    pairs = []
    for i in range(first, count):
        j = ((i - first) ^ step) + first
        if j < count:
            pairs.append((i, j))
    return lax.ppermute(value, "space", pairs)


def sum_space(value, count):
    bits = count.bit_length() - 1
    assert 1 << bits == count
    stages = []
    at = 0
    while at < bits:
        width = 2 if at == 1 and bits - at >= 3 else 1
        stages.append([m << at for m in range(1, 1 << width)])
        at += width
    for masks in stages[:-1]:
        got = []
        for m in masks:
            got.append(lax.ppermute(value, "space", [(i, i ^ m) for i in range(count)]))
        value = value + got[0]
        if len(got) == 3:
            value = value + (got[1] + got[2])
    (mask,) = stages[-1]
    got = lax.ppermute(value, "space", [(i, i ^ mask) for i in range(count)])
    return value, got


def call(body, args, outs, scratch):
    vm = pl.BlockSpec(memory_space=pltpu.VMEM)
    sizes = [int(np.prod(a.shape)) * a.dtype.itemsize for a in list(args) + list(outs)]
    sizes += [int(np.prod(a.shape)) * 4 for a in scratch if a.memory_space == pltpu.VMEM]
    return pl.pallas_call(
        body,
        out_shape=tuple(outs),
        in_specs=[vm] * len(args),
        out_specs=(vm,) * len(outs),
        scratch_shapes=scratch,
        compiler_params=pltpu.CompilerParams(vmem_limit_bytes=sum(sizes) + (12 << 20)),
    )(*args)


def shards(raw, shifts, weight, offset, log_var, goal):
    nf = lax.axis_size("frame")
    n_space = lax.axis_size("space")
    fl, band_rows, W = raw.shape
    T = shifts.shape[3]
    channels, _, ws = goal.shape
    G = W // LANES
    F = nf * fl
    nsc = ws // LANES
    inv_pixels = 1.0 / (band_rows * n_space * W // 4)
    rows_out = max(G, 8)

    def from_frame(value, j):
        return lax.ppermute(value, "frame", [(i, (i - j) % nf) for i in range(nf)])

    def pieces(value):
        return [value] + [from_frame(value, j) for j in range(1, nf)]

    raws = pieces(raw)
    goals = pieces(goal)
    shift_parts = pieces(shifts)
    y = jnp.pad(raw, ((0, F - fl), (0, 0), (0, 0)))
    y = lax.optimization_barrier(y)
    for j in range(1, nf):
        y = lax.dynamic_update_slice(y, raws[j], (j * fl, 0, 0))
    shift_parts = [v + TILE for v in shift_parts]
    small = jnp.concatenate(
        [jnp.exp(log_var), offset, jnp.zeros((6 * LANES - channels,), F32)]
    ).reshape(8, LANES)
    yf = involution(y, n_space, 1, 1)
    yc = involution(y, n_space, 1, 0)
    place, place_t = tap_tables()
    big = dot(weight, jnp.asarray(place.reshape(36, -1), BF16))
    big = big.reshape(channels, 10, 144).transpose(1, 0, 2).reshape(320, 144).astype(BF16)
    bigt = dot(jnp.asarray(place_t.reshape(-1, 36), BF16), weight.T)
    bigt = bigt.reshape(96, 320).astype(BF16)
    side = 4 * G + nf * nsc * channels
    shape = jax.ShapeDtypeStruct
    pack, pc, pf, moments = call(
        functools.partial(merge_kernel, (nf, fl, G, T, nsc)),
        [*shift_parts, *goals, y, yc, yf, small],
        [
            shape((G, TILE, LANES), F32),
            shape((side, LANES), BF16),
            shape((side, LANES), BF16),
            shape((32 * rows_out, LANES), F32),
        ],
        [
            pltpu.VMEM((F * G, 3 * TILE, LANES), F32),
            pltpu.VMEM((F * G, 8, LANES), jnp.int32),
            pltpu.VMEM((256, LANES), F32),
            pltpu.VMEM((256, LANES), F32),
            pltpu.VMEM((16 * rows_out, LANES), F32),
            pltpu.VMEM((nf * nsc, 256, LANES), F32),
            pltpu.VMEM((256, 256), BF16),
            pltpu.VMEM((128, 256), BF16),
            pltpu.VMEM((256, 256), BF16),
            pltpu.VMEM((256, 128), BF16),
            *[pltpu.SMEM(shifts.shape, jnp.int32)] * nf,
            pltpu.SemaphoreType.DMA((nf,)),
        ],
    )
    pf = involution(pf, n_space, 1, 1)
    pc = involution(pc, n_space, 1, 0)
    (partial,) = call(
        functools.partial(demosaic_kernel, (nf, fl, G, nsc, n_space, inv_pixels)),
        [pack, pc, pf, moments, *goals, big, bigt, small],
        [shape((16, LANES), F32)],
        [
            pltpu.VMEM((10, channels, W // 2), F32),
            pltpu.VMEM((256, LANES), F32),
            pltpu.VMEM((G, 24, LANES), F32),
            pltpu.VMEM((rows_out * TILE, LANES), F32),
            pltpu.VMEM((rows_out * TILE, LANES), F32),
            pltpu.VMEM((rows_out * TILE, LANES), F32),
            pltpu.VMEM((256, 256), BF16),
            pltpu.VMEM((256, 512), BF16),
            pltpu.VMEM((256, 512), BF16),
        ],
    )
    merged, grad_weight, grad_bias, grad_noise = call(
        functools.partial(last_sum, nf),
        [pack, *sum_space(partial, n_space)],
        [
            shape((TILE, W // nf), F32),
            shape((channels, 36), F32),
            shape((1, channels), F32),
            shape((2, LANES), F32),
        ],
        [],
    )
    return merged, grad_weight, grad_bias.reshape(channels), grad_noise.reshape(256)


def solution(mesh):
    placed = (
        P("frame", "space", None),
        P("frame", None, "space", None),
        P(),
        P(),
        P(),
        P(None, "space", "frame"),
    )

    return jax.shard_map(
        shards,
        mesh=mesh,
        in_specs=placed,
        out_specs=(P("space", "frame"), P(), P(), P()),
        check_vma=False,
    )
```

```python
import functools
import math

import jax
import jax.numpy as jnp
import ml_dtypes
import numpy as np
from jax import lax
from jax.experimental import pallas as pl
from jax.experimental.pallas import tpu as pltpu
from jax.sharding import PartitionSpec as P


TILE = 16
LANES = 128
F32 = jnp.float32
BF16 = jnp.bfloat16


def dot(a, b, dims=((1,), (0,))):
    return lax.dot_general(a, b, (dims, ((), ())), preferred_element_type=F32)


def split(value, parts):
    terms = []
    for _ in range(parts):
        term = value.astype(BF16)
        terms.append(term)
        value = value - term.astype(F32)
    return terms


def split_table(value, parts):
    terms = []
    for _ in range(parts):
        term = float(np.float32(value).astype(ml_dtypes.bfloat16))
        terms.append(term)
        value = value - term
    return terms


def wave(phase, parts):
    near = jnp.minimum(phase, 16 - phase)
    step = jnp.minimum(near, 8 - near)
    flip = near > 4
    steps = [split_table(math.cos(2.0 * math.pi * k / 16.0), parts) for k in range(4)]
    terms = []
    for p in range(parts):
        value = jnp.zeros(phase.shape, F32)
        for k in range(4):
            value = jnp.where(step == k, float(steps[k][p]), value)
        terms.append(jnp.where(flip, -value, value))
    return terms


def waves(phase, parts):
    phase = phase & 15
    return wave(phase, parts), wave((phase + 12) & 15, parts)


def turn(re, im, k, n):
    if k == 0:
        return re, im
    if 4 * k == n:
        return im, -re
    if 8 * k == n:
        half = math.sqrt(0.5)
        return (re + im) * half, (im - re) * half
    if 8 * k == 3 * n:
        half = math.sqrt(0.5)
        return (im - re) * half, (re + im) * -half
    c, s = math.cos(2.0 * math.pi * k / n), math.sin(2.0 * math.pi * k / n)
    return re * c + im * s, im * c - re * s


def fft(re, im):
    n = len(re)
    if n == 1:
        return re, im
    er, ei = fft(re[0::2], im[0::2])
    our, oi = fft(re[1::2], im[1::2])
    half = n // 2
    xr, xi = [None] * n, [None] * n
    for k in range(half):
        tr, ti = turn(our[k], oi[k], k, n)
        xr[k], xi[k] = er[k] + tr, ei[k] + ti
        xr[k + half], xi[k + half] = er[k] - tr, ei[k] - ti
    return xr, xi


def tree(values):
    while len(values) > 1:
        half = len(values) // 2
        values = [a + b for a, b in zip(values[:half], values[half:])]
    return values[0]


def add_lists(a, b):
    return b if a is None else [x + y for x, y in zip(a, b)]


def table_kernel(weight_ref, var_ref, offs_ref, shift_ref, *refs):
    fwd_ref, fwdl_ref, inv_ref, invl_ref, part_ref, wideh_ref, widel_ref = refs[:7]
    big_ref, bigt_ref, small_ref, shift_out_ref, rows_ref = refs[7:]
    shift_out_ref[...] = shift_ref[...]
    offs = jnp.concatenate([offs_ref[...], jnp.zeros((1, LANES - 32), F32)], axis=1)
    small_ref[...] = jnp.concatenate(
        [jnp.exp(var_ref[...]), offs, jnp.zeros((5, LANES), F32)], axis=0
    )

    lane = lax.broadcasted_iota(jnp.int32, (TILE, LANES), 1)
    line = lax.broadcasted_iota(jnp.int32, (TILE, LANES), 0)
    cos, sin = waves(line * (lane & 15), 3)
    for k in range(8):
        at = slice(k * TILE, (k + 1) * TILE)
        mid = slice(128 + k * TILE, 128 + (k + 1) * TILE)
        here = (lane // TILE) == k
        c = [jnp.where(here, v, 0.0).astype(BF16) for v in cos]
        d = [jnp.where(here, v, 0.0).astype(BF16) for v in sin]
        fwd_ref[at, :] = jnp.concatenate([c[0], d[0]], axis=1)
        fwd_ref[mid, :] = jnp.concatenate([c[1], d[1]], axis=1)
        fwdl_ref[at, :] = jnp.concatenate([c[2], d[2]], axis=1)
        inv_ref[at, :] = jnp.concatenate([c[0], c[1]], axis=1)
        inv_ref[mid, :] = jnp.concatenate([-d[0], -d[1]], axis=1)
        invl_ref[at, :] = c[2]
        invl_ref[mid, :] = -d[2]
    line = lax.broadcasted_iota(jnp.int32, (256, 256), 0)
    column = lax.broadcasted_iota(jnp.int32, (256, 256), 1)
    source = 2 * (column & 127) + (column >> 7)
    part_ref[...] = jnp.where(line == source, 1.0, 0.0).astype(BF16)
    lane8 = lax.broadcasted_iota(jnp.int32, (8, LANES), 1)
    line8 = lax.broadcasted_iota(jnp.int32, (8, LANES), 0)
    empty = jnp.zeros((8, LANES), F32)
    for q in range(2):
        cos, sin = waves((2 * line8 + q) * (lane8 & 15), 2)
        for t in range(0, 16, 2):
            for ref, c, d in ((wideh_ref, cos[0], sin[0]), (widel_ref, cos[1], sin[1])):
                rows = []
                for u in (t, t + 1):
                    here = lane8 // TILE == u % 8
                    row = []
                    for v in (c, d):
                        v = jnp.where(here, v, 0.0)
                        row += [v, empty] if u < 8 else [empty, v]
                    rows.append(jnp.concatenate(row, axis=1))
                at = q * 128 + t * 8
                ref[at : at + 16, :] = jnp.concatenate(rows, axis=0).astype(BF16)

    weight = weight_ref[...].astype(F32)
    weight = jnp.concatenate([weight, jnp.zeros((32, LANES - 36), F32)], axis=1)
    halves = []
    for h in range(2):
        at = lax.broadcasted_iota(jnp.int32, (32, LANES), 1) + h * LANES
        group = (at * 171) >> 12
        row = at - 24 * group
        q = jnp.where(group >= 3, 1, 0)
        tap = (3 * (row >> 1) + group - 3 * q) * 4 + 2 * (row & 1) + q
        valid = (row < 6) & (group < 6)
        taken = jnp.take_along_axis(weight, jnp.where(valid, tap, 0), axis=1)
        halves.append(jnp.where(valid, taken, 0.0))
    base = jnp.concatenate(halves, axis=1)
    for sy in range(10):
        moved = pltpu.roll(base, 2 * sy, 1) if sy else base
        big_ref[sy * 32 : (sy + 1) * 32, :] = moved.astype(BF16)

    turned = jnp.transpose(jnp.concatenate([weight] * 4, axis=0))
    rows_ref[...] = jnp.zeros_like(rows_ref)
    for q in range(2):
        for b in range(3):
            for j in range(6):
                tap = (3 * (j // 2) + b) * 4 + 2 * (j % 2) + q
                rows_ref[q * 3 + b, 16 + j : 17 + j, :] = turned[tap : tap + 1, :]
    quarter = lax.broadcasted_iota(jnp.int32, (TILE, LANES), 1) // 32
    for k in range(6):
        for tile in range(3):
            value = jnp.zeros((TILE, LANES), F32)
            for u in range(4):
                sy = 4 * tile + u
                if sy < 10:
                    block = rows_ref[k, 20 - 2 * sy : 36 - 2 * sy, :]
                    value = jnp.where(quarter == u, block, value)
            width = 64 if tile == 2 else LANES
            at = tile * LANES
            bigt_ref[k * TILE : (k + 1) * TILE, at : at + width] = value[:, :width].astype(BF16)


def merge_kernel(dims, *refs):
    nf, fl, G, T, nsc = dims
    F = nf * fl
    dx_refs, refs = refs[:nf], refs[nf:]
    goal_refs, refs = refs[:nf], refs[nf:]
    y_ref, yc_ref, yf_ref, var_ref = refs[:4]
    fwd_ref, fwdl_ref, inv_ref, invl_ref = refs[4:8]
    pack_ref, pc_ref, pf_ref, h_ref = refs[8:12]
    x_ref, idx_ref, p_ref, q_ref, xs_ref, goal_ref = refs[12:18]
    dy_refs, sems = refs[18 : 18 + nf], refs[18 + nf]
    moves = [
        pltpu.make_async_copy(src, dst, sems.at[j])
        for j, (src, dst) in enumerate(zip(dx_refs, dy_refs))
    ]
    for move in moves:
        move.start()
    s = lax.axis_index("space")
    fr = lax.axis_index("frame")
    odd = lax.rem(s, 2)

    slots = ((y_ref, 1), (yc_ref, 2 - 2 * odd), (yf_ref, 2 * odd))

    def fill(f, carry):
        for ref, slot in slots:
            rows = ref[f].astype(F32)
            for g in range(G):
                block = rows[:, g * LANES : (g + 1) * LANES]
                x_ref[f * G + g, pl.ds(pl.multiple_of(slot * TILE, TILE), TILE), :] = block
        return carry

    lax.fori_loop(0, F, fill, 0, unroll=min(F, 4))

    spot = lax.broadcasted_iota(jnp.int32, (8, LANES), 1)
    for j in range(nf):
        for l in range(fl):
            row = dx_refs[j][l, 1]
            if T < LANES:
                row = jnp.concatenate([row, jnp.zeros((1, LANES - T), jnp.int32)], axis=1)
            row = jnp.broadcast_to(row, (8, LANES))
            for g in range(G):
                moved = jnp.take_along_axis(row, 8 * g + spot // TILE, axis=1)
                idx_ref[(j * fl + l) * G + g] = (moved + spot) & (LANES - 1)

    lead = G * 4
    for j in range(nf):
        for c in range(nsc):
            cols = slice(c * LANES, (c + 1) * LANES)
            goal_ref[j * nsc + c] = goal_refs[j][:, :, cols].astype(F32).reshape(256, LANES)
    for k in range(nf * nsc):
        rows = slice(lead + k * 32, lead + k * 32 + 32)
        pc_ref[rows, :] = goal_ref[k, pl.ds(7 - 7 * odd, 32, stride=8), :].astype(BF16)
        pf_ref[rows, :] = goal_ref[k, pl.ds(7 * odd, 32, stride=8), :].astype(BF16)

    lane = lax.broadcasted_iota(jnp.int32, (TILE, LANES), 1)
    kind = (lane // TILE) % 4

    per = 16 // G
    chunks = F * G // 16
    rows_out = max(G, 8)
    fold = TILE // rows_out
    zero = jnp.zeros((TILE, LANES), F32)

    def place(f):
        if nf == 2:
            return f
        return lax.rem(f // fl + nf - fr, nf) * fl + f % fl

    def row_shift(f, t):
        if isinstance(f, int):
            return dy_refs[f // fl][f % fl, 0, 0, t]
        j = lax.div(f, fl)
        l = lax.rem(f, fl)
        value = dy_refs[0][l, 0, 0, t]
        for k in range(1, nf):
            value = jnp.where(j == k, dy_refs[k][l, 0, 0, t], value)
        return value

    first = lax.rem(nf - fr, nf) * fl
    log_var = var_ref[...]
    variances = []
    for k in range(16):
        row = jnp.broadcast_to(log_var[k // 8 : k // 8 + 1], (8, LANES))
        row = jnp.take_along_axis(row, (k % 8) * TILE + spot % TILE, axis=1)
        variances.append(jnp.concatenate([row, row], axis=0))

    def chunk_step(c, carry):
        sums = carry[0] if carry is not None else None
        blocks = []
        for q in range(16):
            g = q % G
            f = place(c * per + q // G)

            def load(t, group):
                if group < 0 or group >= G:
                    return zero
                start = TILE + row_shift(f, 8 * g + t)
                return x_ref[f * G + group, pl.ds(start, TILE), :]

            idx = idx_ref[f * G + g]
            idx = jnp.concatenate([idx, idx], axis=0)
            mixes = (
                jnp.where(
                    lane < 40,
                    load(0, g),
                    jnp.where(lane < 104, load(4, g), load(0, g - 1)),
                ),
                jnp.where(lane < 56, load(1, g), load(5, g)),
                jnp.where(lane < 72, load(2, g), load(6, g)),
                jnp.where(
                    lane < 24,
                    load(7, g + 1),
                    jnp.where(lane < 88, load(3, g), load(7, g)),
                ),
            )
            moved = [jnp.take_along_axis(m, idx, axis=1) for m in mixes]
            blocks.append(
                jnp.where(
                    kind < 2,
                    jnp.where(kind == 0, moved[0], moved[1]),
                    jnp.where(kind == 2, moved[2], moved[3]),
                )
            )
        part = [tree(blocks[g::G]) for g in range(G)]
        sums = add_lists(sums, part)
        base = [x_ref[first * G + g, TILE : 2 * TILE, :] for g in range(G)]
        both = jnp.concatenate(blocks + base, axis=0).astype(BF16)
        pq = dot(jnp.concatenate([both, both], axis=1), fwd_ref[...]) + dot(both, fwdl_ref[...])
        for q in range(16):
            rows = slice(q * TILE, (q + 1) * TILE)
            ref_rows = slice(256 + (q % G) * TILE, 256 + (q % G + 1) * TILE)
            diff = pq[ref_rows] - pq[rows]
            p_ref[rows, :] = diff[:, :LANES]
            q_ref[rows, :] = -diff[:, LANES:]
        re, im = fft(
            [p_ref[pl.ds(n, 16, stride=16), :] for n in range(16)],
            [q_ref[pl.ds(n, 16, stride=16), :] for n in range(16)],
        )
        out = [[], [], [], []]
        for k in range(16):
            energy = re[k] * re[k] + im[k] * im[k]
            weight = energy / (energy + variances[k])
            wr = weight * re[k]
            wi = weight * im[k]
            rest = 1.0 - weight
            for store, val in zip(out, (wr, wi, wr * rest, wi * rest)):
                if fold == 2:
                    val = val[:8] + val[8:]
                store.append(val)
        flat = out[0] + out[1] + out[2] + out[3]
        return sums, add_lists(carry[1] if carry is not None else None, flat)

    for move in moves:
        move.wait()
    carry = chunk_step(0, None)
    if chunks > 1:
        carry = lax.fori_loop(1, chunks, chunk_step, carry)
    sums, flat = carry
    for k in range(32):
        h_ref[k * rows_out : (k + 1) * rows_out, :] = flat[32 + k]

    vi, ur = fft(flat[16:32], flat[:16])
    uv = jnp.concatenate(
        [jnp.concatenate(ur, axis=0), jnp.concatenate(vi, axis=0)], axis=1
    )
    m = 16 * rows_out
    terms = split(uv, 3)
    wide = dot(jnp.concatenate(terms, axis=0), inv_ref[...])
    pix = wide[:m, :LANES] + (wide[m : 2 * m, :LANES] + wide[:m, LANES:])
    pix = pix + (wide[2 * m :, :LANES] + wide[m : 2 * m, LANES:] + dot(terms[0], invl_ref[...]))
    xs_ref[...] = pix
    for g in range(G):
        val = xs_ref[pl.ds(g, 16, stride=rows_out), :]
        for other in range(g + G, rows_out, G):
            val = val + xs_ref[pl.ds(other, 16, stride=rows_out), :]
        val = (sums[g] + val / 256.0) / F
        pack_ref[g] = val
    low = jnp.concatenate([pack_ref[g, 0:4, :] for g in range(G)], axis=0)
    high = jnp.concatenate([pack_ref[g, 12:16, :] for g in range(G)], axis=0)
    pc_ref[0:lead, :] = jnp.where(odd == 1, low, high).astype(BF16)
    pf_ref[0:lead, :] = jnp.where(odd == 1, high, low).astype(BF16)


def demosaic_kernel(dims, pack_ref, pc_ref, pf_ref, h_ref, *refs):
    nf, fl, G, nsc, n_space, inv_pixels = dims
    F = nf * fl
    W = G * LANES
    half = W // 2
    goal_refs = refs[:nf]
    big_ref, bigt_ref, offs_ref, part_ref, wideh_ref, widel_ref = refs[nf : nf + 6]
    out_ref, goal_ref, raw_ref, mm_ref, p_ref, q_ref, ns_ref = refs[nf + 6 :]
    s = lax.axis_index("space")
    fr = lax.axis_index("frame")
    odd = lax.rem(s, 2)
    rows_out = max(G, 8)

    lead = G * 4
    for j in range(nf):
        at = pl.multiple_of(lax.rem(fr + j, nf) * (nsc * LANES), LANES)
        for c in range(nsc):
            cols = slice(c * LANES, (c + 1) * LANES)
            raw_ref[...] = goal_refs[j][:, :, cols].astype(F32).reshape(256, LANES)
            to = pl.ds(pl.multiple_of(at + c * LANES, LANES), LANES)
            for r in range(8):
                goal_ref[r + 1, :, to] = raw_ref[pl.ds(r, 32, stride=8), :]
        for ref, row in ((pc_ref, 9 - 9 * odd), (pf_ref, 9 * odd)):
            for c in range(nsc):
                first = lead + (j * nsc + c) * 32
                val = ref[first : first + 32, :].astype(F32)
                goal_ref[row, :, pl.ds(pl.multiple_of(at + c * LANES, LANES), LANES)] = val

    near = pc_ref[0:lead, :].astype(F32)
    far = pf_ref[0:lead, :].astype(F32)
    low = jnp.where(odd == 1, near, far)
    high = jnp.where(odd == 1, far, near)
    for g in range(G):
        mm_ref[g, 0:4, :] = low[4 * g : 4 * g + 4]
        mm_ref[g, 4:20, :] = pack_ref[g]
        mm_ref[g, 20:24, :] = high[4 * g : 4 * g + 4]
    pairs = jnp.concatenate(
        [jnp.concatenate([mm_ref[2 * h], mm_ref[2 * h + 1]], axis=1) for h in range(G // 2)],
        axis=0,
    )
    parted = dot(pairs.astype(BF16), part_ref[...])
    site = lax.broadcasted_iota(jnp.int32, (24, half), 1)
    pieces = []
    for q in range(2):
        plane = jnp.concatenate(
            [parted[24 * h : 24 * h + 24, q * 128 : (q + 1) * 128] for h in range(G // 2)], axis=1
        )
        pieces.append(jnp.where(site == 0, 0.0, pltpu.roll(plane, 1, 1)))
        pieces.append(plane)
        pieces.append(jnp.where(site == half - 1, 0.0, pltpu.roll(plane, half - 1, 1)))
    pieces.append(jnp.zeros((112, half), F32))
    taps = jnp.concatenate(pieces, axis=0).astype(BF16)

    preact = dot(big_ref[...], taps)
    diag = lax.broadcasted_iota(jnp.int32, (32, LANES), 0) == lax.broadcasted_iota(
        jnp.int32, (32, LANES), 1
    )
    offs = jnp.where(diag, jnp.broadcast_to(offs_ref[2:3, :], (32, LANES)), 0.0)
    offs = jnp.broadcast_to(jnp.sum(offs, axis=1, keepdims=True), (32, half))
    bias = jnp.zeros((32, half), F32)
    slopes = []
    for sy in range(10):
        v = preact[sy * 32 : sy * 32 + 32] + offs
        sig = jax.nn.sigmoid(v)
        slope = (v * sig - goal_ref[sy]) * inv_pixels * (sig * (1.0 + v * (1.0 - sig)))
        if sy == 0:
            slope = jnp.where(s == 0, 0.0, slope)
        elif sy == 9:
            slope = jnp.where(s == n_space - 1, 0.0, slope)
        else:
            bias = bias + slope
        slopes.append(slope)
    slope_bf = jnp.concatenate(slopes, axis=0).astype(BF16)

    gt = dot(bigt_ref[...], slope_bf)
    site16 = lax.broadcasted_iota(jnp.int32, (TILE, half), 1)
    planes = []
    for q in range(2):
        left, mid, right = (gt[(q * 3 + b) * 16 : (q * 3 + b) * 16 + 16] for b in range(3))
        planes.append(
            mid
            + jnp.where(site16 == half - 1, 0.0, pltpu.roll(left, half - 1, 1))
            + jnp.where(site16 == 0, 0.0, pltpu.roll(right, 1, 1))
        )
    grad = jnp.concatenate(
        [
            jnp.concatenate([p[:, h * 128 : (h + 1) * 128] for p in planes], axis=1)
            for h in range(G // 2)
        ],
        axis=0,
    )
    m = grad.shape[0]
    terms = split(grad, 2)
    pq = dot(jnp.concatenate(terms, axis=0), wideh_ref[...])
    pq = pq[:m] + (pq[m:] + dot(terms[0], widel_ref[...]))
    for r in range(rows_out):
        g = r % G
        rows = slice((g // 2) * TILE, (g // 2 + 1) * TILE)
        c0 = (g % 2) * LANES
        p_ref[r * TILE : (r + 1) * TILE, :] = pq[rows, c0 : c0 + LANES]
        q_ref[r * TILE : (r + 1) * TILE, :] = -pq[rows, 256 + c0 : 256 + c0 + LANES]
    gre, gim = fft(
        [p_ref[pl.ds(n, rows_out, stride=16), :] for n in range(16)],
        [q_ref[pl.ds(n, rows_out, stride=16), :] for n in range(16)],
    )
    for k in range(16):
        rows = slice(k * rows_out, (k + 1) * rows_out)
        rows_im = slice((16 + k) * rows_out, (17 + k) * rows_out)
        ns_ref[rows, :] = gre[k] * h_ref[rows, :] + gim[k] * h_ref[rows_im, :]
    noise = ns_ref[pl.ds(0, 16, stride=rows_out), :]
    for r in range(1, rows_out):
        noise = noise + ns_ref[pl.ds(r, 16, stride=rows_out), :]
    noise = noise * (-1.0 / (256.0 * F))
    for step in (64, 32, 16):
        noise = noise + pltpu.roll(noise, step, 1)

    prod = dot(slope_bf[32:288], taps, ((1,), (1,)))
    gw = jnp.zeros((32, 256), F32)
    for sy in range(1, 9):
        gw = gw + pltpu.roll(prod[(sy - 1) * 32 : sy * 32], 256 - 2 * sy, 1)
    tap = lax.broadcasted_iota(jnp.int32, (32, LANES), 1)
    pair = tap >> 2
    a = (pair * 11) >> 5
    source = ((tap & 1) * 3 + pair - 3 * a) * 24 + 2 * a + ((tap >> 1) & 1)
    source = jnp.where(tap < 36, source, 0)
    lower_part = jnp.take_along_axis(gw[:, :LANES], source & 127, axis=1)
    upper_part = jnp.take_along_axis(gw[:, LANES:], source & 127, axis=1)
    gw = jnp.where(source < LANES, lower_part, upper_part)
    gw = jnp.where(tap == 36, jnp.sum(bias, axis=1, keepdims=True), gw)
    gw = jnp.where(tap < 37, gw, 0.0)
    first = gw[0:8] + (pltpu.roll(gw[8:16], 37, 1) + pltpu.roll(gw[16:24], 74, 1))
    group = lax.broadcasted_iota(jnp.int32, (8, LANES), 1) // TILE
    second = jnp.where(group == 5, noise[:8], jnp.where(group == 6, noise[8:], gw[24:32]))
    out_ref[...] = jnp.concatenate([first, second], axis=0)


def last_sum(nf, pack_ref, own_ref, got_ref, merged_ref, weight_ref, bias_ref, noise_ref):
    own = pack_ref.shape[0] // nf
    fr = lax.axis_index("frame")
    for k in range(own):
        merged_ref[:, k * LANES : (k + 1) * LANES] = pack_ref[fr * own + k]
    total = own_ref[...] + got_ref[...]
    first, second = total[:8], total[8:]
    gw = jnp.concatenate(
        [first, pltpu.roll(first, LANES - 37, 1), pltpu.roll(first, LANES - 74, 1), second], axis=0
    )
    weight_ref[...] = gw[:, :36]
    line = lax.broadcasted_iota(jnp.int32, (32, LANES), 0)
    lane = lax.broadcasted_iota(jnp.int32, (32, LANES), 1)
    bias = jnp.where(line == lane, jnp.broadcast_to(gw[:, 36:37], (32, LANES)), 0.0)
    bias_ref[...] = jnp.sum(bias, axis=0, keepdims=True)[:, :32]
    group = lane[:8] // TILE
    for k in range(2):
        part = jnp.where(group == 5 + k, second, 0.0)
        for step in (16, 32, 64):
            part = part + pltpu.roll(part, step, 1)
        part = jnp.where(group == line[:8], part, 0.0)
        noise_ref[k : k + 1, :] = jnp.sum(part, axis=0, keepdims=True)


def involution(value, count, step, first):
    pairs = []
    for i in range(first, count):
        j = ((i - first) ^ step) + first
        if j < count:
            pairs.append((i, j))
    return lax.ppermute(value, "space", pairs)


def sum_space(value, count):
    bits = count.bit_length() - 1
    assert 1 << bits == count
    stages = []
    at = 0
    while at < bits:
        width = 2 if at == 1 and bits - at >= 3 else 1
        stages.append([m << at for m in range(1, 1 << width)])
        at += width
    for masks in stages[:-1]:
        got = []
        for m in masks:
            got.append(lax.ppermute(value, "space", [(i, i ^ m) for i in range(count)]))
        value = value + got[0]
        if len(got) == 3:
            value = value + (got[1] + got[2])
    (mask,) = stages[-1]
    got = lax.ppermute(value, "space", [(i, i ^ mask) for i in range(count)])
    return value, got


def call(body, args, outs, scratch):
    vm = pl.BlockSpec(memory_space=pltpu.VMEM)
    sizes = [int(np.prod(a.shape)) * a.dtype.itemsize for a in list(args) + list(outs)]
    sizes += [int(np.prod(a.shape)) * 4 for a in scratch if a.memory_space == pltpu.VMEM]
    return pl.pallas_call(
        body,
        out_shape=tuple(outs),
        in_specs=[vm] * len(args),
        out_specs=(vm,) * len(outs),
        scratch_shapes=scratch,
        compiler_params=pltpu.CompilerParams(vmem_limit_bytes=sum(sizes) + (12 << 20)),
    )(*args)


def shards(raw, shifts, weight, offset, log_var, goal):
    nf = lax.axis_size("frame")
    n_space = lax.axis_size("space")
    fl, band_rows, W = raw.shape
    T = shifts.shape[3]
    channels, _, ws = goal.shape
    G = W // LANES
    F = nf * fl
    nsc = ws // LANES
    inv_pixels = 1.0 / (band_rows * n_space * W // 4)
    rows_out = max(G, 8)

    def from_frame(value, j):
        return lax.ppermute(value, "frame", [(i, (i - j) % nf) for i in range(nf)])

    def pieces(value):
        return [value] + [from_frame(value, j) for j in range(1, nf)]

    raws = pieces(raw)
    goals = pieces(goal)
    shift_parts = pieces(shifts)
    y = jnp.pad(raw, ((0, F - fl), (0, 0), (0, 0)))
    y = lax.optimization_barrier(y)
    for j in range(1, nf):
        y = lax.dynamic_update_slice(y, raws[j], (j * fl, 0, 0))
    yf = involution(y, n_space, 1, 1)
    yc = involution(y, n_space, 1, 0)
    shape = jax.ShapeDtypeStruct
    *tables, big, bigt, small, own_shifts = call(
        table_kernel,
        [weight, log_var.reshape(2, LANES), offset.reshape(1, channels), shifts],
        [
            shape((256, 256), BF16),
            shape((128, 256), BF16),
            shape((256, 256), BF16),
            shape((256, 128), BF16),
            shape((256, 256), BF16),
            shape((256, 512), BF16),
            shape((256, 512), BF16),
            shape((320, 256), BF16),
            shape((96, 320), BF16),
            shape((8, LANES), F32),
            shape(shifts.shape, jnp.int32),
        ],
        [pltpu.VMEM((6, 40, LANES), F32)],
    )
    shift_parts[0] = own_shifts

    side = 4 * G + nf * nsc * channels
    pack, pc, pf, moments = call(
        functools.partial(merge_kernel, (nf, fl, G, T, nsc)),
        [*shift_parts, *goals, y, yc, yf, small, *tables[:4]],
        [
            shape((G, TILE, LANES), F32),
            shape((side, LANES), BF16),
            shape((side, LANES), BF16),
            shape((32 * rows_out, LANES), F32),
        ],
        [
            pltpu.VMEM((F * G, 3 * TILE, LANES), F32),
            pltpu.VMEM((F * G, 8, LANES), jnp.int32),
            pltpu.VMEM((256, LANES), F32),
            pltpu.VMEM((256, LANES), F32),
            pltpu.VMEM((16 * rows_out, LANES), F32),
            pltpu.VMEM((nf * nsc, 256, LANES), F32),
            *[pltpu.SMEM(shifts.shape, jnp.int32)] * nf,
            pltpu.SemaphoreType.DMA((nf,)),
        ],
    )
    pf = involution(pf, n_space, 1, 1)
    pc = involution(pc, n_space, 1, 0)
    (partial,) = call(
        functools.partial(demosaic_kernel, (nf, fl, G, nsc, n_space, inv_pixels)),
        [pack, pc, pf, moments, *goals, big, bigt, small, *tables[4:]],
        [shape((16, LANES), F32)],
        [
            pltpu.VMEM((10, channels, W // 2), F32),
            pltpu.VMEM((256, LANES), F32),
            pltpu.VMEM((G, 24, LANES), F32),
            pltpu.VMEM((rows_out * TILE, LANES), F32),
            pltpu.VMEM((rows_out * TILE, LANES), F32),
            pltpu.VMEM((rows_out * TILE, LANES), F32),
        ],
    )
    merged, grad_weight, grad_bias, grad_noise = call(
        functools.partial(last_sum, nf),
        [pack, *sum_space(partial, n_space)],
        [
            shape((TILE, W // nf), F32),
            shape((channels, 36), F32),
            shape((1, channels), F32),
            shape((2, LANES), F32),
        ],
        [],
    )
    return merged, grad_weight, grad_bias.reshape(channels), grad_noise.reshape(256)


def solution(mesh):
    placed = (
        P("frame", "space", None),
        P("frame", None, "space", None),
        P(),
        P(),
        P(),
        P(None, "space", "frame"),
    )

    return jax.shard_map(
        shards,
        mesh=mesh,
        in_specs=placed,
        out_specs=(P("space", "frame"), P(), P(), P()),
        check_vma=False,
    )
```

```python
import functools
import math

import jax
import jax.numpy as jnp
import ml_dtypes
import numpy as np
from jax import lax
from jax.experimental import pallas as pl
from jax.experimental.pallas import tpu as pltpu
from jax.sharding import PartitionSpec as P


TILE = 16
LANES = 128
F32 = jnp.float32
BF16 = jnp.bfloat16


def dot(a, b, dims=((1,), (0,))):
    return lax.dot_general(a, b, (dims, ((), ())), preferred_element_type=F32)


def split(value, parts):
    terms = []
    for _ in range(parts):
        term = value.astype(BF16)
        terms.append(term)
        value = value - term.astype(F32)
    return terms


def split_table(value, parts):
    terms = []
    for _ in range(parts):
        term = float(np.float32(value).astype(ml_dtypes.bfloat16))
        terms.append(term)
        value = value - term
    return terms


def wave(phase, parts):
    near = jnp.minimum(phase, 16 - phase)
    step = jnp.minimum(near, 8 - near)
    flip = near > 4
    steps = [split_table(math.cos(2.0 * math.pi * k / 16.0), parts) for k in range(4)]
    terms = []
    for p in range(parts):
        value = jnp.zeros(phase.shape, F32)
        for k in range(4):
            value = jnp.where(step == k, float(steps[k][p]), value)
        terms.append(jnp.where(flip, -value, value))
    return terms


def waves(phase, parts):
    phase = phase & 15
    return wave(phase, parts), wave((phase + 12) & 15, parts)


def turn(re, im, k, n):
    if k == 0:
        return re, im
    if 4 * k == n:
        return im, -re
    if 8 * k == n:
        half = math.sqrt(0.5)
        return (re + im) * half, (im - re) * half
    if 8 * k == 3 * n:
        half = math.sqrt(0.5)
        return (im - re) * half, (re + im) * -half
    c, s = math.cos(2.0 * math.pi * k / n), math.sin(2.0 * math.pi * k / n)
    return re * c + im * s, im * c - re * s


def fft(re, im):
    n = len(re)
    if n == 1:
        return re, im
    er, ei = fft(re[0::2], im[0::2])
    our, oi = fft(re[1::2], im[1::2])
    half = n // 2
    xr, xi = [None] * n, [None] * n
    for k in range(half):
        tr, ti = turn(our[k], oi[k], k, n)
        xr[k], xi[k] = er[k] + tr, ei[k] + ti
        xr[k + half], xi[k + half] = er[k] - tr, ei[k] - ti
    return xr, xi


def tree(values):
    while len(values) > 1:
        half = len(values) // 2
        values = [a + b for a, b in zip(values[:half], values[half:])]
    return values[0]


def add_lists(a, b):
    return b if a is None else [x + y for x, y in zip(a, b)]


def table_kernel(dims, weight_ref, var_ref, offs_ref, *refs):
    nf, fl, nsc, T = dims
    shift_refs, goal_refs, refs = refs[:nf], refs[nf : 2 * nf], refs[2 * nf :]
    fwd_ref, fwdl_ref, inv_ref, invl_ref, part_ref, wideh_ref, widel_ref = refs[:7]
    big_ref, bigt_ref, small_ref, own_ref, side_ref, edge_ref, goal_ref, rows_ref, raw_ref = refs[7:]
    odd = lax.rem(lax.axis_index("space"), 2)
    fr = lax.axis_index("frame")
    offs = jnp.concatenate([offs_ref[...], jnp.zeros((1, LANES - 32), F32)], axis=1)
    small_ref[...] = jnp.concatenate(
        [jnp.exp(var_ref[...]), offs, jnp.zeros((5, LANES), F32)], axis=0
    )
    for j in range(nf):
        for l in range(fl):
            for c in range(2):
                row = shift_refs[j][l, c]
                if T < LANES:
                    row = jnp.concatenate([row, jnp.zeros((1, LANES - T), jnp.int32)], axis=1)
                at = (j * fl + l) * 2 + c
                own_ref[at : at + 1, :] = row
    count = nf * fl * 2
    words = own_ref[...].astype(F32)
    if count % 16:
        words = jnp.concatenate([words, jnp.zeros((16 - count % 16, LANES), F32)], axis=0)
    lead = nf * nsc * 32
    side_ref[lead:, :] = words.astype(BF16)
    for j in range(nf):
        at = pl.multiple_of(lax.rem(fr + j, nf) * (nsc * LANES), LANES)
        for c in range(nsc):
            cols = slice(c * LANES, (c + 1) * LANES)
            raw_ref[...] = goal_refs[j][:, :, cols].astype(F32).reshape(256, LANES)
            to = pl.ds(pl.multiple_of(at + c * LANES, LANES), LANES)
            for r in range(8):
                goal_ref[r, :, to] = raw_ref[pl.ds(r, 32, stride=8), :]
            rows = slice((j * nsc + c) * 32, (j * nsc + c) * 32 + 32)
            edge_ref[rows, :] = raw_ref[pl.ds(7 - 7 * odd, 32, stride=8), :].astype(BF16)
            side_ref[rows, :] = raw_ref[pl.ds(7 * odd, 32, stride=8), :].astype(BF16)

    lane = lax.broadcasted_iota(jnp.int32, (TILE, LANES), 1)
    line = lax.broadcasted_iota(jnp.int32, (TILE, LANES), 0)
    cos, sin = waves(line * (lane & 15), 3)
    for k in range(8):
        at = slice(k * TILE, (k + 1) * TILE)
        mid = slice(128 + k * TILE, 128 + (k + 1) * TILE)
        here = (lane // TILE) == k
        c = [jnp.where(here, v, 0.0).astype(BF16) for v in cos]
        d = [jnp.where(here, v, 0.0).astype(BF16) for v in sin]
        fwd_ref[at, :] = jnp.concatenate([c[0], d[0]], axis=1)
        fwd_ref[mid, :] = jnp.concatenate([c[1], d[1]], axis=1)
        fwdl_ref[at, :] = jnp.concatenate([c[2], d[2]], axis=1)
        inv_ref[at, :] = jnp.concatenate([c[0], c[1]], axis=1)
        inv_ref[mid, :] = jnp.concatenate([-d[0], -d[1]], axis=1)
        invl_ref[at, :] = c[2]
        invl_ref[mid, :] = -d[2]
    line = lax.broadcasted_iota(jnp.int32, (256, 256), 0)
    column = lax.broadcasted_iota(jnp.int32, (256, 256), 1)
    source = 2 * (column & 127) + (column >> 7)
    part_ref[...] = jnp.where(line == source, 1.0, 0.0).astype(BF16)
    lane8 = lax.broadcasted_iota(jnp.int32, (8, LANES), 1)
    line8 = lax.broadcasted_iota(jnp.int32, (8, LANES), 0)
    empty = jnp.zeros((8, LANES), F32)
    for q in range(2):
        cos, sin = waves((2 * line8 + q) * (lane8 & 15), 2)
        for t in range(0, 16, 2):
            for ref, c, d in ((wideh_ref, cos[0], sin[0]), (widel_ref, cos[1], sin[1])):
                rows = []
                for u in (t, t + 1):
                    here = lane8 // TILE == u % 8
                    row = []
                    for v in (c, d):
                        v = jnp.where(here, v, 0.0)
                        row += [v, empty] if u < 8 else [empty, v]
                    rows.append(jnp.concatenate(row, axis=1))
                at = q * 128 + t * 8
                ref[at : at + 16, :] = jnp.concatenate(rows, axis=0).astype(BF16)

    weight = weight_ref[...].astype(F32)
    weight = jnp.concatenate([weight, jnp.zeros((32, LANES - 36), F32)], axis=1)
    halves = []
    for h in range(2):
        at = lax.broadcasted_iota(jnp.int32, (32, LANES), 1) + h * LANES
        group = (at * 171) >> 12
        row = at - 24 * group
        q = jnp.where(group >= 3, 1, 0)
        tap = (3 * (row >> 1) + group - 3 * q) * 4 + 2 * (row & 1) + q
        valid = (row < 6) & (group < 6)
        taken = jnp.take_along_axis(weight, jnp.where(valid, tap, 0), axis=1)
        halves.append(jnp.where(valid, taken, 0.0))
    base = jnp.concatenate(halves, axis=1)
    for sy in range(10):
        moved = pltpu.roll(base, 2 * sy, 1) if sy else base
        big_ref[sy * 32 : (sy + 1) * 32, :] = moved.astype(BF16)

    turned = jnp.transpose(jnp.concatenate([weight] * 4, axis=0))
    rows_ref[...] = jnp.zeros_like(rows_ref)
    for q in range(2):
        for b in range(3):
            for j in range(6):
                tap = (3 * (j // 2) + b) * 4 + 2 * (j % 2) + q
                rows_ref[q * 3 + b, 16 + j : 17 + j, :] = turned[tap : tap + 1, :]
    quarter = lax.broadcasted_iota(jnp.int32, (TILE, LANES), 1) // 32
    for k in range(6):
        for tile in range(3):
            value = jnp.zeros((TILE, LANES), F32)
            for u in range(4):
                sy = 4 * tile + u
                if sy < 10:
                    block = rows_ref[k, 20 - 2 * sy : 36 - 2 * sy, :]
                    value = jnp.where(quarter == u, block, value)
            width = 64 if tile == 2 else LANES
            at = tile * LANES
            bigt_ref[k * TILE : (k + 1) * TILE, at : at + width] = value[:, :width].astype(BF16)


def merge_kernel(dims, *refs):
    nf, fl, G, _, nsc = dims
    F = nf * fl
    own_ref, side_ref, edge_ref, y_ref, yc_ref, yf_ref, var_ref = refs[:7]
    fwd_ref, fwdl_ref, inv_ref, invl_ref = refs[7:11]
    pack_ref, pc_ref, far_ref, h_ref = refs[11:15]
    x_ref, idx_ref, p_ref, q_ref, xs_ref, words_ref, own_sm, far_sm, sems = refs[15:]
    s = lax.axis_index("space")
    fr = lax.axis_index("frame")
    odd = lax.rem(s, 2)
    lead = nf * nsc * 32

    words = side_ref[lead:, :].astype(F32).astype(jnp.int32)
    words_ref[...] = words[: 2 * F]
    moves = (
        pltpu.make_async_copy(own_ref, own_sm, sems.at[0]),
        pltpu.make_async_copy(words_ref, far_sm, sems.at[1]),
    )
    for move in moves:
        move.start()

    slots = (
        (y_ref, 0, 2 - odd),
        (yc_ref, 0, 3 - 3 * odd),
        (yf_ref, 0, 1 + odd),
        (yf_ref, F, 3 * odd),
    )

    def fill(f, carry):
        for ref, start, slot in slots:
            rows = ref[start + f].astype(F32)
            for g in range(G):
                block = rows[:, g * LANES : (g + 1) * LANES]
                x_ref[f * G + g, pl.ds(pl.multiple_of(slot * TILE, TILE), TILE), :] = block
        return carry

    lax.fori_loop(0, F, fill, 0, unroll=min(F, 4))

    spot = lax.broadcasted_iota(jnp.int32, (8, LANES), 1)
    for which, ref in enumerate((own_ref, words_ref)):
        for f in range(F):
            row = jnp.broadcast_to(ref[2 * f + 1 : 2 * f + 2, :], (8, LANES))
            for g in range(G):
                moved = jnp.take_along_axis(row, 8 * g + spot // TILE, axis=1)
                idx_ref[which, f * G + g] = (moved + spot) & (LANES - 1)
    pc_ref[4 * G :, :] = edge_ref[...]

    lane = lax.broadcasted_iota(jnp.int32, (TILE, LANES), 1)
    kind = (lane // TILE) % 4
    per = 16 // G
    chunks = F * G // 16
    rows_out = max(G, 8)
    fold = TILE // rows_out
    zero = jnp.zeros((TILE, LANES), F32)

    def place(f):
        if nf == 2:
            return f
        return lax.rem(f // fl + nf - fr, nf) * fl + f % fl

    first = lax.rem(nf - fr, nf) * fl
    log_var = var_ref[...]
    variances = []
    for k in range(16):
        row = jnp.broadcast_to(log_var[k // 8 : k // 8 + 1], (8, LANES))
        row = jnp.take_along_axis(row, (k % 8) * TILE + spot % TILE, axis=1)
        variances.append(jnp.concatenate([row, row], axis=0))

    def tile_row(which, row0, dy_ref, c, carry):
        sums = carry[0] if carry is not None else None
        blocks = []
        for q in range(16):
            g = q % G
            f = place(c * per + q // G)

            def load(t, group):
                if group < 0 or group >= G:
                    return zero
                start = row0 + dy_ref[2 * f, 8 * g + t]
                return x_ref[f * G + group, pl.ds(start, TILE), :]

            idx = idx_ref[which, f * G + g]
            idx = jnp.concatenate([idx, idx], axis=0)
            mixes = (
                jnp.where(
                    lane < 40,
                    load(0, g),
                    jnp.where(lane < 104, load(4, g), load(0, g - 1)),
                ),
                jnp.where(lane < 56, load(1, g), load(5, g)),
                jnp.where(lane < 72, load(2, g), load(6, g)),
                jnp.where(
                    lane < 24,
                    load(7, g + 1),
                    jnp.where(lane < 88, load(3, g), load(7, g)),
                ),
            )
            moved = [jnp.take_along_axis(m, idx, axis=1) for m in mixes]
            blocks.append(
                jnp.where(
                    kind < 2,
                    jnp.where(kind == 0, moved[0], moved[1]),
                    jnp.where(kind == 2, moved[2], moved[3]),
                )
            )
        base = [x_ref[first * G + g, pl.ds(pl.multiple_of(row0, TILE), TILE), :] for g in range(G)]
        both = jnp.concatenate(blocks + base, axis=0).astype(BF16)
        pq = dot(jnp.concatenate([both, both], axis=1), fwd_ref[...]) + dot(both, fwdl_ref[...])
        for q in range(16):
            rows = slice(q * TILE, (q + 1) * TILE)
            ref_rows = slice(256 + (q % G) * TILE, 256 + (q % G + 1) * TILE)
            diff = pq[ref_rows] - pq[rows]
            p_ref[which, rows, :] = diff[:, :LANES]
            q_ref[which, rows, :] = -diff[:, LANES:]
        re, im = fft(
            [p_ref[which, pl.ds(n, 16, stride=16), :] for n in range(16)],
            [q_ref[which, pl.ds(n, 16, stride=16), :] for n in range(16)],
        )
        out = [[], [], [], []]
        for k in range(16):
            energy = re[k] * re[k] + im[k] * im[k]
            weight = energy / (energy + variances[k])
            wr = weight * re[k]
            wi = weight * im[k]
            vals = (wr, wi)
            if which == 0:
                rest = 1.0 - weight
                vals = (wr, wi, wr * rest, wi * rest)
            for store, val in zip(out, vals):
                if fold == 2:
                    val = val[:8] + val[8:]
                store.append(val)
        flat = out[0] + out[1] + out[2] + out[3]
        return sums_of(sums, blocks), add_lists(carry[1] if carry is not None else None, flat)

    def sums_of(sums, blocks):
        return add_lists(sums, [tree(blocks[g::G]) for g in range(G)])

    def whole_row(which, row0, dy_ref):
        step = functools.partial(tile_row, which, row0, dy_ref)
        carry = step(0, None)
        if chunks > 1:
            carry = lax.fori_loop(1, chunks, step, carry)
        return carry

    moves[0].wait()
    sums, flat = whole_row(0, (2 - odd) * TILE, own_sm)
    for k in range(32):
        h_ref[k * rows_out : (k + 1) * rows_out, :] = flat[32 + k]
    moves[1].wait()
    far_sums, far_flat = whole_row(1, (1 + odd) * TILE, far_sm)

    vi, ur = fft(flat[16:32], flat[:16])
    far_vi, far_ur = fft(far_flat[16:32], far_flat[:16])
    at_odd = odd == 1
    ur += [jnp.where(at_odd, far_ur[k], far_ur[12 + k]) for k in range(4)]
    vi += [jnp.where(at_odd, far_vi[k], far_vi[12 + k]) for k in range(4)]
    uv = jnp.concatenate([jnp.concatenate(ur, axis=0), jnp.concatenate(vi, axis=0)], axis=1)
    m = 20 * rows_out
    terms = split(uv, 3)
    wide = dot(jnp.concatenate(terms, axis=0), inv_ref[...])
    pix = wide[:m, :LANES] + (wide[m : 2 * m, :LANES] + wide[:m, LANES:])
    pix = pix + (wide[2 * m :, :LANES] + wide[m : 2 * m, LANES:] + dot(terms[0], invl_ref[...]))
    xs_ref[...] = pix
    far_rows = []
    for g in range(G):
        val = xs_ref[pl.ds(g, 16, stride=rows_out), :]
        far = xs_ref[pl.ds(16 * rows_out + g, 4, stride=rows_out), :]
        for other in range(g + G, rows_out, G):
            val = val + xs_ref[pl.ds(other, 16, stride=rows_out), :]
            far = far + xs_ref[pl.ds(16 * rows_out + other, 4, stride=rows_out), :]
        pack_ref[g] = (sums[g] + val / 256.0) / F
        far_sum = jnp.where(at_odd, far_sums[g][0:4], far_sums[g][12:16])
        far_rows.append((far_sum + far / 256.0) / F)
    far_ref[...] = jnp.concatenate(far_rows, axis=0)
    low = jnp.concatenate([pack_ref[g, 0:4, :] for g in range(G)], axis=0)
    high = jnp.concatenate([pack_ref[g, 12:16, :] for g in range(G)], axis=0)
    pc_ref[0 : 4 * G, :] = jnp.where(at_odd, low, high).astype(BF16)


def demosaic_kernel(dims, pack_ref, pc_ref, far_ref, side_ref, goals_ref, h_ref, *refs):
    nf, fl, G, nsc, n_space, inv_pixels = dims
    F = nf * fl
    W = G * LANES
    half = W // 2
    big_ref, bigt_ref, offs_ref, part_ref, wideh_ref, widel_ref = refs[:6]
    out_ref, goal_ref, mm_ref, p_ref, q_ref, ns_ref = refs[6:]
    s = lax.axis_index("space")
    fr = lax.axis_index("frame")
    odd = lax.rem(s, 2)
    rows_out = max(G, 8)

    lead = G * 4
    for j in range(nf):
        at = pl.multiple_of(lax.rem(fr + j, nf) * (nsc * LANES), LANES)
        for c in range(nsc):
            first = (j * nsc + c) * 32
            to = pl.ds(pl.multiple_of(at + c * LANES, LANES), LANES)
            goal_ref[1 - odd, :, to] = pc_ref[lead + first : lead + first + 32, :].astype(F32)
            goal_ref[odd, :, to] = side_ref[first : first + 32, :].astype(F32)

    near = pc_ref[0:lead, :].astype(F32)
    far = far_ref[...]
    low = jnp.where(odd == 1, near, far)
    high = jnp.where(odd == 1, far, near)
    for g in range(G):
        mm_ref[g, 0:4, :] = low[4 * g : 4 * g + 4]
        mm_ref[g, 4:20, :] = pack_ref[g]
        mm_ref[g, 20:24, :] = high[4 * g : 4 * g + 4]
    pairs = jnp.concatenate(
        [jnp.concatenate([mm_ref[2 * h], mm_ref[2 * h + 1]], axis=1) for h in range(G // 2)],
        axis=0,
    )
    parted = dot(pairs.astype(BF16), part_ref[...])
    site = lax.broadcasted_iota(jnp.int32, (24, half), 1)
    pieces = []
    for q in range(2):
        plane = jnp.concatenate(
            [parted[24 * h : 24 * h + 24, q * 128 : (q + 1) * 128] for h in range(G // 2)], axis=1
        )
        pieces.append(jnp.where(site == 0, 0.0, pltpu.roll(plane, 1, 1)))
        pieces.append(plane)
        pieces.append(jnp.where(site == half - 1, 0.0, pltpu.roll(plane, half - 1, 1)))
    pieces.append(jnp.zeros((112, half), F32))
    taps = jnp.concatenate(pieces, axis=0).astype(BF16)

    preact = dot(big_ref[...], taps)
    diag = lax.broadcasted_iota(jnp.int32, (32, LANES), 0) == lax.broadcasted_iota(
        jnp.int32, (32, LANES), 1
    )
    offs = jnp.where(diag, jnp.broadcast_to(offs_ref[2:3, :], (32, LANES)), 0.0)
    offs = jnp.broadcast_to(jnp.sum(offs, axis=1, keepdims=True), (32, half))
    bias = jnp.zeros((32, half), F32)
    slopes = []
    for sy in range(10):
        v = preact[sy * 32 : sy * 32 + 32] + offs
        sig = jax.nn.sigmoid(v)
        goal = goal_ref[0] if sy == 0 else goal_ref[1] if sy == 9 else goals_ref[sy - 1]
        slope = (v * sig - goal) * inv_pixels * (sig * (1.0 + v * (1.0 - sig)))
        if sy == 0:
            slope = jnp.where(s == 0, 0.0, slope)
        elif sy == 9:
            slope = jnp.where(s == n_space - 1, 0.0, slope)
        else:
            bias = bias + slope
        slopes.append(slope)
    slope_bf = jnp.concatenate(slopes, axis=0).astype(BF16)

    gt = dot(bigt_ref[...], slope_bf)
    site16 = lax.broadcasted_iota(jnp.int32, (TILE, half), 1)
    planes = []
    for q in range(2):
        left, mid, right = (gt[(q * 3 + b) * 16 : (q * 3 + b) * 16 + 16] for b in range(3))
        planes.append(
            mid
            + jnp.where(site16 == half - 1, 0.0, pltpu.roll(left, half - 1, 1))
            + jnp.where(site16 == 0, 0.0, pltpu.roll(right, 1, 1))
        )
    grad = jnp.concatenate(
        [
            jnp.concatenate([p[:, h * 128 : (h + 1) * 128] for p in planes], axis=1)
            for h in range(G // 2)
        ],
        axis=0,
    )
    m = grad.shape[0]
    terms = split(grad, 2)
    pq = dot(jnp.concatenate(terms, axis=0), wideh_ref[...])
    pq = pq[:m] + (pq[m:] + dot(terms[0], widel_ref[...]))
    for r in range(rows_out):
        g = r % G
        rows = slice((g // 2) * TILE, (g // 2 + 1) * TILE)
        c0 = (g % 2) * LANES
        p_ref[r * TILE : (r + 1) * TILE, :] = pq[rows, c0 : c0 + LANES]
        q_ref[r * TILE : (r + 1) * TILE, :] = -pq[rows, 256 + c0 : 256 + c0 + LANES]
    gre, gim = fft(
        [p_ref[pl.ds(n, rows_out, stride=16), :] for n in range(16)],
        [q_ref[pl.ds(n, rows_out, stride=16), :] for n in range(16)],
    )
    for k in range(16):
        rows = slice(k * rows_out, (k + 1) * rows_out)
        rows_im = slice((16 + k) * rows_out, (17 + k) * rows_out)
        ns_ref[rows, :] = gre[k] * h_ref[rows, :] + gim[k] * h_ref[rows_im, :]
    noise = ns_ref[pl.ds(0, 16, stride=rows_out), :]
    for r in range(1, rows_out):
        noise = noise + ns_ref[pl.ds(r, 16, stride=rows_out), :]
    noise = noise * (-1.0 / (256.0 * F))
    for step in (64, 32, 16):
        noise = noise + pltpu.roll(noise, step, 1)

    prod = dot(slope_bf[32:288], taps, ((1,), (1,)))
    gw = jnp.zeros((32, 256), F32)
    for sy in range(1, 9):
        gw = gw + pltpu.roll(prod[(sy - 1) * 32 : sy * 32], 256 - 2 * sy, 1)
    tap = lax.broadcasted_iota(jnp.int32, (32, LANES), 1)
    pair = tap >> 2
    a = (pair * 11) >> 5
    source = ((tap & 1) * 3 + pair - 3 * a) * 24 + 2 * a + ((tap >> 1) & 1)
    source = jnp.where(tap < 36, source, 0)
    lower_part = jnp.take_along_axis(gw[:, :LANES], source & 127, axis=1)
    upper_part = jnp.take_along_axis(gw[:, LANES:], source & 127, axis=1)
    gw = jnp.where(source < LANES, lower_part, upper_part)
    gw = jnp.where(tap == 36, jnp.sum(bias, axis=1, keepdims=True), gw)
    gw = jnp.where(tap < 37, gw, 0.0)
    first = gw[0:8] + (pltpu.roll(gw[8:16], 37, 1) + pltpu.roll(gw[16:24], 74, 1))
    group = lax.broadcasted_iota(jnp.int32, (8, LANES), 1) // TILE
    second = jnp.where(group == 5, noise[:8], jnp.where(group == 6, noise[8:], gw[24:32]))
    out_ref[...] = jnp.concatenate([first, second], axis=0)


def last_sum(nf, pack_ref, own_ref, got_ref, merged_ref, weight_ref, bias_ref, noise_ref):
    own = pack_ref.shape[0] // nf
    fr = lax.axis_index("frame")
    for k in range(own):
        merged_ref[:, k * LANES : (k + 1) * LANES] = pack_ref[fr * own + k]
    total = own_ref[...] + got_ref[...]
    first, second = total[:8], total[8:]
    gw = jnp.concatenate(
        [first, pltpu.roll(first, LANES - 37, 1), pltpu.roll(first, LANES - 74, 1), second], axis=0
    )
    weight_ref[...] = gw[:, :36]
    line = lax.broadcasted_iota(jnp.int32, (32, LANES), 0)
    lane = lax.broadcasted_iota(jnp.int32, (32, LANES), 1)
    bias = jnp.where(line == lane, jnp.broadcast_to(gw[:, 36:37], (32, LANES)), 0.0)
    bias_ref[...] = jnp.sum(bias, axis=0, keepdims=True)[:, :32]
    group = lane[:8] // TILE
    for k in range(2):
        part = jnp.where(group == 5 + k, second, 0.0)
        for step in (16, 32, 64):
            part = part + pltpu.roll(part, step, 1)
        part = jnp.where(group == line[:8], part, 0.0)
        noise_ref[k : k + 1, :] = jnp.sum(part, axis=0, keepdims=True)


def involution(value, count, step, first):
    pairs = []
    for i in range(first, count):
        j = ((i - first) ^ step) + first
        if j < count:
            pairs.append((i, j))
    return lax.ppermute(value, "space", pairs)


def sum_space(value, count):
    bits = count.bit_length() - 1
    assert 1 << bits == count
    stages = []
    at = 0
    while at < bits:
        width = 2 if at == 1 and bits - at >= 3 else 1
        stages.append([m << at for m in range(1, 1 << width)])
        at += width
    for masks in stages[:-1]:
        got = []
        for m in masks:
            got.append(lax.ppermute(value, "space", [(i, i ^ m) for i in range(count)]))
        value = value + got[0]
        if len(got) == 3:
            value = value + (got[1] + got[2])
    (mask,) = stages[-1]
    got = lax.ppermute(value, "space", [(i, i ^ mask) for i in range(count)])
    return value, got


def call(body, args, outs, scratch):
    vm = pl.BlockSpec(memory_space=pltpu.VMEM)
    sizes = [int(np.prod(a.shape)) * a.dtype.itemsize for a in list(args) + list(outs)]
    sizes += [int(np.prod(a.shape)) * 4 for a in scratch if a.memory_space == pltpu.VMEM]
    return pl.pallas_call(
        body,
        out_shape=tuple(outs),
        in_specs=[vm] * len(args),
        out_specs=(vm,) * len(outs),
        scratch_shapes=scratch,
        compiler_params=pltpu.CompilerParams(vmem_limit_bytes=sum(sizes) + (12 << 20)),
    )(*args)


def shards(raw, shifts, weight, offset, log_var, goal):
    nf = lax.axis_size("frame")
    n_space = lax.axis_size("space")
    fl, band_rows, W = raw.shape
    T = shifts.shape[3]
    channels, _, ws = goal.shape
    G = W // LANES
    F = nf * fl
    nsc = ws // LANES
    inv_pixels = 1.0 / (band_rows * n_space * W // 4)
    rows_out = max(G, 8)

    def from_frame(value, j):
        return lax.ppermute(value, "frame", [(i, (i - j) % nf) for i in range(nf)])

    def pieces(value):
        return [value] + [from_frame(value, j) for j in range(1, nf)]

    raws = pieces(raw)
    goals = pieces(goal)
    shift_parts = pieces(shifts)
    y = jnp.pad(raw, ((0, F - fl), (0, 0), (0, 0)))
    y = lax.optimization_barrier(y)
    for j in range(1, nf):
        y = lax.dynamic_update_slice(y, raws[j], (j * fl, 0, 0))
    yc = involution(y, n_space, 1, 0)
    pair = jnp.concatenate([y, yc], axis=0)
    yf = involution(pair, n_space, 1, 1)

    shape = jax.ShapeDtypeStruct
    side_rows = nf * nsc * channels + -(-2 * F // 16) * 16
    *tables, big, bigt, small, own_rows, side, edge, site_goals = call(
        functools.partial(table_kernel, (nf, fl, nsc, T)),
        [weight, log_var.reshape(2, LANES), offset.reshape(1, channels), *shift_parts, *goals],
        [
            shape((256, 256), BF16),
            shape((128, 256), BF16),
            shape((256, 256), BF16),
            shape((256, 128), BF16),
            shape((256, 256), BF16),
            shape((256, 512), BF16),
            shape((256, 512), BF16),
            shape((320, 256), BF16),
            shape((96, 320), BF16),
            shape((8, LANES), F32),
            shape((2 * F, LANES), jnp.int32),
            shape((side_rows, LANES), BF16),
            shape((nf * nsc * channels, LANES), BF16),
            shape((8, channels, W // 2), F32),
        ],
        [pltpu.VMEM((6, 40, LANES), F32), pltpu.VMEM((256, LANES), F32)],
    )
    side = involution(side, n_space, 1, 1)

    pack, pc, far, moments = call(
        functools.partial(merge_kernel, (nf, fl, G, T, nsc)),
        [own_rows, side, edge, y, yc, yf, small, *tables[:4]],
        [
            shape((G, TILE, LANES), F32),
            shape((4 * G + nf * nsc * channels, LANES), BF16),
            shape((4 * G, LANES), F32),
            shape((32 * rows_out, LANES), F32),
        ],
        [
            pltpu.VMEM((F * G, 4 * TILE, LANES), F32),
            pltpu.VMEM((2, F * G, 8, LANES), jnp.int32),
            pltpu.VMEM((2, 256, LANES), F32),
            pltpu.VMEM((2, 256, LANES), F32),
            pltpu.VMEM((20 * rows_out, LANES), F32),
            pltpu.VMEM((2 * F, LANES), jnp.int32),
            pltpu.SMEM((2 * F, LANES), jnp.int32),
            pltpu.SMEM((2 * F, LANES), jnp.int32),
            pltpu.SemaphoreType.DMA((2,)),
        ],
    )
    pc = involution(pc, n_space, 1, 0)
    (partial,) = call(
        functools.partial(demosaic_kernel, (nf, fl, G, nsc, n_space, inv_pixels)),
        [pack, pc, far, side, site_goals, moments, big, bigt, small, *tables[4:]],
        [shape((16, LANES), F32)],
        [
            pltpu.VMEM((2, channels, W // 2), F32),
            pltpu.VMEM((G, 24, LANES), F32),
            pltpu.VMEM((rows_out * TILE, LANES), F32),
            pltpu.VMEM((rows_out * TILE, LANES), F32),
            pltpu.VMEM((rows_out * TILE, LANES), F32),
        ],
    )
    merged, grad_weight, grad_bias, grad_noise = call(
        functools.partial(last_sum, nf),
        [pack, *sum_space(partial, n_space)],
        [
            shape((TILE, W // nf), F32),
            shape((channels, 36), F32),
            shape((1, channels), F32),
            shape((2, LANES), F32),
        ],
        [],
    )
    return merged, grad_weight, grad_bias.reshape(channels), grad_noise.reshape(256)


def solution(mesh):
    placed = (
        P("frame", "space", None),
        P("frame", None, "space", None),
        P(),
        P(),
        P(),
        P(None, "space", "frame"),
    )

    return jax.shard_map(
        shards,
        mesh=mesh,
        in_specs=placed,
        out_specs=(P("space", "frame"), P(), P(), P()),
        check_vma=False,
    )
```

```python
import functools
import math

import jax
import jax.numpy as jnp
import ml_dtypes
import numpy as np
from jax import lax
from jax.experimental import pallas as pl
from jax.experimental.pallas import tpu as pltpu
from jax.sharding import PartitionSpec as P


TILE = 16
LANES = 128
F32 = jnp.float32
BF16 = jnp.bfloat16


def dot(a, b, dims=((1,), (0,))):
    return lax.dot_general(a, b, (dims, ((), ())), preferred_element_type=F32)


def split(value, parts):
    terms = []
    for _ in range(parts):
        term = value.astype(BF16)
        terms.append(term)
        value = value - term.astype(F32)
    return terms


def split_table(value, parts):
    terms = []
    for _ in range(parts):
        term = float(np.float32(value).astype(ml_dtypes.bfloat16))
        terms.append(term)
        value = value - term
    return terms


def wave(phase, parts):
    near = jnp.minimum(phase, 16 - phase)
    step = jnp.minimum(near, 8 - near)
    flip = near > 4
    steps = [split_table(math.cos(2.0 * math.pi * k / 16.0), parts) for k in range(4)]
    terms = []
    for p in range(parts):
        value = jnp.zeros(phase.shape, F32)
        for k in range(4):
            value = jnp.where(step == k, float(steps[k][p]), value)
        terms.append(jnp.where(flip, -value, value))
    return terms


def waves(phase, parts):
    phase = phase & 15
    return wave(phase, parts), wave((phase + 12) & 15, parts)


def turn(re, im, k, n):
    if k == 0:
        return re, im
    if 4 * k == n:
        return im, -re
    if 8 * k == n:
        half = math.sqrt(0.5)
        return (re + im) * half, (im - re) * half
    if 8 * k == 3 * n:
        half = math.sqrt(0.5)
        return (im - re) * half, (re + im) * -half
    c, s = math.cos(2.0 * math.pi * k / n), math.sin(2.0 * math.pi * k / n)
    return re * c + im * s, im * c - re * s


def fft(re, im):
    n = len(re)
    if n == 1:
        return re, im
    er, ei = fft(re[0::2], im[0::2])
    our, oi = fft(re[1::2], im[1::2])
    half = n // 2
    xr, xi = [None] * n, [None] * n
    for k in range(half):
        tr, ti = turn(our[k], oi[k], k, n)
        xr[k], xi[k] = er[k] + tr, ei[k] + ti
        xr[k + half], xi[k + half] = er[k] - tr, ei[k] - ti
    return xr, xi


def tree(values):
    while len(values) > 1:
        half = len(values) // 2
        values = [a + b for a, b in zip(values[:half], values[half:])]
    return values[0]


def add_lists(a, b):
    return b if a is None else [x + y for x, y in zip(a, b)]


def table_kernel(dims, weight_ref, *refs):
    nf, fl, nsc, T = dims
    shift_refs, goal_refs, refs = refs[:nf], refs[nf : 2 * nf], refs[2 * nf :]
    fwd_ref, fwdl_ref, inv_ref, invl_ref, part_ref, wideh_ref, widel_ref = refs[:7]
    big_ref, bigt_ref, own_ref, side_ref, edge_ref, goal_ref, rows_ref, raw_ref = refs[7:]
    odd = lax.rem(lax.axis_index("space"), 2)
    fr = lax.axis_index("frame")
    for j in range(nf):
        for l in range(fl):
            for c in range(2):
                row = shift_refs[j][l, c]
                if T < LANES:
                    row = jnp.concatenate([row, jnp.zeros((1, LANES - T), jnp.int32)], axis=1)
                at = (j * fl + l) * 2 + c
                own_ref[at : at + 1, :] = row
    count = nf * fl * 2
    words = own_ref[...].astype(F32)
    if count % 16:
        words = jnp.concatenate([words, jnp.zeros((16 - count % 16, LANES), F32)], axis=0)
    G = side_ref.shape[2] // LANES
    blocks = [words[16 * k : 16 * k + 16] for k in range(words.shape[0] // 16)]
    for j in range(nf):
        at = pl.multiple_of(lax.rem(fr + j, nf) * (nsc * LANES), LANES)
        for c in range(nsc):
            cols = slice(c * LANES, (c + 1) * LANES)
            raw_ref[...] = goal_refs[j][:, :, cols].astype(F32).reshape(256, LANES)
            to = pl.ds(pl.multiple_of(at + c * LANES, LANES), LANES)
            for r in range(8):
                goal_ref[r, :, to] = raw_ref[pl.ds(r, 32, stride=8), :]
            rows = slice((j * nsc + c) * 32, (j * nsc + c) * 32 + 32)
            edge_ref[rows, :] = raw_ref[pl.ds(7 - 7 * odd, 32, stride=8), :].astype(BF16)
            edge = raw_ref[pl.ds(7 * odd, 32, stride=8), :]
            blocks += [edge[:16], edge[16:]]
    for k, block in enumerate(blocks):
        at = (k % G) * LANES
        side_ref[k // G, :, at : at + LANES] = block.astype(BF16)
    for k in range(len(blocks), side_ref.shape[0] * G):
        at = (k % G) * LANES
        side_ref[k // G, :, at : at + LANES] = jnp.zeros((TILE, LANES), BF16)

    lane = lax.broadcasted_iota(jnp.int32, (TILE, LANES), 1)
    line = lax.broadcasted_iota(jnp.int32, (TILE, LANES), 0)
    cos, sin = waves(line * (lane & 15), 3)
    for k in range(8):
        at = slice(k * TILE, (k + 1) * TILE)
        mid = slice(128 + k * TILE, 128 + (k + 1) * TILE)
        here = (lane // TILE) == k
        c = [jnp.where(here, v, 0.0).astype(BF16) for v in cos]
        d = [jnp.where(here, v, 0.0).astype(BF16) for v in sin]
        fwd_ref[at, :] = jnp.concatenate([c[0], d[0]], axis=1)
        fwd_ref[mid, :] = jnp.concatenate([c[1], d[1]], axis=1)
        fwdl_ref[at, :] = jnp.concatenate([c[2], d[2]], axis=1)
        inv_ref[at, :] = jnp.concatenate([c[0], c[1]], axis=1)
        inv_ref[mid, :] = jnp.concatenate([-d[0], -d[1]], axis=1)
        invl_ref[at, :] = c[2]
        invl_ref[mid, :] = -d[2]
    line = lax.broadcasted_iota(jnp.int32, (256, 256), 0)
    column = lax.broadcasted_iota(jnp.int32, (256, 256), 1)
    source = 2 * (column & 127) + (column >> 7)
    part_ref[...] = jnp.where(line == source, 1.0, 0.0).astype(BF16)
    lane8 = lax.broadcasted_iota(jnp.int32, (8, LANES), 1)
    line8 = lax.broadcasted_iota(jnp.int32, (8, LANES), 0)
    empty = jnp.zeros((8, LANES), F32)
    for q in range(2):
        cos, sin = waves((2 * line8 + q) * (lane8 & 15), 2)
        for t in range(0, 16, 2):
            for ref, c, d in ((wideh_ref, cos[0], sin[0]), (widel_ref, cos[1], sin[1])):
                rows = []
                for u in (t, t + 1):
                    here = lane8 // TILE == u % 8
                    row = []
                    for v in (c, d):
                        v = jnp.where(here, v, 0.0)
                        row += [v, empty] if u < 8 else [empty, v]
                    rows.append(jnp.concatenate(row, axis=1))
                at = q * 128 + t * 8
                ref[at : at + 16, :] = jnp.concatenate(rows, axis=0).astype(BF16)

    weight = weight_ref[...].astype(F32)
    weight = jnp.concatenate([weight, jnp.zeros((32, LANES - 36), F32)], axis=1)
    halves = []
    for h in range(2):
        at = lax.broadcasted_iota(jnp.int32, (32, LANES), 1) + h * LANES
        group = (at * 171) >> 12
        row = at - 24 * group
        q = jnp.where(group >= 3, 1, 0)
        tap = (3 * (row >> 1) + group - 3 * q) * 4 + 2 * (row & 1) + q
        valid = (row < 6) & (group < 6)
        taken = jnp.take_along_axis(weight, jnp.where(valid, tap, 0), axis=1)
        halves.append(jnp.where(valid, taken, 0.0))
    base = jnp.concatenate(halves, axis=1)
    for sy in range(10):
        moved = pltpu.roll(base, 2 * sy, 1) if sy else base
        big_ref[sy * 32 : (sy + 1) * 32, :] = moved.astype(BF16)

    turned = jnp.transpose(jnp.concatenate([weight] * 4, axis=0))
    rows_ref[...] = jnp.zeros_like(rows_ref)
    for q in range(2):
        for b in range(3):
            for j in range(6):
                tap = (3 * (j // 2) + b) * 4 + 2 * (j % 2) + q
                rows_ref[q * 3 + b, 16 + j : 17 + j, :] = turned[tap : tap + 1, :]
    quarter = lax.broadcasted_iota(jnp.int32, (TILE, LANES), 1) // 32
    for k in range(6):
        for tile in range(3):
            value = jnp.zeros((TILE, LANES), F32)
            for u in range(4):
                sy = 4 * tile + u
                if sy < 10:
                    block = rows_ref[k, 20 - 2 * sy : 36 - 2 * sy, :]
                    value = jnp.where(quarter == u, block, value)
            width = 64 if tile == 2 else LANES
            at = tile * LANES
            bigt_ref[k * TILE : (k + 1) * TILE, at : at + width] = value[:, :width].astype(BF16)


def side_block(ref, plane, k):
    per = ref.shape[2] // LANES
    at = (k % per) * LANES
    return ref[plane + k // per, :, at : at + LANES].astype(F32)


def merge_kernel(dims, *refs):
    nf, fl, G, _, _ = dims
    F = nf * fl
    own_ref, edge_ref, y_ref, yc_ref, yf_ref, var_ref = refs[:6]
    fwd_ref, fwdl_ref, inv_ref, invl_ref = refs[6:10]
    pack_ref, pc_ref, far_ref, h_ref = refs[10:14]
    x_ref, idx_ref, p_ref, q_ref, xs_ref, words_ref, own_sm, far_sm, sems = refs[14:]
    s = lax.axis_index("space")
    fr = lax.axis_index("frame")
    odd = lax.rem(s, 2)

    words = [side_block(yf_ref, 2 * F, k) for k in range(-(-2 * F // 16))]
    words_ref[...] = jnp.concatenate(words, axis=0)[: 2 * F].astype(jnp.int32)
    moves = (
        pltpu.make_async_copy(own_ref, own_sm, sems.at[0]),
        pltpu.make_async_copy(words_ref, far_sm, sems.at[1]),
    )
    for move in moves:
        move.start()

    slots = (
        (y_ref, 0, 2 - odd),
        (yc_ref, 0, 3 - 3 * odd),
        (yf_ref, 0, 1 + odd),
        (yf_ref, F, 3 * odd),
    )

    def fill(f, carry):
        for ref, start, slot in slots:
            rows = ref[start + f].astype(F32)
            for g in range(G):
                block = rows[:, g * LANES : (g + 1) * LANES]
                x_ref[f * G + g, pl.ds(pl.multiple_of(slot * TILE, TILE), TILE), :] = block
        return carry

    lax.fori_loop(0, F, fill, 0, unroll=min(F, 4))

    spot = lax.broadcasted_iota(jnp.int32, (8, LANES), 1)
    for which, ref in enumerate((own_ref, words_ref)):
        for f in range(F):
            row = jnp.broadcast_to(ref[2 * f + 1 : 2 * f + 2, :], (8, LANES))
            for g in range(G):
                moved = jnp.take_along_axis(row, 8 * g + spot // TILE, axis=1)
                idx_ref[which, f * G + g] = (moved + spot) & (LANES - 1)
    pc_ref[4 * G :, :] = edge_ref[...]

    lane = lax.broadcasted_iota(jnp.int32, (TILE, LANES), 1)
    kind = (lane // TILE) % 4
    per = 16 // G
    chunks = F * G // 16
    rows_out = max(G, 8)
    fold = TILE // rows_out
    zero = jnp.zeros((TILE, LANES), F32)

    def place(f):
        if nf == 2:
            return f
        return lax.rem(f // fl + nf - fr, nf) * fl + f % fl

    first = lax.rem(nf - fr, nf) * fl
    log_var = var_ref[...]
    variances = []
    for k in range(16):
        row = jnp.broadcast_to(log_var[k // 8 : k // 8 + 1], (8, LANES))
        row = jnp.take_along_axis(row, (k % 8) * TILE + spot % TILE, axis=1)
        variances.append(jnp.concatenate([row, row], axis=0))

    def tile_row(which, row0, dy_ref, c, carry):
        sums = carry[0] if carry is not None else None
        blocks = []
        for q in range(16):
            g = q % G
            f = place(c * per + q // G)

            def load(t, group):
                if group < 0 or group >= G:
                    return zero
                start = row0 + dy_ref[2 * f, 8 * g + t]
                return x_ref[f * G + group, pl.ds(start, TILE), :]

            idx = idx_ref[which, f * G + g]
            idx = jnp.concatenate([idx, idx], axis=0)
            mixes = (
                jnp.where(
                    lane < 40,
                    load(0, g),
                    jnp.where(lane < 104, load(4, g), load(0, g - 1)),
                ),
                jnp.where(lane < 56, load(1, g), load(5, g)),
                jnp.where(lane < 72, load(2, g), load(6, g)),
                jnp.where(
                    lane < 24,
                    load(7, g + 1),
                    jnp.where(lane < 88, load(3, g), load(7, g)),
                ),
            )
            moved = [jnp.take_along_axis(m, idx, axis=1) for m in mixes]
            blocks.append(
                jnp.where(
                    kind < 2,
                    jnp.where(kind == 0, moved[0], moved[1]),
                    jnp.where(kind == 2, moved[2], moved[3]),
                )
            )
        base = [x_ref[first * G + g, pl.ds(pl.multiple_of(row0, TILE), TILE), :] for g in range(G)]
        both = jnp.concatenate(blocks + base, axis=0).astype(BF16)
        pq = dot(jnp.concatenate([both, both], axis=1), fwd_ref[...]) + dot(both, fwdl_ref[...])
        for q in range(16):
            rows = slice(q * TILE, (q + 1) * TILE)
            ref_rows = slice(256 + (q % G) * TILE, 256 + (q % G + 1) * TILE)
            diff = pq[ref_rows] - pq[rows]
            p_ref[which, rows, :] = diff[:, :LANES]
            q_ref[which, rows, :] = -diff[:, LANES:]
        re, im = fft(
            [p_ref[which, pl.ds(n, 16, stride=16), :] for n in range(16)],
            [q_ref[which, pl.ds(n, 16, stride=16), :] for n in range(16)],
        )
        out = [[], [], [], []]
        for k in range(16):
            energy = re[k] * re[k] + im[k] * im[k]
            weight = energy / (energy + variances[k])
            wr = weight * re[k]
            wi = weight * im[k]
            vals = (wr, wi)
            if which == 0:
                rest = 1.0 - weight
                vals = (wr, wi, wr * rest, wi * rest)
            for store, val in zip(out, vals):
                if fold == 2:
                    val = val[:8] + val[8:]
                store.append(val)
        flat = out[0] + out[1] + out[2] + out[3]
        return sums_of(sums, blocks), add_lists(carry[1] if carry is not None else None, flat)

    def sums_of(sums, blocks):
        return add_lists(sums, [tree(blocks[g::G]) for g in range(G)])

    def whole_row(which, row0, dy_ref):
        step = functools.partial(tile_row, which, row0, dy_ref)
        carry = step(0, None)
        if chunks > 1:
            carry = lax.fori_loop(1, chunks, step, carry)
        return carry

    moves[0].wait()
    sums, flat = whole_row(0, (2 - odd) * TILE, own_sm)
    for k in range(32):
        h_ref[k * rows_out : (k + 1) * rows_out, :] = flat[32 + k]
    moves[1].wait()
    far_sums, far_flat = whole_row(1, (1 + odd) * TILE, far_sm)

    vi, ur = fft(flat[16:32], flat[:16])
    far_vi, far_ur = fft(far_flat[16:32], far_flat[:16])
    at_odd = odd == 1
    ur += [jnp.where(at_odd, far_ur[k], far_ur[12 + k]) for k in range(4)]
    vi += [jnp.where(at_odd, far_vi[k], far_vi[12 + k]) for k in range(4)]
    uv = jnp.concatenate([jnp.concatenate(ur, axis=0), jnp.concatenate(vi, axis=0)], axis=1)
    m = 20 * rows_out
    terms = split(uv, 3)
    wide = dot(jnp.concatenate(terms, axis=0), inv_ref[...])
    pix = wide[:m, :LANES] + (wide[m : 2 * m, :LANES] + wide[:m, LANES:])
    pix = pix + (wide[2 * m :, :LANES] + wide[m : 2 * m, LANES:] + dot(terms[0], invl_ref[...]))
    xs_ref[...] = pix
    far_rows = []
    for g in range(G):
        val = xs_ref[pl.ds(g, 16, stride=rows_out), :]
        far = xs_ref[pl.ds(16 * rows_out + g, 4, stride=rows_out), :]
        for other in range(g + G, rows_out, G):
            val = val + xs_ref[pl.ds(other, 16, stride=rows_out), :]
            far = far + xs_ref[pl.ds(16 * rows_out + other, 4, stride=rows_out), :]
        pack_ref[g] = (sums[g] + val / 256.0) / F
        far_sum = jnp.where(at_odd, far_sums[g][0:4], far_sums[g][12:16])
        far_rows.append((far_sum + far / 256.0) / F)
    far_ref[...] = jnp.concatenate(far_rows, axis=0)
    low = jnp.concatenate([pack_ref[g, 0:4, :] for g in range(G)], axis=0)
    high = jnp.concatenate([pack_ref[g, 12:16, :] for g in range(G)], axis=0)
    pc_ref[0 : 4 * G, :] = jnp.where(at_odd, low, high).astype(BF16)


def demosaic_kernel(dims, pack_ref, pc_ref, far_ref, yf_ref, goals_ref, h_ref, *refs):
    nf, fl, G, nsc, n_space, inv_pixels = dims
    F = nf * fl
    W = G * LANES
    half = W // 2
    big_ref, bigt_ref, offs_ref, part_ref, wideh_ref, widel_ref = refs[:6]
    out_ref, goal_ref, mm_ref, p_ref, q_ref, ns_ref = refs[6:]
    s = lax.axis_index("space")
    fr = lax.axis_index("frame")
    odd = lax.rem(s, 2)
    rows_out = max(G, 8)

    lead = G * 4
    for j in range(nf):
        at = pl.multiple_of(lax.rem(fr + j, nf) * (nsc * LANES), LANES)
        for c in range(nsc):
            first = (j * nsc + c) * 32
            to = pl.ds(pl.multiple_of(at + c * LANES, LANES), LANES)
            goal_ref[1 - odd, :, to] = pc_ref[lead + first : lead + first + 32, :].astype(F32)
            block = -(-2 * F // 16) + 2 * (j * nsc + c)
            goal_ref[odd, :, to] = jnp.concatenate(
                [side_block(yf_ref, 2 * F, block), side_block(yf_ref, 2 * F, block + 1)], axis=0
            )

    near = pc_ref[0:lead, :].astype(F32)
    far = far_ref[...]
    low = jnp.where(odd == 1, near, far)
    high = jnp.where(odd == 1, far, near)
    for g in range(G):
        mm_ref[g, 0:4, :] = low[4 * g : 4 * g + 4]
        mm_ref[g, 4:20, :] = pack_ref[g]
        mm_ref[g, 20:24, :] = high[4 * g : 4 * g + 4]
    pairs = jnp.concatenate(
        [jnp.concatenate([mm_ref[2 * h], mm_ref[2 * h + 1]], axis=1) for h in range(G // 2)],
        axis=0,
    )
    parted = dot(pairs.astype(BF16), part_ref[...])
    site = lax.broadcasted_iota(jnp.int32, (24, half), 1)
    pieces = []
    for q in range(2):
        plane = jnp.concatenate(
            [parted[24 * h : 24 * h + 24, q * 128 : (q + 1) * 128] for h in range(G // 2)], axis=1
        )
        pieces.append(jnp.where(site == 0, 0.0, pltpu.roll(plane, 1, 1)))
        pieces.append(plane)
        pieces.append(jnp.where(site == half - 1, 0.0, pltpu.roll(plane, half - 1, 1)))
    pieces.append(jnp.zeros((112, half), F32))
    taps = jnp.concatenate(pieces, axis=0).astype(BF16)

    preact = dot(big_ref[...], taps)
    diag = lax.broadcasted_iota(jnp.int32, (32, LANES), 0) == lax.broadcasted_iota(
        jnp.int32, (32, LANES), 1
    )
    offs = jnp.where(diag, jnp.broadcast_to(offs_ref[2:3, :], (32, LANES)), 0.0)
    offs = jnp.broadcast_to(jnp.sum(offs, axis=1, keepdims=True), (32, half))
    bias = jnp.zeros((32, half), F32)
    slopes = []
    for sy in range(10):
        v = preact[sy * 32 : sy * 32 + 32] + offs
        sig = jax.nn.sigmoid(v)
        goal = goal_ref[0] if sy == 0 else goal_ref[1] if sy == 9 else goals_ref[sy - 1]
        slope = (v * sig - goal) * inv_pixels * (sig * (1.0 + v * (1.0 - sig)))
        if sy == 0:
            slope = jnp.where(s == 0, 0.0, slope)
        elif sy == 9:
            slope = jnp.where(s == n_space - 1, 0.0, slope)
        else:
            bias = bias + slope
        slopes.append(slope)
    slope_bf = jnp.concatenate(slopes, axis=0).astype(BF16)

    gt = dot(bigt_ref[...], slope_bf)
    site16 = lax.broadcasted_iota(jnp.int32, (TILE, half), 1)
    planes = []
    for q in range(2):
        left, mid, right = (gt[(q * 3 + b) * 16 : (q * 3 + b) * 16 + 16] for b in range(3))
        planes.append(
            mid
            + jnp.where(site16 == half - 1, 0.0, pltpu.roll(left, half - 1, 1))
            + jnp.where(site16 == 0, 0.0, pltpu.roll(right, 1, 1))
        )
    grad = jnp.concatenate(
        [
            jnp.concatenate([p[:, h * 128 : (h + 1) * 128] for p in planes], axis=1)
            for h in range(G // 2)
        ],
        axis=0,
    )
    m = grad.shape[0]
    terms = split(grad, 2)
    pq = dot(jnp.concatenate(terms, axis=0), wideh_ref[...])
    pq = pq[:m] + (pq[m:] + dot(terms[0], widel_ref[...]))
    for r in range(rows_out):
        g = r % G
        rows = slice((g // 2) * TILE, (g // 2 + 1) * TILE)
        c0 = (g % 2) * LANES
        p_ref[r * TILE : (r + 1) * TILE, :] = pq[rows, c0 : c0 + LANES]
        q_ref[r * TILE : (r + 1) * TILE, :] = -pq[rows, 256 + c0 : 256 + c0 + LANES]
    gre, gim = fft(
        [p_ref[pl.ds(n, rows_out, stride=16), :] for n in range(16)],
        [q_ref[pl.ds(n, rows_out, stride=16), :] for n in range(16)],
    )
    for k in range(16):
        rows = slice(k * rows_out, (k + 1) * rows_out)
        rows_im = slice((16 + k) * rows_out, (17 + k) * rows_out)
        ns_ref[rows, :] = gre[k] * h_ref[rows, :] + gim[k] * h_ref[rows_im, :]
    noise = ns_ref[pl.ds(0, 16, stride=rows_out), :]
    for r in range(1, rows_out):
        noise = noise + ns_ref[pl.ds(r, 16, stride=rows_out), :]
    noise = noise * (-1.0 / (256.0 * F))
    for step in (64, 32, 16):
        noise = noise + pltpu.roll(noise, step, 1)

    prod = dot(slope_bf[32:288], taps, ((1,), (1,)))
    gw = jnp.zeros((32, 256), F32)
    for sy in range(1, 9):
        gw = gw + pltpu.roll(prod[(sy - 1) * 32 : sy * 32], 256 - 2 * sy, 1)
    tap = lax.broadcasted_iota(jnp.int32, (32, LANES), 1)
    pair = tap >> 2
    a = (pair * 11) >> 5
    source = ((tap & 1) * 3 + pair - 3 * a) * 24 + 2 * a + ((tap >> 1) & 1)
    source = jnp.where(tap < 36, source, 0)
    lower_part = jnp.take_along_axis(gw[:, :LANES], source & 127, axis=1)
    upper_part = jnp.take_along_axis(gw[:, LANES:], source & 127, axis=1)
    gw = jnp.where(source < LANES, lower_part, upper_part)
    gw = jnp.where(tap == 36, jnp.sum(bias, axis=1, keepdims=True), gw)
    gw = jnp.where(tap < 37, gw, 0.0)
    first = gw[0:8] + (pltpu.roll(gw[8:16], 37, 1) + pltpu.roll(gw[16:24], 74, 1))
    group = lax.broadcasted_iota(jnp.int32, (8, LANES), 1) // TILE
    second = jnp.where(group == 5, noise[:8], jnp.where(group == 6, noise[8:], gw[24:32]))
    out_ref[...] = jnp.concatenate([first, second], axis=0)


def last_sum(nf, pack_ref, own_ref, got_ref, merged_ref, weight_ref, bias_ref, noise_ref):
    own = pack_ref.shape[0] // nf
    fr = lax.axis_index("frame")
    for k in range(own):
        merged_ref[:, k * LANES : (k + 1) * LANES] = pack_ref[fr * own + k]
    total = own_ref[...] + got_ref[...]
    first, second = total[:8], total[8:]
    gw = jnp.concatenate(
        [first, pltpu.roll(first, LANES - 37, 1), pltpu.roll(first, LANES - 74, 1), second], axis=0
    )
    weight_ref[...] = gw[:, :36]
    line = lax.broadcasted_iota(jnp.int32, (32, LANES), 0)
    lane = lax.broadcasted_iota(jnp.int32, (32, LANES), 1)
    bias = jnp.where(line == lane, jnp.broadcast_to(gw[:, 36:37], (32, LANES)), 0.0)
    bias_ref[...] = jnp.sum(bias, axis=0, keepdims=True)[:, :32]
    group = lane[:8] // TILE
    for k in range(2):
        part = jnp.where(group == 5 + k, second, 0.0)
        for step in (16, 32, 64):
            part = part + pltpu.roll(part, step, 1)
        part = jnp.where(group == line[:8], part, 0.0)
        noise_ref[k : k + 1, :] = jnp.sum(part, axis=0, keepdims=True)


def involution(value, count, step, first):
    pairs = []
    for i in range(first, count):
        j = ((i - first) ^ step) + first
        if j < count:
            pairs.append((i, j))
    return lax.ppermute(value, "space", pairs)


def sum_space(value, count):
    bits = count.bit_length() - 1
    assert 1 << bits == count
    stages = []
    at = 0
    while at < bits:
        width = 2 if at == 1 and bits - at >= 3 else 1
        stages.append([m << at for m in range(1, 1 << width)])
        at += width
    for masks in stages[:-1]:
        got = []
        for m in masks:
            got.append(lax.ppermute(value, "space", [(i, i ^ m) for i in range(count)]))
        value = value + got[0]
        if len(got) == 3:
            value = value + (got[1] + got[2])
    (mask,) = stages[-1]
    got = lax.ppermute(value, "space", [(i, i ^ mask) for i in range(count)])
    return value, got


def call(body, args, outs, scratch):
    vm = pl.BlockSpec(memory_space=pltpu.VMEM)
    sizes = [int(np.prod(a.shape)) * a.dtype.itemsize for a in list(args) + list(outs)]
    sizes += [int(np.prod(a.shape)) * 4 for a in scratch if a.memory_space == pltpu.VMEM]
    return pl.pallas_call(
        body,
        out_shape=tuple(outs),
        in_specs=[vm] * len(args),
        out_specs=(vm,) * len(outs),
        scratch_shapes=scratch,
        compiler_params=pltpu.CompilerParams(vmem_limit_bytes=sum(sizes) + (12 << 20)),
    )(*args)


def shards(raw, shifts, weight, offset, log_var, goal):
    nf = lax.axis_size("frame")
    n_space = lax.axis_size("space")
    fl, band_rows, W = raw.shape
    T = shifts.shape[3]
    channels, _, ws = goal.shape
    G = W // LANES
    F = nf * fl
    nsc = ws // LANES
    inv_pixels = 1.0 / (band_rows * n_space * W // 4)
    rows_out = max(G, 8)

    def from_frame(value, j):
        return lax.ppermute(value, "frame", [(i, (i - j) % nf) for i in range(nf)])

    def pieces(value):
        return [value] + [from_frame(value, j) for j in range(1, nf)]

    raws = pieces(raw)
    goals = pieces(goal)
    shift_parts = pieces(shifts)
    y = jnp.pad(raw, ((0, F - fl), (0, 0), (0, 0)))
    y = lax.optimization_barrier(y)
    for j in range(1, nf):
        y = lax.dynamic_update_slice(y, raws[j], (j * fl, 0, 0))
    yc = involution(y, n_space, 1, 0)
    shape = jax.ShapeDtypeStruct
    planes = -(-(2 * nf * nsc + -(-2 * F // 16)) // G)
    *tables, big, bigt, own_rows, side, edge, site_goals = call(
        functools.partial(table_kernel, (nf, fl, nsc, T)),
        [weight, *shift_parts, *goals],
        [
            shape((256, 256), BF16),
            shape((128, 256), BF16),
            shape((256, 256), BF16),
            shape((256, 128), BF16),
            shape((256, 256), BF16),
            shape((256, 512), BF16),
            shape((256, 512), BF16),
            shape((320, 256), BF16),
            shape((96, 320), BF16),
            shape((2 * F, LANES), jnp.int32),
            shape((planes, TILE, W), BF16),
            shape((nf * nsc * channels, LANES), BF16),
            shape((8, channels, W // 2), F32),
        ],
        [pltpu.VMEM((6, 40, LANES), F32), pltpu.VMEM((256, LANES), F32)],
    )
    pair = jnp.concatenate([y, yc, side], axis=0)
    yf = involution(pair, n_space, 1, 1)
    small = jnp.concatenate(
        [jnp.exp(log_var), offset, jnp.zeros((6 * LANES - channels,), F32)]
    ).reshape(8, LANES)

    pack, pc, far, moments = call(
        functools.partial(merge_kernel, (nf, fl, G, T, nsc)),
        [own_rows, edge, y, yc, yf, small, *tables[:4]],
        [
            shape((G, TILE, LANES), F32),
            shape((4 * G + nf * nsc * channels, LANES), BF16),
            shape((4 * G, LANES), F32),
            shape((32 * rows_out, LANES), F32),
        ],
        [
            pltpu.VMEM((F * G, 4 * TILE, LANES), F32),
            pltpu.VMEM((2, F * G, 8, LANES), jnp.int32),
            pltpu.VMEM((2, 256, LANES), F32),
            pltpu.VMEM((2, 256, LANES), F32),
            pltpu.VMEM((20 * rows_out, LANES), F32),
            pltpu.VMEM((2 * F, LANES), jnp.int32),
            pltpu.SMEM((2 * F, LANES), jnp.int32),
            pltpu.SMEM((2 * F, LANES), jnp.int32),
            pltpu.SemaphoreType.DMA((2,)),
        ],
    )
    pc = involution(pc, n_space, 1, 0)
    (partial,) = call(
        functools.partial(demosaic_kernel, (nf, fl, G, nsc, n_space, inv_pixels)),
        [pack, pc, far, yf, site_goals, moments, big, bigt, small, *tables[4:]],
        [shape((16, LANES), F32)],
        [
            pltpu.VMEM((2, channels, W // 2), F32),
            pltpu.VMEM((G, 24, LANES), F32),
            pltpu.VMEM((rows_out * TILE, LANES), F32),
            pltpu.VMEM((rows_out * TILE, LANES), F32),
            pltpu.VMEM((rows_out * TILE, LANES), F32),
        ],
    )
    merged, grad_weight, grad_bias, grad_noise = call(
        functools.partial(last_sum, nf),
        [pack, *sum_space(partial, n_space)],
        [
            shape((TILE, W // nf), F32),
            shape((channels, 36), F32),
            shape((1, channels), F32),
            shape((2, LANES), F32),
        ],
        [],
    )
    return merged, grad_weight, grad_bias.reshape(channels), grad_noise.reshape(256)


def solution(mesh):
    placed = (
        P("frame", "space", None),
        P("frame", None, "space", None),
        P(),
        P(),
        P(),
        P(None, "space", "frame"),
    )

    return jax.shard_map(
        shards,
        mesh=mesh,
        in_specs=placed,
        out_specs=(P("space", "frame"), P(), P(), P()),
        check_vma=False,
    )
```

```python
import functools
import math

import jax
import jax.numpy as jnp
import ml_dtypes
import numpy as np
from jax import lax
from jax.experimental import pallas as pl
from jax.experimental.pallas import tpu as pltpu
from jax.sharding import PartitionSpec as P


TILE = 16
LANES = 128
F32 = jnp.float32
BF16 = jnp.bfloat16


def dot(a, b, dims=((1,), (0,))):
    return lax.dot_general(a, b, (dims, ((), ())), preferred_element_type=F32)


def split(value, parts):
    terms = []
    for _ in range(parts):
        term = value.astype(BF16)
        terms.append(term)
        value = value - term.astype(F32)
    return terms


def split_table(value, parts):
    terms = []
    for _ in range(parts):
        term = float(np.float32(value).astype(ml_dtypes.bfloat16))
        terms.append(term)
        value = value - term
    return terms


def wave(phase, parts):
    near = jnp.minimum(phase, 16 - phase)
    step = jnp.minimum(near, 8 - near)
    flip = near > 4
    steps = [split_table(math.cos(2.0 * math.pi * k / 16.0), parts) for k in range(4)]
    terms = []
    for p in range(parts):
        value = jnp.zeros(phase.shape, F32)
        for k in range(4):
            value = jnp.where(step == k, float(steps[k][p]), value)
        terms.append(jnp.where(flip, -value, value))
    return terms


def waves(phase, parts):
    phase = phase & 15
    return wave(phase, parts), wave((phase + 12) & 15, parts)


def turn(re, im, k, n):
    if k == 0:
        return re, im
    if 4 * k == n:
        return im, -re
    if 8 * k == n:
        half = math.sqrt(0.5)
        return (re + im) * half, (im - re) * half
    if 8 * k == 3 * n:
        half = math.sqrt(0.5)
        return (im - re) * half, (re + im) * -half
    c, s = math.cos(2.0 * math.pi * k / n), math.sin(2.0 * math.pi * k / n)
    return re * c + im * s, im * c - re * s


def fft(re, im):
    n = len(re)
    if n == 1:
        return re, im
    er, ei = fft(re[0::2], im[0::2])
    our, oi = fft(re[1::2], im[1::2])
    half = n // 2
    xr, xi = [None] * n, [None] * n
    for k in range(half):
        tr, ti = turn(our[k], oi[k], k, n)
        xr[k], xi[k] = er[k] + tr, ei[k] + ti
        xr[k + half], xi[k + half] = er[k] - tr, ei[k] - ti
    return xr, xi


def tree(values):
    while len(values) > 1:
        half = len(values) // 2
        values = [a + b for a, b in zip(values[:half], values[half:])]
    return values[0]


def add_lists(a, b):
    return b if a is None else [x + y for x, y in zip(a, b)]


def side_kernel(dims, shift_ref, goal_ref, side_ref, raw_ref, words_ref):
    fl, nsc, T = dims
    odd = lax.rem(lax.axis_index("space"), 2)
    G = side_ref.shape[2] // LANES
    for l in range(fl):
        for c in range(2):
            row = shift_ref[l, c]
            if T < LANES:
                row = jnp.concatenate([row, jnp.zeros((1, LANES - T), jnp.int32)], axis=1)
            words_ref[l * 2 + c : l * 2 + c + 1, :] = row
    far, core = [], []
    for c in range(nsc):
        raw_ref[...] = goal_ref[:, :, c * LANES : (c + 1) * LANES].astype(F32).reshape(256, LANES)
        edge = raw_ref[pl.ds(7 * odd, 32, stride=8), :]
        far += [edge[:16], edge[16:]]
        edge = raw_ref[pl.ds(7 - 7 * odd, 32, stride=8), :]
        core += [edge[:16], edge[16:]]
    words = words_ref[...].astype(F32)
    blocks = far + [words[16 * k : 16 * k + 16] for k in range(words.shape[0] // 16)]
    blocks += [jnp.zeros((TILE, LANES), F32)] * (-len(blocks) % G)
    blocks += core
    blocks += [jnp.zeros((TILE, LANES), F32)] * (-len(blocks) % G)
    for k, block in enumerate(blocks):
        at = (k % G) * LANES
        side_ref[k // G, :, at : at + LANES] = block.astype(BF16)


def target_kernel(dims, *refs):
    nf, nsc = dims
    goal_refs, goal_ref, raw_ref = refs[:nf], refs[nf], refs[nf + 1]
    fr = lax.axis_index("frame")
    for j in range(nf):
        at = pl.multiple_of(lax.rem(fr + j, nf) * (nsc * LANES), LANES)
        for c in range(nsc):
            cols = slice(c * LANES, (c + 1) * LANES)
            raw_ref[...] = goal_refs[j][:, :, cols].astype(F32).reshape(256, LANES)
            to = pl.ds(pl.multiple_of(at + c * LANES, LANES), LANES)
            for r in range(8):
                goal_ref[r, :, to] = raw_ref[pl.ds(r, 32, stride=8), :]


def table_kernel(weight_ref, *refs):
    fwd_ref, fwdl_ref, inv_ref, invl_ref, part_ref, wideh_ref, widel_ref = refs[:7]
    big_ref, bigt_ref, rows_ref = refs[7:]
    lane = lax.broadcasted_iota(jnp.int32, (TILE, LANES), 1)
    line = lax.broadcasted_iota(jnp.int32, (TILE, LANES), 0)
    cos, sin = waves(line * (lane & 15), 3)
    for k in range(8):
        at = slice(k * TILE, (k + 1) * TILE)
        mid = slice(128 + k * TILE, 128 + (k + 1) * TILE)
        here = (lane // TILE) == k
        c = [jnp.where(here, v, 0.0).astype(BF16) for v in cos]
        d = [jnp.where(here, v, 0.0).astype(BF16) for v in sin]
        fwd_ref[at, :] = jnp.concatenate([c[0], d[0]], axis=1)
        fwd_ref[mid, :] = jnp.concatenate([c[1], d[1]], axis=1)
        fwdl_ref[at, :] = jnp.concatenate([c[2], d[2]], axis=1)
        inv_ref[at, :] = jnp.concatenate([c[0], c[1]], axis=1)
        inv_ref[mid, :] = jnp.concatenate([-d[0], -d[1]], axis=1)
        invl_ref[at, :] = c[2]
        invl_ref[mid, :] = -d[2]
    line = lax.broadcasted_iota(jnp.int32, (256, 256), 0)
    column = lax.broadcasted_iota(jnp.int32, (256, 256), 1)
    source = 2 * (column & 127) + (column >> 7)
    part_ref[...] = jnp.where(line == source, 1.0, 0.0).astype(BF16)
    lane8 = lax.broadcasted_iota(jnp.int32, (8, LANES), 1)
    line8 = lax.broadcasted_iota(jnp.int32, (8, LANES), 0)
    empty = jnp.zeros((8, LANES), F32)
    for q in range(2):
        cos, sin = waves((2 * line8 + q) * (lane8 & 15), 2)
        for t in range(0, 16, 2):
            for ref, c, d in ((wideh_ref, cos[0], sin[0]), (widel_ref, cos[1], sin[1])):
                rows = []
                for u in (t, t + 1):
                    here = lane8 // TILE == u % 8
                    row = []
                    for v in (c, d):
                        v = jnp.where(here, v, 0.0)
                        row += [v, empty] if u < 8 else [empty, v]
                    rows.append(jnp.concatenate(row, axis=1))
                at = q * 128 + t * 8
                ref[at : at + 16, :] = jnp.concatenate(rows, axis=0).astype(BF16)

    weight = weight_ref[...].astype(F32)
    weight = jnp.concatenate([weight, jnp.zeros((32, LANES - 36), F32)], axis=1)
    halves = []
    for h in range(2):
        at = lax.broadcasted_iota(jnp.int32, (32, LANES), 1) + h * LANES
        group = (at * 171) >> 12
        row = at - 24 * group
        q = jnp.where(group >= 3, 1, 0)
        tap = (3 * (row >> 1) + group - 3 * q) * 4 + 2 * (row & 1) + q
        valid = (row < 6) & (group < 6)
        taken = jnp.take_along_axis(weight, jnp.where(valid, tap, 0), axis=1)
        halves.append(jnp.where(valid, taken, 0.0))
    base = jnp.concatenate(halves, axis=1)
    for sy in range(10):
        moved = pltpu.roll(base, 2 * sy, 1) if sy else base
        big_ref[sy * 32 : (sy + 1) * 32, :] = moved.astype(BF16)

    turned = jnp.transpose(jnp.concatenate([weight] * 4, axis=0))
    rows_ref[...] = jnp.zeros_like(rows_ref)
    for q in range(2):
        for b in range(3):
            for j in range(6):
                tap = (3 * (j // 2) + b) * 4 + 2 * (j % 2) + q
                rows_ref[q * 3 + b, 16 + j : 17 + j, :] = turned[tap : tap + 1, :]
    quarter = lax.broadcasted_iota(jnp.int32, (TILE, LANES), 1) // 32
    for k in range(6):
        for tile in range(3):
            value = jnp.zeros((TILE, LANES), F32)
            for u in range(4):
                sy = 4 * tile + u
                if sy < 10:
                    block = rows_ref[k, 20 - 2 * sy : 36 - 2 * sy, :]
                    value = jnp.where(quarter == u, block, value)
            width = 64 if tile == 2 else LANES
            at = tile * LANES
            bigt_ref[k * TILE : (k + 1) * TILE, at : at + width] = value[:, :width].astype(BF16)


def side_block(ref, plane, k):
    per = ref.shape[2] // LANES
    at = (k % per) * LANES
    return ref[plane + k // per, :, at : at + LANES].astype(F32)


def merge_kernel(dims, *refs):
    nf, fl, G, _, nsc = dims
    F = nf * fl
    near_refs, far_refs, refs = refs[:nf], refs[nf : 2 * nf], refs[2 * nf :]
    var_ref, fwd_ref, fwdl_ref, inv_ref, invl_ref = refs[:5]
    pack_ref, pc_ref, far_ref, h_ref = refs[5:9]
    x_ref, idx_ref, p_ref, q_ref, xs_ref, own_ref, words_ref, own_sm, far_sm, sems = refs[9:]
    s = lax.axis_index("space")
    fr = lax.axis_index("frame")
    odd = lax.rem(s, 2)

    wb = -(-2 * fl // 16)
    for group, ref in ((near_refs, own_ref), (far_refs, words_ref)):
        for j in range(nf):
            words = [side_block(group[j], 2 * fl, 2 * nsc + k) for k in range(wb)]
            words = jnp.concatenate(words, axis=0)[: 2 * fl].astype(jnp.int32)
            ref[2 * fl * j : 2 * fl * (j + 1), :] = words
    moves = (
        pltpu.make_async_copy(own_ref, own_sm, sems.at[0]),
        pltpu.make_async_copy(words_ref, far_sm, sems.at[1]),
    )
    for move in moves:
        move.start()

    slots = (
        (near_refs, 0, 2 - odd),
        (near_refs, fl, 3 - 3 * odd),
        (far_refs, 0, 1 + odd),
        (far_refs, fl, 3 * odd),
    )
    for group, start, slot in slots:
        for j in range(nf):
            for l in range(fl):
                rows = group[j][start + l].astype(F32)
                for g in range(G):
                    block = rows[:, g * LANES : (g + 1) * LANES]
                    at = pl.ds(pl.multiple_of(slot * TILE, TILE), TILE)
                    x_ref[(j * fl + l) * G + g, at, :] = block

    spot = lax.broadcasted_iota(jnp.int32, (8, LANES), 1)
    for which, ref in enumerate((own_ref, words_ref)):
        for f in range(F):
            row = jnp.broadcast_to(ref[2 * f + 1 : 2 * f + 2, :], (8, LANES))
            for g in range(G):
                moved = jnp.take_along_axis(row, 8 * g + spot // TILE, axis=1)
                idx_ref[which, f * G + g] = (moved + spot) & (LANES - 1)
    first_core = -(-(2 * nsc + wb) // G) * G
    for j in range(nf):
        for k in range(2 * nsc):
            at = 4 * G + (j * 2 * nsc + k) * TILE
            block = side_block(near_refs[j], 2 * fl, first_core + k)
            pc_ref[at : at + TILE, :] = block.astype(BF16)

    lane = lax.broadcasted_iota(jnp.int32, (TILE, LANES), 1)
    kind = (lane // TILE) % 4
    per = 16 // G
    chunks = F * G // 16
    rows_out = max(G, 8)
    fold = TILE // rows_out
    zero = jnp.zeros((TILE, LANES), F32)

    def place(f):
        if nf == 2:
            return f
        return lax.rem(f // fl + nf - fr, nf) * fl + f % fl

    first = lax.rem(nf - fr, nf) * fl
    log_var = var_ref[...]
    variances = []
    for k in range(16):
        row = jnp.broadcast_to(log_var[k // 8 : k // 8 + 1], (8, LANES))
        row = jnp.take_along_axis(row, (k % 8) * TILE + spot % TILE, axis=1)
        variances.append(jnp.concatenate([row, row], axis=0))

    def tile_row(which, row0, dy_ref, c, carry):
        sums = carry[0] if carry is not None else None
        blocks = []
        for q in range(16):
            g = q % G
            f = place(c * per + q // G)

            def load(t, group):
                if group < 0 or group >= G:
                    return zero
                start = row0 + dy_ref[2 * f, 8 * g + t]
                return x_ref[f * G + group, pl.ds(start, TILE), :]

            idx = idx_ref[which, f * G + g]
            idx = jnp.concatenate([idx, idx], axis=0)
            mixes = (
                jnp.where(
                    lane < 40,
                    load(0, g),
                    jnp.where(lane < 104, load(4, g), load(0, g - 1)),
                ),
                jnp.where(lane < 56, load(1, g), load(5, g)),
                jnp.where(lane < 72, load(2, g), load(6, g)),
                jnp.where(
                    lane < 24,
                    load(7, g + 1),
                    jnp.where(lane < 88, load(3, g), load(7, g)),
                ),
            )
            moved = [jnp.take_along_axis(m, idx, axis=1) for m in mixes]
            blocks.append(
                jnp.where(
                    kind < 2,
                    jnp.where(kind == 0, moved[0], moved[1]),
                    jnp.where(kind == 2, moved[2], moved[3]),
                )
            )
        base = [x_ref[first * G + g, pl.ds(pl.multiple_of(row0, TILE), TILE), :] for g in range(G)]
        both = jnp.concatenate(blocks + base, axis=0).astype(BF16)
        pq = dot(jnp.concatenate([both, both], axis=1), fwd_ref[...]) + dot(both, fwdl_ref[...])
        for q in range(16):
            rows = slice(q * TILE, (q + 1) * TILE)
            ref_rows = slice(256 + (q % G) * TILE, 256 + (q % G + 1) * TILE)
            diff = pq[ref_rows] - pq[rows]
            p_ref[which, rows, :] = diff[:, :LANES]
            q_ref[which, rows, :] = -diff[:, LANES:]
        re, im = fft(
            [p_ref[which, pl.ds(n, 16, stride=16), :] for n in range(16)],
            [q_ref[which, pl.ds(n, 16, stride=16), :] for n in range(16)],
        )
        out = [[], [], [], []]
        for k in range(16):
            energy = re[k] * re[k] + im[k] * im[k]
            weight = energy / (energy + variances[k])
            wr = weight * re[k]
            wi = weight * im[k]
            vals = (wr, wi)
            if which == 0:
                rest = 1.0 - weight
                vals = (wr, wi, wr * rest, wi * rest)
            for store, val in zip(out, vals):
                if fold == 2:
                    val = val[:8] + val[8:]
                store.append(val)
        flat = out[0] + out[1] + out[2] + out[3]
        return sums_of(sums, blocks), add_lists(carry[1] if carry is not None else None, flat)

    def sums_of(sums, blocks):
        return add_lists(sums, [tree(blocks[g::G]) for g in range(G)])

    def whole_row(which, row0, dy_ref):
        step = functools.partial(tile_row, which, row0, dy_ref)
        carry = step(0, None)
        if chunks > 1:
            carry = lax.fori_loop(1, chunks, step, carry)
        return carry

    moves[0].wait()
    sums, flat = whole_row(0, (2 - odd) * TILE, own_sm)
    for k in range(32):
        h_ref[k * rows_out : (k + 1) * rows_out, :] = flat[32 + k]
    moves[1].wait()
    far_sums, far_flat = whole_row(1, (1 + odd) * TILE, far_sm)

    vi, ur = fft(flat[16:32], flat[:16])
    far_vi, far_ur = fft(far_flat[16:32], far_flat[:16])
    at_odd = odd == 1
    ur += [jnp.where(at_odd, far_ur[k], far_ur[12 + k]) for k in range(4)]
    vi += [jnp.where(at_odd, far_vi[k], far_vi[12 + k]) for k in range(4)]
    uv = jnp.concatenate([jnp.concatenate(ur, axis=0), jnp.concatenate(vi, axis=0)], axis=1)
    m = 20 * rows_out
    terms = split(uv, 3)
    wide = dot(jnp.concatenate(terms, axis=0), inv_ref[...])
    pix = wide[:m, :LANES] + (wide[m : 2 * m, :LANES] + wide[:m, LANES:])
    pix = pix + (wide[2 * m :, :LANES] + wide[m : 2 * m, LANES:] + dot(terms[0], invl_ref[...]))
    xs_ref[...] = pix
    far_rows = []
    for g in range(G):
        val = xs_ref[pl.ds(g, 16, stride=rows_out), :]
        far = xs_ref[pl.ds(16 * rows_out + g, 4, stride=rows_out), :]
        for other in range(g + G, rows_out, G):
            val = val + xs_ref[pl.ds(other, 16, stride=rows_out), :]
            far = far + xs_ref[pl.ds(16 * rows_out + other, 4, stride=rows_out), :]
        pack_ref[g] = (sums[g] + val / 256.0) / F
        far_sum = jnp.where(at_odd, far_sums[g][0:4], far_sums[g][12:16])
        far_rows.append((far_sum + far / 256.0) / F)
    far_ref[...] = jnp.concatenate(far_rows, axis=0)
    low = jnp.concatenate([pack_ref[g, 0:4, :] for g in range(G)], axis=0)
    high = jnp.concatenate([pack_ref[g, 12:16, :] for g in range(G)], axis=0)
    pc_ref[0 : 4 * G, :] = jnp.where(at_odd, low, high).astype(BF16)


def demosaic_kernel(dims, pack_ref, pc_ref, far_ref, goals_ref, h_ref, *refs):
    nf, fl, G, nsc, n_space, inv_pixels = dims
    F = nf * fl
    W = G * LANES
    half = W // 2
    far_refs, refs = refs[:nf], refs[nf:]
    big_ref, bigt_ref, offs_ref, part_ref, wideh_ref, widel_ref = refs[:6]
    out_ref, goal_ref, mm_ref, p_ref, q_ref, ns_ref = refs[6:]
    s = lax.axis_index("space")
    fr = lax.axis_index("frame")
    odd = lax.rem(s, 2)
    rows_out = max(G, 8)

    lead = G * 4
    for j in range(nf):
        at = pl.multiple_of(lax.rem(fr + j, nf) * (nsc * LANES), LANES)
        for c in range(nsc):
            first = (j * nsc + c) * 32
            to = pl.ds(pl.multiple_of(at + c * LANES, LANES), LANES)
            goal_ref[1 - odd, :, to] = pc_ref[lead + first : lead + first + 32, :].astype(F32)
            blocks = [side_block(far_refs[j], 2 * fl, 2 * c + k) for k in range(2)]
            goal_ref[odd, :, to] = jnp.concatenate(blocks, axis=0)

    near = pc_ref[0:lead, :].astype(F32)
    far = far_ref[...]
    low = jnp.where(odd == 1, near, far)
    high = jnp.where(odd == 1, far, near)
    for g in range(G):
        mm_ref[g, 0:4, :] = low[4 * g : 4 * g + 4]
        mm_ref[g, 4:20, :] = pack_ref[g]
        mm_ref[g, 20:24, :] = high[4 * g : 4 * g + 4]
    pairs = jnp.concatenate(
        [jnp.concatenate([mm_ref[2 * h], mm_ref[2 * h + 1]], axis=1) for h in range(G // 2)],
        axis=0,
    )
    parted = dot(pairs.astype(BF16), part_ref[...])
    site = lax.broadcasted_iota(jnp.int32, (24, half), 1)
    pieces = []
    for q in range(2):
        plane = jnp.concatenate(
            [parted[24 * h : 24 * h + 24, q * 128 : (q + 1) * 128] for h in range(G // 2)], axis=1
        )
        pieces.append(jnp.where(site == 0, 0.0, pltpu.roll(plane, 1, 1)))
        pieces.append(plane)
        pieces.append(jnp.where(site == half - 1, 0.0, pltpu.roll(plane, half - 1, 1)))
    pieces.append(jnp.zeros((112, half), F32))
    taps = jnp.concatenate(pieces, axis=0).astype(BF16)

    preact = dot(big_ref[...], taps)
    diag = lax.broadcasted_iota(jnp.int32, (32, LANES), 0) == lax.broadcasted_iota(
        jnp.int32, (32, LANES), 1
    )
    offs = jnp.where(diag, jnp.broadcast_to(offs_ref[2:3, :], (32, LANES)), 0.0)
    offs = jnp.broadcast_to(jnp.sum(offs, axis=1, keepdims=True), (32, half))
    bias = jnp.zeros((32, half), F32)
    slopes = []
    for sy in range(10):
        v = preact[sy * 32 : sy * 32 + 32] + offs
        sig = jax.nn.sigmoid(v)
        goal = goal_ref[0] if sy == 0 else goal_ref[1] if sy == 9 else goals_ref[sy - 1]
        slope = (v * sig - goal) * inv_pixels * (sig * (1.0 + v * (1.0 - sig)))
        if sy == 0:
            slope = jnp.where(s == 0, 0.0, slope)
        elif sy == 9:
            slope = jnp.where(s == n_space - 1, 0.0, slope)
        else:
            bias = bias + slope
        slopes.append(slope)
    slope_bf = jnp.concatenate(slopes, axis=0).astype(BF16)

    gt = dot(bigt_ref[...], slope_bf)
    site16 = lax.broadcasted_iota(jnp.int32, (TILE, half), 1)
    planes = []
    for q in range(2):
        left, mid, right = (gt[(q * 3 + b) * 16 : (q * 3 + b) * 16 + 16] for b in range(3))
        planes.append(
            mid
            + jnp.where(site16 == half - 1, 0.0, pltpu.roll(left, half - 1, 1))
            + jnp.where(site16 == 0, 0.0, pltpu.roll(right, 1, 1))
        )
    grad = jnp.concatenate(
        [
            jnp.concatenate([p[:, h * 128 : (h + 1) * 128] for p in planes], axis=1)
            for h in range(G // 2)
        ],
        axis=0,
    )
    m = grad.shape[0]
    terms = split(grad, 2)
    pq = dot(jnp.concatenate(terms, axis=0), wideh_ref[...])
    pq = pq[:m] + (pq[m:] + dot(terms[0], widel_ref[...]))
    for r in range(rows_out):
        g = r % G
        rows = slice((g // 2) * TILE, (g // 2 + 1) * TILE)
        c0 = (g % 2) * LANES
        p_ref[r * TILE : (r + 1) * TILE, :] = pq[rows, c0 : c0 + LANES]
        q_ref[r * TILE : (r + 1) * TILE, :] = -pq[rows, 256 + c0 : 256 + c0 + LANES]
    gre, gim = fft(
        [p_ref[pl.ds(n, rows_out, stride=16), :] for n in range(16)],
        [q_ref[pl.ds(n, rows_out, stride=16), :] for n in range(16)],
    )
    for k in range(16):
        rows = slice(k * rows_out, (k + 1) * rows_out)
        rows_im = slice((16 + k) * rows_out, (17 + k) * rows_out)
        ns_ref[rows, :] = gre[k] * h_ref[rows, :] + gim[k] * h_ref[rows_im, :]
    noise = ns_ref[pl.ds(0, 16, stride=rows_out), :]
    for r in range(1, rows_out):
        noise = noise + ns_ref[pl.ds(r, 16, stride=rows_out), :]
    noise = noise * (-1.0 / (256.0 * F))
    for step in (64, 32, 16):
        noise = noise + pltpu.roll(noise, step, 1)

    prod = dot(slope_bf[32:288], taps, ((1,), (1,)))
    gw = jnp.zeros((32, 256), F32)
    for sy in range(1, 9):
        gw = gw + pltpu.roll(prod[(sy - 1) * 32 : sy * 32], 256 - 2 * sy, 1)
    tap = lax.broadcasted_iota(jnp.int32, (32, LANES), 1)
    pair = tap >> 2
    a = (pair * 11) >> 5
    source = ((tap & 1) * 3 + pair - 3 * a) * 24 + 2 * a + ((tap >> 1) & 1)
    source = jnp.where(tap < 36, source, 0)
    lower_part = jnp.take_along_axis(gw[:, :LANES], source & 127, axis=1)
    upper_part = jnp.take_along_axis(gw[:, LANES:], source & 127, axis=1)
    gw = jnp.where(source < LANES, lower_part, upper_part)
    gw = jnp.where(tap == 36, jnp.sum(bias, axis=1, keepdims=True), gw)
    gw = jnp.where(tap < 37, gw, 0.0)
    first = gw[0:8] + (pltpu.roll(gw[8:16], 37, 1) + pltpu.roll(gw[16:24], 74, 1))
    group = lax.broadcasted_iota(jnp.int32, (8, LANES), 1) // TILE
    second = jnp.where(group == 5, noise[:8], jnp.where(group == 6, noise[8:], gw[24:32]))
    out_ref[...] = jnp.concatenate([first, second], axis=0)


def last_sum(nf, pack_ref, own_ref, got_ref, merged_ref, weight_ref, bias_ref, noise_ref):
    own = pack_ref.shape[0] // nf
    fr = lax.axis_index("frame")
    for k in range(own):
        merged_ref[:, k * LANES : (k + 1) * LANES] = pack_ref[fr * own + k]
    total = own_ref[...] + got_ref[...]
    first, second = total[:8], total[8:]
    gw = jnp.concatenate(
        [first, pltpu.roll(first, LANES - 37, 1), pltpu.roll(first, LANES - 74, 1), second], axis=0
    )
    weight_ref[...] = gw[:, :36]
    line = lax.broadcasted_iota(jnp.int32, (32, LANES), 0)
    lane = lax.broadcasted_iota(jnp.int32, (32, LANES), 1)
    bias = jnp.where(line == lane, jnp.broadcast_to(gw[:, 36:37], (32, LANES)), 0.0)
    bias_ref[...] = jnp.sum(bias, axis=0, keepdims=True)[:, :32]
    group = lane[:8] // TILE
    for k in range(2):
        part = jnp.where(group == 5 + k, second, 0.0)
        for step in (16, 32, 64):
            part = part + pltpu.roll(part, step, 1)
        part = jnp.where(group == line[:8], part, 0.0)
        noise_ref[k : k + 1, :] = jnp.sum(part, axis=0, keepdims=True)


def involution(value, count, step, first):
    pairs = []
    for i in range(first, count):
        j = ((i - first) ^ step) + first
        if j < count:
            pairs.append((i, j))
    return lax.ppermute(value, "space", pairs)


def sum_space(value, count):
    bits = count.bit_length() - 1
    assert 1 << bits == count
    stages = []
    at = 0
    while at < bits:
        width = 2 if at == 1 and bits - at >= 3 else 1
        stages.append([m << at for m in range(1, 1 << width)])
        at += width
    for masks in stages[:-1]:
        got = []
        for m in masks:
            got.append(lax.ppermute(value, "space", [(i, i ^ m) for i in range(count)]))
        value = value + got[0]
        if len(got) == 3:
            value = value + (got[1] + got[2])
    (mask,) = stages[-1]
    got = lax.ppermute(value, "space", [(i, i ^ mask) for i in range(count)])
    return value, got


def call(body, args, outs, scratch):
    vm = pl.BlockSpec(memory_space=pltpu.VMEM)
    sizes = [int(np.prod(a.shape)) * a.dtype.itemsize for a in list(args) + list(outs)]
    sizes += [int(np.prod(a.shape)) * 4 for a in scratch if a.memory_space == pltpu.VMEM]
    return pl.pallas_call(
        body,
        out_shape=tuple(outs),
        in_specs=[vm] * len(args),
        out_specs=(vm,) * len(outs),
        scratch_shapes=scratch,
        compiler_params=pltpu.CompilerParams(vmem_limit_bytes=sum(sizes) + (12 << 20)),
    )(*args)


def shards(raw, shifts, weight, offset, log_var, goal):
    nf = lax.axis_size("frame")
    n_space = lax.axis_size("space")
    fl, band_rows, W = raw.shape
    T = shifts.shape[3]
    channels, _, ws = goal.shape
    G = W // LANES
    F = nf * fl
    nsc = ws // LANES
    inv_pixels = 1.0 / (band_rows * n_space * W // 4)
    rows_out = max(G, 8)

    def from_frame(value, j):
        return lax.ppermute(value, "frame", [(i, (i - j) % nf) for i in range(nf)])

    def pieces(value):
        return [value] + [from_frame(value, j) for j in range(1, nf)]

    shape = jax.ShapeDtypeStruct
    words = -(-2 * fl // 16)
    far_planes = -(-(2 * nsc + words) // G)
    planes = far_planes + -(-2 * nsc // G)
    raw_core = involution(raw, n_space, 1, 0)
    (side,) = call(
        functools.partial(side_kernel, (fl, nsc, T)),
        [shifts, goal],
        [shape((planes, TILE, W), BF16)],
        [pltpu.VMEM((256, LANES), F32), pltpu.VMEM((16 * words, LANES), jnp.int32)],
    )
    near = lax.optimization_barrier(jnp.pad(raw, ((0, fl + planes), (0, 0), (0, 0))))
    near = lax.dynamic_update_slice(near, side, (2 * fl, 0, 0))
    near = lax.dynamic_update_slice(near, raw_core, (fl, 0, 0))
    far_own = involution(near[: 2 * fl + far_planes], n_space, 1, 1)
    nears = pieces(near)
    *tables, big, bigt = call(
        table_kernel,
        [weight],
        [
            shape((256, 256), BF16),
            shape((128, 256), BF16),
            shape((256, 256), BF16),
            shape((256, 128), BF16),
            shape((256, 256), BF16),
            shape((256, 512), BF16),
            shape((256, 512), BF16),
            shape((320, 256), BF16),
            shape((96, 320), BF16),
        ],
        [pltpu.VMEM((6, 40, LANES), F32)],
    )
    small = jnp.concatenate(
        [jnp.exp(log_var), offset, jnp.zeros((6 * LANES - channels,), F32)]
    ).reshape(8, LANES)
    fars = pieces(far_own)
    goals = pieces(goal)
    (site_goals,) = call(
        functools.partial(target_kernel, (nf, nsc)),
        goals,
        [shape((8, channels, W // 2), F32)],
        [pltpu.VMEM((256, LANES), F32)],
    )

    pack, pc, far, moments = call(
        functools.partial(merge_kernel, (nf, fl, G, T, nsc)),
        [*nears, *fars, small, *tables[:4]],
        [
            shape((G, TILE, LANES), F32),
            shape((4 * G + nf * nsc * channels, LANES), BF16),
            shape((4 * G, LANES), F32),
            shape((32 * rows_out, LANES), F32),
        ],
        [
            pltpu.VMEM((F * G, 4 * TILE, LANES), F32),
            pltpu.VMEM((2, F * G, 8, LANES), jnp.int32),
            pltpu.VMEM((2, 256, LANES), F32),
            pltpu.VMEM((2, 256, LANES), F32),
            pltpu.VMEM((20 * rows_out, LANES), F32),
            pltpu.VMEM((2 * F, LANES), jnp.int32),
            pltpu.VMEM((2 * F, LANES), jnp.int32),
            pltpu.SMEM((2 * F, LANES), jnp.int32),
            pltpu.SMEM((2 * F, LANES), jnp.int32),
            pltpu.SemaphoreType.DMA((2,)),
        ],
    )
    pc = involution(pc, n_space, 1, 0)
    (partial,) = call(
        functools.partial(demosaic_kernel, (nf, fl, G, nsc, n_space, inv_pixels)),
        [pack, pc, far, site_goals, moments, *fars, big, bigt, small, *tables[4:]],
        [shape((16, LANES), F32)],
        [
            pltpu.VMEM((2, channels, W // 2), F32),
            pltpu.VMEM((G, 24, LANES), F32),
            pltpu.VMEM((rows_out * TILE, LANES), F32),
            pltpu.VMEM((rows_out * TILE, LANES), F32),
            pltpu.VMEM((rows_out * TILE, LANES), F32),
        ],
    )
    merged, grad_weight, grad_bias, grad_noise = call(
        functools.partial(last_sum, nf),
        [pack, *sum_space(partial, n_space)],
        [
            shape((TILE, W // nf), F32),
            shape((channels, 36), F32),
            shape((1, channels), F32),
            shape((2, LANES), F32),
        ],
        [],
    )
    return merged, grad_weight, grad_bias.reshape(channels), grad_noise.reshape(256)


def solution(mesh):
    placed = (
        P("frame", "space", None),
        P("frame", None, "space", None),
        P(),
        P(),
        P(),
        P(None, "space", "frame"),
    )

    return jax.shard_map(
        shards,
        mesh=mesh,
        in_specs=placed,
        out_specs=(P("space", "frame"), P(), P(), P()),
        check_vma=False,
    )
```

```python
import functools
import math

import jax
import jax.numpy as jnp
import ml_dtypes
import numpy as np
from jax import lax
from jax.experimental import pallas as pl
from jax.experimental.pallas import tpu as pltpu
from jax.sharding import PartitionSpec as P


TILE = 16
LANES = 128
F32 = jnp.float32
BF16 = jnp.bfloat16


def dot(a, b, dims=((1,), (0,))):
    return lax.dot_general(a, b, (dims, ((), ())), preferred_element_type=F32)


def split(value, parts):
    terms = []
    for _ in range(parts):
        term = value.astype(BF16)
        terms.append(term)
        value = value - term.astype(F32)
    return terms


def split_table(value, parts):
    terms = []
    for _ in range(parts):
        term = float(np.float32(value).astype(ml_dtypes.bfloat16))
        terms.append(term)
        value = value - term
    return terms


def wave(phase, parts):
    near = jnp.minimum(phase, 16 - phase)
    step = jnp.minimum(near, 8 - near)
    flip = near > 4
    steps = [split_table(math.cos(2.0 * math.pi * k / 16.0), parts) for k in range(4)]
    terms = []
    for p in range(parts):
        value = jnp.zeros(phase.shape, F32)
        for k in range(4):
            value = jnp.where(step == k, float(steps[k][p]), value)
        terms.append(jnp.where(flip, -value, value))
    return terms


def waves(phase, parts):
    phase = phase & 15
    return wave(phase, parts), wave((phase + 12) & 15, parts)


def turn(re, im, k, n):
    if k == 0:
        return re, im
    if 4 * k == n:
        return im, -re
    if 8 * k == n:
        half = math.sqrt(0.5)
        return (re + im) * half, (im - re) * half
    if 8 * k == 3 * n:
        half = math.sqrt(0.5)
        return (im - re) * half, (re + im) * -half
    c, s = math.cos(2.0 * math.pi * k / n), math.sin(2.0 * math.pi * k / n)
    return re * c + im * s, im * c - re * s


def fft(re, im):
    n = len(re)
    if n == 1:
        return re, im
    er, ei = fft(re[0::2], im[0::2])
    our, oi = fft(re[1::2], im[1::2])
    half = n // 2
    xr, xi = [None] * n, [None] * n
    for k in range(half):
        tr, ti = turn(our[k], oi[k], k, n)
        xr[k], xi[k] = er[k] + tr, ei[k] + ti
        xr[k + half], xi[k + half] = er[k] - tr, ei[k] - ti
    return xr, xi


def tree(values):
    while len(values) > 1:
        half = len(values) // 2
        values = [a + b for a, b in zip(values[:half], values[half:])]
    return values[0]


def add_lists(a, b):
    return b if a is None else [x + y for x, y in zip(a, b)]


def side_kernel(dims, shift_ref, goal_ref, side_ref, raw_ref, words_ref):
    fl, nsc, T = dims
    odd = lax.rem(lax.axis_index("space"), 2)
    G = side_ref.shape[2] // LANES
    for l in range(fl):
        for c in range(2):
            row = shift_ref[l, c]
            if T < LANES:
                row = jnp.concatenate([row, jnp.zeros((1, LANES - T), jnp.int32)], axis=1)
            words_ref[l * 2 + c : l * 2 + c + 1, :] = row
    far, core = [], []
    for c in range(nsc):
        raw_ref[...] = goal_ref[:, :, c * LANES : (c + 1) * LANES].astype(F32).reshape(256, LANES)
        edge = raw_ref[pl.ds(7 * odd, 32, stride=8), :]
        far += [edge[:16], edge[16:]]
        edge = raw_ref[pl.ds(7 - 7 * odd, 32, stride=8), :]
        core += [edge[:16], edge[16:]]
    words = words_ref[...].astype(F32)
    words = [words[16 * k : 16 * k + 16] for k in range(words.shape[0] // 16)]
    blocks = []
    for group in (words + core, far + words):
        blocks += group + [jnp.zeros((TILE, LANES), F32)] * (-len(group) % G)
    for k, block in enumerate(blocks):
        at = (k % G) * LANES
        side_ref[k // G, :, at : at + LANES] = block.astype(BF16)


def target_kernel(dims, *refs):
    nf, nsc = dims
    goal_refs, goal_ref, raw_ref = refs[:nf], refs[nf], refs[nf + 1]
    fr = lax.axis_index("frame")
    for j in range(nf):
        at = pl.multiple_of(lax.rem(fr + j, nf) * (nsc * LANES), LANES)
        for c in range(nsc):
            cols = slice(c * LANES, (c + 1) * LANES)
            raw_ref[...] = goal_refs[j][:, :, cols].astype(F32).reshape(256, LANES)
            to = pl.ds(pl.multiple_of(at + c * LANES, LANES), LANES)
            for r in range(8):
                goal_ref[r, :, to] = raw_ref[pl.ds(r, 32, stride=8), :]


def table_kernel(weight_ref, *refs):
    fwd_ref, fwdl_ref, inv_ref, invl_ref, part_ref, wideh_ref, widel_ref = refs[:7]
    big_ref, bigt_ref, rows_ref = refs[7:]
    lane = lax.broadcasted_iota(jnp.int32, (TILE, LANES), 1)
    line = lax.broadcasted_iota(jnp.int32, (TILE, LANES), 0)
    cos, sin = waves(line * (lane & 15), 3)
    for k in range(8):
        at = slice(k * TILE, (k + 1) * TILE)
        mid = slice(128 + k * TILE, 128 + (k + 1) * TILE)
        here = (lane // TILE) == k
        c = [jnp.where(here, v, 0.0).astype(BF16) for v in cos]
        d = [jnp.where(here, v, 0.0).astype(BF16) for v in sin]
        fwd_ref[at, :] = jnp.concatenate([c[0], d[0]], axis=1)
        fwd_ref[mid, :] = jnp.concatenate([c[1], d[1]], axis=1)
        fwdl_ref[at, :] = jnp.concatenate([c[2], d[2]], axis=1)
        inv_ref[at, :] = jnp.concatenate([c[0], c[1]], axis=1)
        inv_ref[mid, :] = jnp.concatenate([-d[0], -d[1]], axis=1)
        invl_ref[at, :] = c[2]
        invl_ref[mid, :] = -d[2]
    line = lax.broadcasted_iota(jnp.int32, (256, 256), 0)
    column = lax.broadcasted_iota(jnp.int32, (256, 256), 1)
    source = 2 * (column & 127) + (column >> 7)
    part_ref[...] = jnp.where(line == source, 1.0, 0.0).astype(BF16)
    lane8 = lax.broadcasted_iota(jnp.int32, (8, LANES), 1)
    line8 = lax.broadcasted_iota(jnp.int32, (8, LANES), 0)
    empty = jnp.zeros((8, LANES), F32)
    for q in range(2):
        cos, sin = waves((2 * line8 + q) * (lane8 & 15), 2)
        for t in range(0, 16, 2):
            for ref, c, d in ((wideh_ref, cos[0], sin[0]), (widel_ref, cos[1], sin[1])):
                rows = []
                for u in (t, t + 1):
                    here = lane8 // TILE == u % 8
                    row = []
                    for v in (c, d):
                        v = jnp.where(here, v, 0.0)
                        row += [v, empty] if u < 8 else [empty, v]
                    rows.append(jnp.concatenate(row, axis=1))
                at = q * 128 + t * 8
                ref[at : at + 16, :] = jnp.concatenate(rows, axis=0).astype(BF16)

    weight = weight_ref[...].astype(F32)
    weight = jnp.concatenate([weight, jnp.zeros((32, LANES - 36), F32)], axis=1)
    halves = []
    for h in range(2):
        at = lax.broadcasted_iota(jnp.int32, (32, LANES), 1) + h * LANES
        group = (at * 171) >> 12
        row = at - 24 * group
        q = jnp.where(group >= 3, 1, 0)
        tap = (3 * (row >> 1) + group - 3 * q) * 4 + 2 * (row & 1) + q
        valid = (row < 6) & (group < 6)
        taken = jnp.take_along_axis(weight, jnp.where(valid, tap, 0), axis=1)
        halves.append(jnp.where(valid, taken, 0.0))
    base = jnp.concatenate(halves, axis=1)
    for sy in range(10):
        moved = pltpu.roll(base, 2 * sy, 1) if sy else base
        big_ref[sy * 32 : (sy + 1) * 32, :] = moved.astype(BF16)

    turned = jnp.transpose(jnp.concatenate([weight] * 4, axis=0))
    rows_ref[...] = jnp.zeros_like(rows_ref)
    for q in range(2):
        for b in range(3):
            for j in range(6):
                tap = (3 * (j // 2) + b) * 4 + 2 * (j % 2) + q
                rows_ref[q * 3 + b, 16 + j : 17 + j, :] = turned[tap : tap + 1, :]
    quarter = lax.broadcasted_iota(jnp.int32, (TILE, LANES), 1) // 32
    for k in range(6):
        for tile in range(3):
            value = jnp.zeros((TILE, LANES), F32)
            for u in range(4):
                sy = 4 * tile + u
                if sy < 10:
                    block = rows_ref[k, 20 - 2 * sy : 36 - 2 * sy, :]
                    value = jnp.where(quarter == u, block, value)
            width = 64 if tile == 2 else LANES
            at = tile * LANES
            bigt_ref[k * TILE : (k + 1) * TILE, at : at + width] = value[:, :width].astype(BF16)


def side_block(ref, plane, k):
    per = ref.shape[2] // LANES
    at = (k % per) * LANES
    return ref[plane + k // per, :, at : at + LANES].astype(F32)


def merge_kernel(dims, *refs):
    nf, fl, G, _, nsc = dims
    F = nf * fl
    near_refs, far_refs, refs = refs[:nf], refs[nf : 2 * nf], refs[2 * nf :]
    var_ref, fwd_ref, fwdl_ref, inv_ref, invl_ref = refs[:5]
    pack_ref, pc_ref, far_ref, h_ref = refs[5:9]
    x_ref, idx_ref, p_ref, q_ref, xs_ref, own_ref, words_ref, own_sm, far_sm, sems = refs[9:]
    s = lax.axis_index("space")
    fr = lax.axis_index("frame")
    odd = lax.rem(s, 2)

    wb = -(-2 * fl // 16)
    for group, ref, at in ((near_refs, own_ref, 0), (far_refs, words_ref, 2 * nsc)):
        for j in range(nf):
            words = [side_block(group[j], 2 * fl, at + k) for k in range(wb)]
            words = jnp.concatenate(words, axis=0)[: 2 * fl].astype(jnp.int32)
            ref[2 * fl * j : 2 * fl * (j + 1), :] = words
    moves = (
        pltpu.make_async_copy(own_ref, own_sm, sems.at[0]),
        pltpu.make_async_copy(words_ref, far_sm, sems.at[1]),
    )
    for move in moves:
        move.start()

    slots = (
        (near_refs, 0, 2 - odd),
        (near_refs, fl, 3 - 3 * odd),
        (far_refs, 0, 1 + odd),
        (far_refs, fl, 3 * odd),
    )
    for group, start, slot in slots:
        for j in range(nf):
            for l in range(fl):
                rows = group[j][start + l].astype(F32)
                for g in range(G):
                    block = rows[:, g * LANES : (g + 1) * LANES]
                    at = pl.ds(pl.multiple_of(slot * TILE, TILE), TILE)
                    x_ref[(j * fl + l) * G + g, at, :] = block

    spot = lax.broadcasted_iota(jnp.int32, (8, LANES), 1)
    for which, ref in enumerate((own_ref, words_ref)):
        for f in range(F):
            row = jnp.broadcast_to(ref[2 * f + 1 : 2 * f + 2, :], (8, LANES))
            for g in range(G):
                moved = jnp.take_along_axis(row, 8 * g + spot // TILE, axis=1)
                idx_ref[which, f * G + g] = (moved + spot) & (LANES - 1)
    for j in range(nf):
        for k in range(2 * nsc):
            at = 4 * G + (j * 2 * nsc + k) * TILE
            block = side_block(near_refs[j], 2 * fl, wb + k)
            pc_ref[at : at + TILE, :] = block.astype(BF16)

    lane = lax.broadcasted_iota(jnp.int32, (TILE, LANES), 1)
    kind = (lane // TILE) % 4
    per = 16 // G
    chunks = F * G // 16
    rows_out = max(G, 8)
    fold = TILE // rows_out
    zero = jnp.zeros((TILE, LANES), F32)

    def place(f):
        if nf == 2:
            return f
        return lax.rem(f // fl + nf - fr, nf) * fl + f % fl

    first = lax.rem(nf - fr, nf) * fl
    log_var = var_ref[...]
    variances = []
    for k in range(16):
        row = jnp.broadcast_to(log_var[k // 8 : k // 8 + 1], (8, LANES))
        row = jnp.take_along_axis(row, (k % 8) * TILE + spot % TILE, axis=1)
        variances.append(jnp.concatenate([row, row], axis=0))

    def tile_row(which, row0, dy_ref, c, carry):
        sums = carry[0] if carry is not None else None
        blocks = []
        for q in range(16):
            g = q % G
            f = place(c * per + q // G)

            def load(t, group):
                if group < 0 or group >= G:
                    return zero
                start = row0 + dy_ref[2 * f, 8 * g + t]
                return x_ref[f * G + group, pl.ds(start, TILE), :]

            idx = idx_ref[which, f * G + g]
            idx = jnp.concatenate([idx, idx], axis=0)
            mixes = (
                jnp.where(
                    lane < 40,
                    load(0, g),
                    jnp.where(lane < 104, load(4, g), load(0, g - 1)),
                ),
                jnp.where(lane < 56, load(1, g), load(5, g)),
                jnp.where(lane < 72, load(2, g), load(6, g)),
                jnp.where(
                    lane < 24,
                    load(7, g + 1),
                    jnp.where(lane < 88, load(3, g), load(7, g)),
                ),
            )
            moved = [jnp.take_along_axis(m, idx, axis=1) for m in mixes]
            blocks.append(
                jnp.where(
                    kind < 2,
                    jnp.where(kind == 0, moved[0], moved[1]),
                    jnp.where(kind == 2, moved[2], moved[3]),
                )
            )
        base = [x_ref[first * G + g, pl.ds(pl.multiple_of(row0, TILE), TILE), :] for g in range(G)]
        both = jnp.concatenate(blocks + base, axis=0).astype(BF16)
        pq = dot(jnp.concatenate([both, both], axis=1), fwd_ref[...]) + dot(both, fwdl_ref[...])
        for q in range(16):
            rows = slice(q * TILE, (q + 1) * TILE)
            ref_rows = slice(256 + (q % G) * TILE, 256 + (q % G + 1) * TILE)
            diff = pq[ref_rows] - pq[rows]
            p_ref[which, rows, :] = diff[:, :LANES]
            q_ref[which, rows, :] = -diff[:, LANES:]
        re, im = fft(
            [p_ref[which, pl.ds(n, 16, stride=16), :] for n in range(16)],
            [q_ref[which, pl.ds(n, 16, stride=16), :] for n in range(16)],
        )
        out = [[], [], [], []]
        for k in range(16):
            energy = re[k] * re[k] + im[k] * im[k]
            weight = energy / (energy + variances[k])
            wr = weight * re[k]
            wi = weight * im[k]
            vals = (wr, wi)
            if which == 0:
                rest = 1.0 - weight
                vals = (wr, wi, wr * rest, wi * rest)
            for store, val in zip(out, vals):
                if fold == 2:
                    val = val[:8] + val[8:]
                store.append(val)
        flat = out[0] + out[1] + out[2] + out[3]
        return sums_of(sums, blocks), add_lists(carry[1] if carry is not None else None, flat)

    def sums_of(sums, blocks):
        return add_lists(sums, [tree(blocks[g::G]) for g in range(G)])

    def whole_row(which, row0, dy_ref):
        step = functools.partial(tile_row, which, row0, dy_ref)
        carry = step(0, None)
        if chunks > 1:
            carry = lax.fori_loop(1, chunks, step, carry)
        return carry

    moves[0].wait()
    sums, flat = whole_row(0, (2 - odd) * TILE, own_sm)
    for k in range(32):
        h_ref[k * rows_out : (k + 1) * rows_out, :] = flat[32 + k]
    moves[1].wait()
    far_sums, far_flat = whole_row(1, (1 + odd) * TILE, far_sm)

    vi, ur = fft(flat[16:32], flat[:16])
    far_vi, far_ur = fft(far_flat[16:32], far_flat[:16])
    at_odd = odd == 1
    ur += [jnp.where(at_odd, far_ur[k], far_ur[12 + k]) for k in range(4)]
    vi += [jnp.where(at_odd, far_vi[k], far_vi[12 + k]) for k in range(4)]
    uv = jnp.concatenate([jnp.concatenate(ur, axis=0), jnp.concatenate(vi, axis=0)], axis=1)
    m = 20 * rows_out
    terms = split(uv, 3)
    wide = dot(jnp.concatenate(terms, axis=0), inv_ref[...])
    pix = wide[:m, :LANES] + (wide[m : 2 * m, :LANES] + wide[:m, LANES:])
    pix = pix + (wide[2 * m :, :LANES] + wide[m : 2 * m, LANES:] + dot(terms[0], invl_ref[...]))
    xs_ref[...] = pix
    far_rows = []
    for g in range(G):
        val = xs_ref[pl.ds(g, 16, stride=rows_out), :]
        far = xs_ref[pl.ds(16 * rows_out + g, 4, stride=rows_out), :]
        for other in range(g + G, rows_out, G):
            val = val + xs_ref[pl.ds(other, 16, stride=rows_out), :]
            far = far + xs_ref[pl.ds(16 * rows_out + other, 4, stride=rows_out), :]
        pack_ref[g] = (sums[g] + val / 256.0) / F
        far_sum = jnp.where(at_odd, far_sums[g][0:4], far_sums[g][12:16])
        far_rows.append((far_sum + far / 256.0) / F)
    far_ref[...] = jnp.concatenate(far_rows, axis=0)
    low = jnp.concatenate([pack_ref[g, 0:4, :] for g in range(G)], axis=0)
    high = jnp.concatenate([pack_ref[g, 12:16, :] for g in range(G)], axis=0)
    pc_ref[0 : 4 * G, :] = jnp.where(at_odd, low, high).astype(BF16)


def demosaic_kernel(dims, pack_ref, pc_ref, far_ref, goals_ref, h_ref, *refs):
    nf, fl, G, nsc, n_space, inv_pixels = dims
    F = nf * fl
    W = G * LANES
    half = W // 2
    far_refs, refs = refs[:nf], refs[nf:]
    big_ref, bigt_ref, offs_ref, part_ref, wideh_ref, widel_ref = refs[:6]
    out_ref, goal_ref, mm_ref, p_ref, q_ref, ns_ref = refs[6:]
    s = lax.axis_index("space")
    fr = lax.axis_index("frame")
    odd = lax.rem(s, 2)
    rows_out = max(G, 8)

    lead = G * 4
    for j in range(nf):
        at = pl.multiple_of(lax.rem(fr + j, nf) * (nsc * LANES), LANES)
        for c in range(nsc):
            first = (j * nsc + c) * 32
            to = pl.ds(pl.multiple_of(at + c * LANES, LANES), LANES)
            goal_ref[1 - odd, :, to] = pc_ref[lead + first : lead + first + 32, :].astype(F32)
            blocks = [side_block(far_refs[j], 2 * fl, 2 * c + k) for k in range(2)]
            goal_ref[odd, :, to] = jnp.concatenate(blocks, axis=0)

    near = pc_ref[0:lead, :].astype(F32)
    far = far_ref[...]
    low = jnp.where(odd == 1, near, far)
    high = jnp.where(odd == 1, far, near)
    for g in range(G):
        mm_ref[g, 0:4, :] = low[4 * g : 4 * g + 4]
        mm_ref[g, 4:20, :] = pack_ref[g]
        mm_ref[g, 20:24, :] = high[4 * g : 4 * g + 4]
    pairs = jnp.concatenate(
        [jnp.concatenate([mm_ref[2 * h], mm_ref[2 * h + 1]], axis=1) for h in range(G // 2)],
        axis=0,
    )
    parted = dot(pairs.astype(BF16), part_ref[...])
    site = lax.broadcasted_iota(jnp.int32, (24, half), 1)
    pieces = []
    for q in range(2):
        plane = jnp.concatenate(
            [parted[24 * h : 24 * h + 24, q * 128 : (q + 1) * 128] for h in range(G // 2)], axis=1
        )
        pieces.append(jnp.where(site == 0, 0.0, pltpu.roll(plane, 1, 1)))
        pieces.append(plane)
        pieces.append(jnp.where(site == half - 1, 0.0, pltpu.roll(plane, half - 1, 1)))
    pieces.append(jnp.zeros((112, half), F32))
    taps = jnp.concatenate(pieces, axis=0).astype(BF16)

    preact = dot(big_ref[...], taps)
    diag = lax.broadcasted_iota(jnp.int32, (32, LANES), 0) == lax.broadcasted_iota(
        jnp.int32, (32, LANES), 1
    )
    offs = jnp.where(diag, jnp.broadcast_to(offs_ref[2:3, :], (32, LANES)), 0.0)
    offs = jnp.broadcast_to(jnp.sum(offs, axis=1, keepdims=True), (32, half))
    bias = jnp.zeros((32, half), F32)
    slopes = []
    for sy in range(10):
        v = preact[sy * 32 : sy * 32 + 32] + offs
        sig = jax.nn.sigmoid(v)
        goal = goal_ref[0] if sy == 0 else goal_ref[1] if sy == 9 else goals_ref[sy - 1]
        slope = (v * sig - goal) * inv_pixels * (sig * (1.0 + v * (1.0 - sig)))
        if sy == 0:
            slope = jnp.where(s == 0, 0.0, slope)
        elif sy == 9:
            slope = jnp.where(s == n_space - 1, 0.0, slope)
        else:
            bias = bias + slope
        slopes.append(slope)
    slope_bf = jnp.concatenate(slopes, axis=0).astype(BF16)

    gt = dot(bigt_ref[...], slope_bf)
    site16 = lax.broadcasted_iota(jnp.int32, (TILE, half), 1)
    planes = []
    for q in range(2):
        left, mid, right = (gt[(q * 3 + b) * 16 : (q * 3 + b) * 16 + 16] for b in range(3))
        planes.append(
            mid
            + jnp.where(site16 == half - 1, 0.0, pltpu.roll(left, half - 1, 1))
            + jnp.where(site16 == 0, 0.0, pltpu.roll(right, 1, 1))
        )
    grad = jnp.concatenate(
        [
            jnp.concatenate([p[:, h * 128 : (h + 1) * 128] for p in planes], axis=1)
            for h in range(G // 2)
        ],
        axis=0,
    )
    m = grad.shape[0]
    terms = split(grad, 2)
    pq = dot(jnp.concatenate(terms, axis=0), wideh_ref[...])
    pq = pq[:m] + (pq[m:] + dot(terms[0], widel_ref[...]))
    for r in range(rows_out):
        g = r % G
        rows = slice((g // 2) * TILE, (g // 2 + 1) * TILE)
        c0 = (g % 2) * LANES
        p_ref[r * TILE : (r + 1) * TILE, :] = pq[rows, c0 : c0 + LANES]
        q_ref[r * TILE : (r + 1) * TILE, :] = -pq[rows, 256 + c0 : 256 + c0 + LANES]
    gre, gim = fft(
        [p_ref[pl.ds(n, rows_out, stride=16), :] for n in range(16)],
        [q_ref[pl.ds(n, rows_out, stride=16), :] for n in range(16)],
    )
    for k in range(16):
        rows = slice(k * rows_out, (k + 1) * rows_out)
        rows_im = slice((16 + k) * rows_out, (17 + k) * rows_out)
        ns_ref[rows, :] = gre[k] * h_ref[rows, :] + gim[k] * h_ref[rows_im, :]
    noise = ns_ref[pl.ds(0, 16, stride=rows_out), :]
    for r in range(1, rows_out):
        noise = noise + ns_ref[pl.ds(r, 16, stride=rows_out), :]
    noise = noise * (-1.0 / (256.0 * F))
    for step in (64, 32, 16):
        noise = noise + pltpu.roll(noise, step, 1)

    prod = dot(slope_bf[32:288], taps, ((1,), (1,)))
    gw = jnp.zeros((32, 256), F32)
    for sy in range(1, 9):
        gw = gw + pltpu.roll(prod[(sy - 1) * 32 : sy * 32], 256 - 2 * sy, 1)
    tap = lax.broadcasted_iota(jnp.int32, (32, LANES), 1)
    pair = tap >> 2
    a = (pair * 11) >> 5
    source = ((tap & 1) * 3 + pair - 3 * a) * 24 + 2 * a + ((tap >> 1) & 1)
    source = jnp.where(tap < 36, source, 0)
    lower_part = jnp.take_along_axis(gw[:, :LANES], source & 127, axis=1)
    upper_part = jnp.take_along_axis(gw[:, LANES:], source & 127, axis=1)
    gw = jnp.where(source < LANES, lower_part, upper_part)
    gw = jnp.where(tap == 36, jnp.sum(bias, axis=1, keepdims=True), gw)
    gw = jnp.where(tap < 37, gw, 0.0)
    first = gw[0:8] + (pltpu.roll(gw[8:16], 37, 1) + pltpu.roll(gw[16:24], 74, 1))
    group = lax.broadcasted_iota(jnp.int32, (8, LANES), 1) // TILE
    second = jnp.where(group == 5, noise[:8], jnp.where(group == 6, noise[8:], gw[24:32]))
    out_ref[...] = jnp.concatenate([first, second], axis=0)


def last_sum(nf, pack_ref, own_ref, got_ref, merged_ref, weight_ref, bias_ref, noise_ref):
    own = pack_ref.shape[0] // nf
    fr = lax.axis_index("frame")
    for k in range(own):
        merged_ref[:, k * LANES : (k + 1) * LANES] = pack_ref[fr * own + k]
    total = own_ref[...] + got_ref[...]
    first, second = total[:8], total[8:]
    gw = jnp.concatenate(
        [first, pltpu.roll(first, LANES - 37, 1), pltpu.roll(first, LANES - 74, 1), second], axis=0
    )
    weight_ref[...] = gw[:, :36]
    line = lax.broadcasted_iota(jnp.int32, (32, LANES), 0)
    lane = lax.broadcasted_iota(jnp.int32, (32, LANES), 1)
    bias = jnp.where(line == lane, jnp.broadcast_to(gw[:, 36:37], (32, LANES)), 0.0)
    bias_ref[...] = jnp.sum(bias, axis=0, keepdims=True)[:, :32]
    group = lane[:8] // TILE
    for k in range(2):
        part = jnp.where(group == 5 + k, second, 0.0)
        for step in (16, 32, 64):
            part = part + pltpu.roll(part, step, 1)
        part = jnp.where(group == line[:8], part, 0.0)
        noise_ref[k : k + 1, :] = jnp.sum(part, axis=0, keepdims=True)


def involution(value, count, step, first):
    pairs = []
    for i in range(first, count):
        j = ((i - first) ^ step) + first
        if j < count:
            pairs.append((i, j))
    return lax.ppermute(value, "space", pairs)


def sum_space(value, count):
    bits = count.bit_length() - 1
    assert 1 << bits == count
    stages = []
    at = 0
    while at < bits:
        width = 2 if at == 1 and bits - at >= 3 else 1
        stages.append([m << at for m in range(1, 1 << width)])
        at += width
    for masks in stages[:-1]:
        got = []
        for m in masks:
            got.append(lax.ppermute(value, "space", [(i, i ^ m) for i in range(count)]))
        value = value + got[0]
        if len(got) == 3:
            value = value + (got[1] + got[2])
    (mask,) = stages[-1]
    got = lax.ppermute(value, "space", [(i, i ^ mask) for i in range(count)])
    return value, got


def call(body, args, outs, scratch):
    vm = pl.BlockSpec(memory_space=pltpu.VMEM)
    sizes = [int(np.prod(a.shape)) * a.dtype.itemsize for a in list(args) + list(outs)]
    sizes += [int(np.prod(a.shape)) * 4 for a in scratch if a.memory_space == pltpu.VMEM]
    return pl.pallas_call(
        body,
        out_shape=tuple(outs),
        in_specs=[vm] * len(args),
        out_specs=(vm,) * len(outs),
        scratch_shapes=scratch,
        compiler_params=pltpu.CompilerParams(vmem_limit_bytes=sum(sizes) + (12 << 20)),
    )(*args)


def shards(raw, shifts, weight, offset, log_var, goal):
    nf = lax.axis_size("frame")
    n_space = lax.axis_size("space")
    fl, band_rows, W = raw.shape
    T = shifts.shape[3]
    channels, _, ws = goal.shape
    G = W // LANES
    F = nf * fl
    nsc = ws // LANES
    inv_pixels = 1.0 / (band_rows * n_space * W // 4)
    rows_out = max(G, 8)

    def from_frame(value, j):
        return lax.ppermute(value, "frame", [(i, (i - j) % nf) for i in range(nf)])

    def pieces(value):
        return [value] + [from_frame(value, j) for j in range(1, nf)]

    shape = jax.ShapeDtypeStruct
    words = -(-2 * fl // 16)
    planes = -(-(2 * nsc + words) // G)
    raw_core = involution(raw, n_space, 1, 0)
    (side,) = call(
        functools.partial(side_kernel, (fl, nsc, T)),
        [shifts, goal],
        [shape((2 * planes, TILE, W), BF16)],
        [pltpu.VMEM((256, LANES), F32), pltpu.VMEM((16 * words, LANES), jnp.int32)],
    )
    near = lax.optimization_barrier(jnp.pad(raw, ((0, fl + planes), (0, 0), (0, 0))))
    near = lax.dynamic_update_slice(near, side[:planes], (2 * fl, 0, 0))
    near = lax.dynamic_update_slice(near, raw_core, (fl, 0, 0))
    far_own = jnp.concatenate([near[: 2 * fl], side[planes:]], axis=0)
    far_own = involution(far_own, n_space, 1, 1)
    nears = pieces(near)
    *tables, big, bigt = call(
        table_kernel,
        [weight],
        [
            shape((256, 256), BF16),
            shape((128, 256), BF16),
            shape((256, 256), BF16),
            shape((256, 128), BF16),
            shape((256, 256), BF16),
            shape((256, 512), BF16),
            shape((256, 512), BF16),
            shape((320, 256), BF16),
            shape((96, 320), BF16),
        ],
        [pltpu.VMEM((6, 40, LANES), F32)],
    )
    small = jnp.concatenate(
        [jnp.exp(log_var), offset, jnp.zeros((6 * LANES - channels,), F32)]
    ).reshape(8, LANES)
    fars = pieces(far_own)
    goals = pieces(goal)
    (site_goals,) = call(
        functools.partial(target_kernel, (nf, nsc)),
        goals,
        [shape((8, channels, W // 2), F32)],
        [pltpu.VMEM((256, LANES), F32)],
    )

    pack, pc, far, moments = call(
        functools.partial(merge_kernel, (nf, fl, G, T, nsc)),
        [*nears, *fars, small, *tables[:4]],
        [
            shape((G, TILE, LANES), F32),
            shape((4 * G + nf * nsc * channels, LANES), BF16),
            shape((4 * G, LANES), F32),
            shape((32 * rows_out, LANES), F32),
        ],
        [
            pltpu.VMEM((F * G, 4 * TILE, LANES), F32),
            pltpu.VMEM((2, F * G, 8, LANES), jnp.int32),
            pltpu.VMEM((2, 256, LANES), F32),
            pltpu.VMEM((2, 256, LANES), F32),
            pltpu.VMEM((20 * rows_out, LANES), F32),
            pltpu.VMEM((2 * F, LANES), jnp.int32),
            pltpu.VMEM((2 * F, LANES), jnp.int32),
            pltpu.SMEM((2 * F, LANES), jnp.int32),
            pltpu.SMEM((2 * F, LANES), jnp.int32),
            pltpu.SemaphoreType.DMA((2,)),
        ],
    )
    pc = involution(pc, n_space, 1, 0)
    (partial,) = call(
        functools.partial(demosaic_kernel, (nf, fl, G, nsc, n_space, inv_pixels)),
        [pack, pc, far, site_goals, moments, *fars, big, bigt, small, *tables[4:]],
        [shape((16, LANES), F32)],
        [
            pltpu.VMEM((2, channels, W // 2), F32),
            pltpu.VMEM((G, 24, LANES), F32),
            pltpu.VMEM((rows_out * TILE, LANES), F32),
            pltpu.VMEM((rows_out * TILE, LANES), F32),
            pltpu.VMEM((rows_out * TILE, LANES), F32),
        ],
    )
    merged, grad_weight, grad_bias, grad_noise = call(
        functools.partial(last_sum, nf),
        [pack, *sum_space(partial, n_space)],
        [
            shape((TILE, W // nf), F32),
            shape((channels, 36), F32),
            shape((1, channels), F32),
            shape((2, LANES), F32),
        ],
        [],
    )
    return merged, grad_weight, grad_bias.reshape(channels), grad_noise.reshape(256)


def solution(mesh):
    placed = (
        P("frame", "space", None),
        P("frame", None, "space", None),
        P(),
        P(),
        P(),
        P(None, "space", "frame"),
    )

    return jax.shard_map(
        shards,
        mesh=mesh,
        in_specs=placed,
        out_specs=(P("space", "frame"), P(), P(), P()),
        check_vma=False,
    )
```

```python
import functools
import math

import jax
import jax.numpy as jnp
import ml_dtypes
import numpy as np
from jax import lax
from jax.experimental import pallas as pl
from jax.experimental.pallas import tpu as pltpu
from jax.sharding import PartitionSpec as P


TILE = 16
LANES = 128
F32 = jnp.float32
BF16 = jnp.bfloat16


def dot(a, b, dims=((1,), (0,))):
    return lax.dot_general(a, b, (dims, ((), ())), preferred_element_type=F32)


def split(value, parts):
    terms = []
    for _ in range(parts):
        term = value.astype(BF16)
        terms.append(term)
        value = value - term.astype(F32)
    return terms


def split_table(value, parts):
    terms = []
    for _ in range(parts):
        term = float(np.float32(value).astype(ml_dtypes.bfloat16))
        terms.append(term)
        value = value - term
    return terms


def wave(phase, parts):
    near = jnp.minimum(phase, 16 - phase)
    step = jnp.minimum(near, 8 - near)
    flip = near > 4
    steps = [split_table(math.cos(2.0 * math.pi * k / 16.0), parts) for k in range(4)]
    terms = []
    for p in range(parts):
        value = jnp.zeros(phase.shape, F32)
        for k in range(4):
            value = jnp.where(step == k, float(steps[k][p]), value)
        terms.append(jnp.where(flip, -value, value))
    return terms


def waves(phase, parts):
    phase = phase & 15
    return wave(phase, parts), wave((phase + 12) & 15, parts)


def turn(re, im, k, n):
    if k == 0:
        return re, im
    if 4 * k == n:
        return im, -re
    if 8 * k == n:
        half = math.sqrt(0.5)
        return (re + im) * half, (im - re) * half
    if 8 * k == 3 * n:
        half = math.sqrt(0.5)
        return (im - re) * half, (re + im) * -half
    c, s = math.cos(2.0 * math.pi * k / n), math.sin(2.0 * math.pi * k / n)
    return re * c + im * s, im * c - re * s


def fft(re, im):
    n = len(re)
    if n == 1:
        return re, im
    er, ei = fft(re[0::2], im[0::2])
    our, oi = fft(re[1::2], im[1::2])
    half = n // 2
    xr, xi = [None] * n, [None] * n
    for k in range(half):
        tr, ti = turn(our[k], oi[k], k, n)
        xr[k], xi[k] = er[k] + tr, ei[k] + ti
        xr[k + half], xi[k + half] = er[k] - tr, ei[k] - ti
    return xr, xi


def tree(values):
    while len(values) > 1:
        half = len(values) // 2
        values = [a + b for a, b in zip(values[:half], values[half:])]
    return values[0]


def add_lists(a, b):
    return b if a is None else [x + y for x, y in zip(a, b)]


def side_kernel(dims, shift_ref, goal_ref, side_ref, raw_ref, words_ref):
    fl, nsc, T = dims
    odd = lax.rem(lax.axis_index("space"), 2)
    G = side_ref.shape[2] // LANES
    for l in range(fl):
        for c in range(2):
            row = shift_ref[l, c]
            if T < LANES:
                row = jnp.concatenate([row, jnp.zeros((1, LANES - T), jnp.int32)], axis=1)
            words_ref[l * 2 + c : l * 2 + c + 1, :] = row
    far, core = [], []
    for c in range(nsc):
        raw_ref[...] = goal_ref[:, :, c * LANES : (c + 1) * LANES].astype(F32).reshape(256, LANES)
        edge = raw_ref[pl.ds(7 * odd, 32, stride=8), :]
        far += [edge[:16], edge[16:]]
        edge = raw_ref[pl.ds(7 - 7 * odd, 32, stride=8), :]
        core += [edge[:16], edge[16:]]
    words = words_ref[...].astype(F32)
    words = [words[16 * k : 16 * k + 16] for k in range(words.shape[0] // 16)]
    blocks = []
    for group in (words + core, far + words):
        blocks += group + [jnp.zeros((TILE, LANES), F32)] * (-len(group) % G)
    for k, block in enumerate(blocks):
        at = (k % G) * LANES
        side_ref[k // G, :, at : at + LANES] = block.astype(BF16)


def target_kernel(dims, *refs):
    nf, nsc = dims
    goal_refs, goal_ref, raw_ref = refs[:nf], refs[nf], refs[nf + 1]
    fr = lax.axis_index("frame")
    for j in range(nf):
        at = pl.multiple_of(lax.rem(fr + j, nf) * (nsc * LANES), LANES)
        for c in range(nsc):
            cols = slice(c * LANES, (c + 1) * LANES)
            raw_ref[...] = goal_refs[j][:, :, cols].astype(F32).reshape(256, LANES)
            to = pl.ds(pl.multiple_of(at + c * LANES, LANES), LANES)
            for r in range(8):
                goal_ref[r, :, to] = raw_ref[pl.ds(r, 32, stride=8), :]


def table_kernel(weight_ref, *refs):
    fwd_ref, fwdl_ref, inv_ref, invl_ref, part_ref, wideh_ref, widel_ref = refs[:7]
    big_ref, bigt_ref, rows_ref = refs[7:]
    lane = lax.broadcasted_iota(jnp.int32, (TILE, LANES), 1)
    line = lax.broadcasted_iota(jnp.int32, (TILE, LANES), 0)
    cos, sin = waves(line * (lane & 15), 3)
    for k in range(8):
        at = slice(k * TILE, (k + 1) * TILE)
        mid = slice(128 + k * TILE, 128 + (k + 1) * TILE)
        here = (lane // TILE) == k
        c = [jnp.where(here, v, 0.0).astype(BF16) for v in cos]
        d = [jnp.where(here, v, 0.0).astype(BF16) for v in sin]
        fwd_ref[at, :] = jnp.concatenate([c[0], d[0]], axis=1)
        fwd_ref[mid, :] = jnp.concatenate([c[1], d[1]], axis=1)
        fwdl_ref[at, :] = jnp.concatenate([c[2], d[2]], axis=1)
        inv_ref[at, :] = jnp.concatenate([c[0], c[1]], axis=1)
        inv_ref[mid, :] = jnp.concatenate([-d[0], -d[1]], axis=1)
        invl_ref[at, :] = c[2]
        invl_ref[mid, :] = -d[2]
    line = lax.broadcasted_iota(jnp.int32, (256, 256), 0)
    column = lax.broadcasted_iota(jnp.int32, (256, 256), 1)
    source = 2 * (column & 127) + (column >> 7)
    part_ref[...] = jnp.where(line == source, 1.0, 0.0).astype(BF16)
    lane8 = lax.broadcasted_iota(jnp.int32, (8, LANES), 1)
    line8 = lax.broadcasted_iota(jnp.int32, (8, LANES), 0)
    empty = jnp.zeros((8, LANES), F32)
    for q in range(2):
        cos, sin = waves((2 * line8 + q) * (lane8 & 15), 2)
        for t in range(0, 16, 2):
            for ref, c, d in ((wideh_ref, cos[0], sin[0]), (widel_ref, cos[1], sin[1])):
                rows = []
                for u in (t, t + 1):
                    here = lane8 // TILE == u % 8
                    row = []
                    for v in (c, d):
                        v = jnp.where(here, v, 0.0)
                        row += [v, empty] if u < 8 else [empty, v]
                    rows.append(jnp.concatenate(row, axis=1))
                at = q * 128 + t * 8
                ref[at : at + 16, :] = jnp.concatenate(rows, axis=0).astype(BF16)

    weight = weight_ref[...].astype(F32)
    weight = jnp.concatenate([weight, jnp.zeros((32, LANES - 36), F32)], axis=1)
    halves = []
    for h in range(2):
        at = lax.broadcasted_iota(jnp.int32, (32, LANES), 1) + h * LANES
        group = (at * 171) >> 12
        row = at - 24 * group
        q = jnp.where(group >= 3, 1, 0)
        tap = (3 * (row >> 1) + group - 3 * q) * 4 + 2 * (row & 1) + q
        valid = (row < 6) & (group < 6)
        taken = jnp.take_along_axis(weight, jnp.where(valid, tap, 0), axis=1)
        halves.append(jnp.where(valid, taken, 0.0))
    base = jnp.concatenate(halves, axis=1)
    for sy in range(10):
        moved = pltpu.roll(base, 2 * sy, 1) if sy else base
        big_ref[sy * 32 : (sy + 1) * 32, :] = moved.astype(BF16)

    turned = jnp.transpose(jnp.concatenate([weight] * 4, axis=0))
    rows_ref[...] = jnp.zeros_like(rows_ref)
    for q in range(2):
        for b in range(3):
            for j in range(6):
                tap = (3 * (j // 2) + b) * 4 + 2 * (j % 2) + q
                rows_ref[q * 3 + b, 16 + j : 17 + j, :] = turned[tap : tap + 1, :]
    quarter = lax.broadcasted_iota(jnp.int32, (TILE, LANES), 1) // 32
    for k in range(6):
        for tile in range(3):
            value = jnp.zeros((TILE, LANES), F32)
            for u in range(4):
                sy = 4 * tile + u
                if sy < 10:
                    block = rows_ref[k, 20 - 2 * sy : 36 - 2 * sy, :]
                    value = jnp.where(quarter == u, block, value)
            width = 64 if tile == 2 else LANES
            at = tile * LANES
            bigt_ref[k * TILE : (k + 1) * TILE, at : at + width] = value[:, :width].astype(BF16)


def side_block(ref, plane, k):
    per = ref.shape[2] // LANES
    at = (k % per) * LANES
    return ref[plane + k // per, :, at : at + LANES].astype(F32)


def merge_kernel(dims, *refs):
    nf, fl, G, _, nsc = dims
    F = nf * fl
    near_refs, far_refs, refs = refs[:nf], refs[nf : 2 * nf], refs[2 * nf :]
    var_ref, fwd_ref, fwdl_ref, inv_ref, invl_ref = refs[:5]
    pack_ref, pc_ref, far_ref, h_ref = refs[5:9]
    x_ref, idx_ref, p_ref, q_ref, xs_ref, own_ref, words_ref, own_sm, far_sm, sems = refs[9:]
    s = lax.axis_index("space")
    fr = lax.axis_index("frame")
    odd = lax.rem(s, 2)

    wb = -(-2 * fl // 16)
    for group, ref, at in ((near_refs, own_ref, 0), (far_refs, words_ref, 2 * nsc)):
        for j in range(nf):
            words = [side_block(group[j], 2 * fl, at + k) for k in range(wb)]
            words = jnp.concatenate(words, axis=0)[: 2 * fl].astype(jnp.int32)
            ref[2 * fl * j : 2 * fl * (j + 1), :] = words
    moves = (
        pltpu.make_async_copy(own_ref, own_sm, sems.at[0]),
        pltpu.make_async_copy(words_ref, far_sm, sems.at[1]),
    )
    for move in moves:
        move.start()

    slots = (
        (near_refs, 0, 2 - odd),
        (near_refs, fl, 3 - 3 * odd),
        (far_refs, 0, 1 + odd),
        (far_refs, fl, 3 * odd),
    )
    for group, start, slot in slots:
        for j in range(nf):
            for l in range(fl):
                rows = group[j][start + l].astype(F32)
                for g in range(G):
                    block = rows[:, g * LANES : (g + 1) * LANES]
                    at = pl.ds(pl.multiple_of(slot * TILE, TILE), TILE)
                    x_ref[(j * fl + l) * G + g, at, :] = block

    spot = lax.broadcasted_iota(jnp.int32, (8, LANES), 1)
    for which, ref in enumerate((own_ref, words_ref)):
        for f in range(F):
            row = jnp.broadcast_to(ref[2 * f + 1 : 2 * f + 2, :], (8, LANES))
            for g in range(G):
                moved = jnp.take_along_axis(row, 8 * g + spot // TILE, axis=1)
                idx_ref[which, f * G + g] = (moved + spot) & (LANES - 1)
    for j in range(nf):
        for k in range(2 * nsc):
            at = 4 * G + (j * 2 * nsc + k) * TILE
            block = side_block(near_refs[j], 2 * fl, wb + k)
            pc_ref[at : at + TILE, :] = block.astype(BF16)

    lane = lax.broadcasted_iota(jnp.int32, (TILE, LANES), 1)
    kind = (lane // TILE) % 4
    per = 16 // G
    chunks = F * G // 16
    rows_out = max(G, 8)
    fold = TILE // rows_out
    zero = jnp.zeros((TILE, LANES), F32)

    def place(f):
        if nf == 2:
            return f
        return lax.rem(f // fl + nf - fr, nf) * fl + f % fl

    first = lax.rem(nf - fr, nf) * fl
    log_var = var_ref[...]
    variances = []
    for k in range(16):
        row = jnp.broadcast_to(log_var[k // 8 : k // 8 + 1], (8, LANES))
        row = jnp.take_along_axis(row, (k % 8) * TILE + spot % TILE, axis=1)
        variances.append(jnp.concatenate([row, row], axis=0))

    def tile_row(which, row0, dy_ref, c, carry):
        sums = carry[0] if carry is not None else None
        blocks = []
        for q in range(16):
            g = q % G
            f = place(c * per + q // G)

            def load(t, group):
                if group < 0 or group >= G:
                    return zero
                start = row0 + dy_ref[2 * f, 8 * g + t]
                return x_ref[f * G + group, pl.ds(start, TILE), :]

            idx = idx_ref[which, f * G + g]
            idx = jnp.concatenate([idx, idx], axis=0)
            mixes = (
                jnp.where(
                    lane < 40,
                    load(0, g),
                    jnp.where(lane < 104, load(4, g), load(0, g - 1)),
                ),
                jnp.where(lane < 56, load(1, g), load(5, g)),
                jnp.where(lane < 72, load(2, g), load(6, g)),
                jnp.where(
                    lane < 24,
                    load(7, g + 1),
                    jnp.where(lane < 88, load(3, g), load(7, g)),
                ),
            )
            moved = [jnp.take_along_axis(m, idx, axis=1) for m in mixes]
            blocks.append(
                jnp.where(
                    kind < 2,
                    jnp.where(kind == 0, moved[0], moved[1]),
                    jnp.where(kind == 2, moved[2], moved[3]),
                )
            )
        base = [x_ref[first * G + g, pl.ds(pl.multiple_of(row0, TILE), TILE), :] for g in range(G)]
        both = jnp.concatenate(blocks + base, axis=0).astype(BF16)
        pq = dot(jnp.concatenate([both, both], axis=1), fwd_ref[...]) + dot(both, fwdl_ref[...])
        for q in range(16):
            rows = slice(q * TILE, (q + 1) * TILE)
            ref_rows = slice(256 + (q % G) * TILE, 256 + (q % G + 1) * TILE)
            diff = pq[ref_rows] - pq[rows]
            p_ref[which, rows, :] = diff[:, :LANES]
            q_ref[which, rows, :] = -diff[:, LANES:]
        re, im = fft(
            [p_ref[which, pl.ds(n, 16, stride=16), :] for n in range(16)],
            [q_ref[which, pl.ds(n, 16, stride=16), :] for n in range(16)],
        )
        out = [[], [], [], []]
        for k in range(16):
            energy = re[k] * re[k] + im[k] * im[k]
            weight = energy / (energy + variances[k])
            wr = weight * re[k]
            wi = weight * im[k]
            vals = (wr, wi)
            if which == 0:
                rest = 1.0 - weight
                vals = (wr, wi, wr * rest, wi * rest)
            for store, val in zip(out, vals):
                if fold == 2:
                    val = val[:8] + val[8:]
                store.append(val)
        flat = out[0] + out[1] + out[2] + out[3]
        return sums_of(sums, blocks), add_lists(carry[1] if carry is not None else None, flat)

    def sums_of(sums, blocks):
        return add_lists(sums, [tree(blocks[g::G]) for g in range(G)])

    def whole_row(which, row0, dy_ref):
        step = functools.partial(tile_row, which, row0, dy_ref)
        carry = step(0, None)
        if chunks > 1:
            carry = lax.fori_loop(1, chunks, step, carry)
        return carry

    moves[0].wait()
    sums, flat = whole_row(0, (2 - odd) * TILE, own_sm)
    for k in range(32):
        h_ref[k * rows_out : (k + 1) * rows_out, :] = flat[32 + k]
    moves[1].wait()
    far_sums, far_flat = whole_row(1, (1 + odd) * TILE, far_sm)

    vi, ur = fft(flat[16:32], flat[:16])
    far_vi, far_ur = fft(far_flat[16:32], far_flat[:16])
    at_odd = odd == 1
    ur += [jnp.where(at_odd, far_ur[k], far_ur[12 + k]) for k in range(4)]
    vi += [jnp.where(at_odd, far_vi[k], far_vi[12 + k]) for k in range(4)]
    uv = jnp.concatenate([jnp.concatenate(ur, axis=0), jnp.concatenate(vi, axis=0)], axis=1)
    m = 20 * rows_out
    terms = split(uv, 3)
    wide = dot(jnp.concatenate(terms, axis=0), inv_ref[...])
    pix = wide[:m, :LANES] + (wide[m : 2 * m, :LANES] + wide[:m, LANES:])
    pix = pix + (wide[2 * m :, :LANES] + wide[m : 2 * m, LANES:] + dot(terms[0], invl_ref[...]))
    xs_ref[...] = pix
    far_rows = []
    for g in range(G):
        val = xs_ref[pl.ds(g, 16, stride=rows_out), :]
        far = xs_ref[pl.ds(16 * rows_out + g, 4, stride=rows_out), :]
        for other in range(g + G, rows_out, G):
            val = val + xs_ref[pl.ds(other, 16, stride=rows_out), :]
            far = far + xs_ref[pl.ds(16 * rows_out + other, 4, stride=rows_out), :]
        pack_ref[g] = (sums[g] + val / 256.0) / F
        far_sum = jnp.where(at_odd, far_sums[g][0:4], far_sums[g][12:16])
        far_rows.append((far_sum + far / 256.0) / F)
    far_ref[...] = jnp.concatenate(far_rows, axis=0)
    low = jnp.concatenate([pack_ref[g, 0:4, :] for g in range(G)], axis=0)
    high = jnp.concatenate([pack_ref[g, 12:16, :] for g in range(G)], axis=0)
    pc_ref[0 : 4 * G, :] = jnp.where(at_odd, low, high).astype(BF16)


def demosaic_kernel(dims, pack_ref, pc_ref, far_ref, goals_ref, h_ref, *refs):
    nf, fl, G, nsc, n_space, inv_pixels = dims
    F = nf * fl
    W = G * LANES
    half = W // 2
    far_refs, refs = refs[:nf], refs[nf:]
    big_ref, bigt_ref, offs_ref, part_ref, wideh_ref, widel_ref = refs[:6]
    out_ref, goal_ref, mm_ref, p_ref, q_ref, ns_ref = refs[6:]
    s = lax.axis_index("space")
    fr = lax.axis_index("frame")
    odd = lax.rem(s, 2)
    rows_out = max(G, 8)

    lead = G * 4
    for j in range(nf):
        at = pl.multiple_of(lax.rem(fr + j, nf) * (nsc * LANES), LANES)
        for c in range(nsc):
            first = (j * nsc + c) * 32
            to = pl.ds(pl.multiple_of(at + c * LANES, LANES), LANES)
            goal_ref[1 - odd, :, to] = pc_ref[lead + first : lead + first + 32, :].astype(F32)
            blocks = [side_block(far_refs[j], 2 * fl, 2 * c + k) for k in range(2)]
            goal_ref[odd, :, to] = jnp.concatenate(blocks, axis=0)

    near = pc_ref[0:lead, :].astype(F32)
    far = far_ref[...]
    low = jnp.where(odd == 1, near, far)
    high = jnp.where(odd == 1, far, near)
    for g in range(G):
        mm_ref[g, 0:4, :] = low[4 * g : 4 * g + 4]
        mm_ref[g, 4:20, :] = pack_ref[g]
        mm_ref[g, 20:24, :] = high[4 * g : 4 * g + 4]
    pairs = jnp.concatenate(
        [jnp.concatenate([mm_ref[2 * h], mm_ref[2 * h + 1]], axis=1) for h in range(G // 2)],
        axis=0,
    )
    parted = dot(pairs.astype(BF16), part_ref[...])
    site = lax.broadcasted_iota(jnp.int32, (24, half), 1)
    pieces = []
    for q in range(2):
        plane = jnp.concatenate(
            [parted[24 * h : 24 * h + 24, q * 128 : (q + 1) * 128] for h in range(G // 2)], axis=1
        )
        pieces.append(jnp.where(site == 0, 0.0, pltpu.roll(plane, 1, 1)))
        pieces.append(plane)
        pieces.append(jnp.where(site == half - 1, 0.0, pltpu.roll(plane, half - 1, 1)))
    pieces.append(jnp.zeros((112, half), F32))
    taps = jnp.concatenate(pieces, axis=0).astype(BF16)

    preact = dot(big_ref[...], taps)
    diag = lax.broadcasted_iota(jnp.int32, (32, LANES), 0) == lax.broadcasted_iota(
        jnp.int32, (32, LANES), 1
    )
    offs = jnp.where(diag, jnp.broadcast_to(offs_ref[2:3, :], (32, LANES)), 0.0)
    offs = jnp.broadcast_to(jnp.sum(offs, axis=1, keepdims=True), (32, half))
    bias = jnp.zeros((32, half), F32)
    slopes = []
    for sy in range(10):
        v = preact[sy * 32 : sy * 32 + 32] + offs
        sig = jax.nn.sigmoid(v)
        goal = goal_ref[0] if sy == 0 else goal_ref[1] if sy == 9 else goals_ref[sy - 1]
        slope = (v * sig - goal) * inv_pixels * (sig * (1.0 + v * (1.0 - sig)))
        if sy == 0:
            slope = jnp.where(s == 0, 0.0, slope)
        elif sy == 9:
            slope = jnp.where(s == n_space - 1, 0.0, slope)
        else:
            bias = bias + slope
        slopes.append(slope)
    slope_bf = jnp.concatenate(slopes, axis=0).astype(BF16)

    gt = dot(bigt_ref[...], slope_bf)
    site16 = lax.broadcasted_iota(jnp.int32, (TILE, half), 1)
    planes = []
    for q in range(2):
        left, mid, right = (gt[(q * 3 + b) * 16 : (q * 3 + b) * 16 + 16] for b in range(3))
        planes.append(
            mid
            + jnp.where(site16 == half - 1, 0.0, pltpu.roll(left, half - 1, 1))
            + jnp.where(site16 == 0, 0.0, pltpu.roll(right, 1, 1))
        )
    grad = jnp.concatenate(
        [
            jnp.concatenate([p[:, h * 128 : (h + 1) * 128] for p in planes], axis=1)
            for h in range(G // 2)
        ],
        axis=0,
    )
    m = grad.shape[0]
    terms = split(grad, 2)
    pq = dot(jnp.concatenate(terms, axis=0), wideh_ref[...])
    pq = pq[:m] + (pq[m:] + dot(terms[0], widel_ref[...]))
    for r in range(rows_out):
        g = r % G
        rows = slice((g // 2) * TILE, (g // 2 + 1) * TILE)
        c0 = (g % 2) * LANES
        p_ref[r * TILE : (r + 1) * TILE, :] = pq[rows, c0 : c0 + LANES]
        q_ref[r * TILE : (r + 1) * TILE, :] = -pq[rows, 256 + c0 : 256 + c0 + LANES]
    gre, gim = fft(
        [p_ref[pl.ds(n, rows_out, stride=16), :] for n in range(16)],
        [q_ref[pl.ds(n, rows_out, stride=16), :] for n in range(16)],
    )
    for k in range(16):
        rows = slice(k * rows_out, (k + 1) * rows_out)
        rows_im = slice((16 + k) * rows_out, (17 + k) * rows_out)
        ns_ref[rows, :] = gre[k] * h_ref[rows, :] + gim[k] * h_ref[rows_im, :]
    noise = ns_ref[pl.ds(0, 16, stride=rows_out), :]
    for r in range(1, rows_out):
        noise = noise + ns_ref[pl.ds(r, 16, stride=rows_out), :]
    noise = noise * (-1.0 / (256.0 * F))
    for step in (64, 32, 16):
        noise = noise + pltpu.roll(noise, step, 1)

    prod = dot(slope_bf[32:288], taps, ((1,), (1,)))
    gw = jnp.zeros((32, 256), F32)
    for sy in range(1, 9):
        gw = gw + pltpu.roll(prod[(sy - 1) * 32 : sy * 32], 256 - 2 * sy, 1)
    tap = lax.broadcasted_iota(jnp.int32, (32, LANES), 1)
    pair = tap >> 2
    a = (pair * 11) >> 5
    source = ((tap & 1) * 3 + pair - 3 * a) * 24 + 2 * a + ((tap >> 1) & 1)
    source = jnp.where(tap < 36, source, 0)
    lower_part = jnp.take_along_axis(gw[:, :LANES], source & 127, axis=1)
    upper_part = jnp.take_along_axis(gw[:, LANES:], source & 127, axis=1)
    gw = jnp.where(source < LANES, lower_part, upper_part)
    gw = jnp.where(tap == 36, jnp.sum(bias, axis=1, keepdims=True), gw)
    gw = jnp.where(tap < 37, gw, 0.0)
    first = gw[0:8] + (pltpu.roll(gw[8:16], 37, 1) + pltpu.roll(gw[16:24], 74, 1))
    group = lax.broadcasted_iota(jnp.int32, (8, LANES), 1) // TILE
    second = jnp.where(group == 5, noise[:8], jnp.where(group == 6, noise[8:], gw[24:32]))
    out_ref[...] = jnp.concatenate([first, second], axis=0)


def store_merged(nf, pack_ref, merged_ref):
    own = pack_ref.shape[0] // nf
    fr = lax.axis_index("frame")
    for k in range(own):
        merged_ref[:, k * LANES : (k + 1) * LANES] = pack_ref[fr * own + k]


def last_sum(own_ref, got_ref, weight_ref, bias_ref, noise_ref):
    total = own_ref[...] + got_ref[...]
    first, second = total[:8], total[8:]
    gw = jnp.concatenate(
        [first, pltpu.roll(first, LANES - 37, 1), pltpu.roll(first, LANES - 74, 1), second], axis=0
    )
    weight_ref[...] = gw[:, :36]
    line = lax.broadcasted_iota(jnp.int32, (32, LANES), 0)
    lane = lax.broadcasted_iota(jnp.int32, (32, LANES), 1)
    bias = jnp.where(line == lane, jnp.broadcast_to(gw[:, 36:37], (32, LANES)), 0.0)
    bias_ref[...] = jnp.sum(bias, axis=0, keepdims=True)[:, :32]
    group = lane[:8] // TILE
    for k in range(2):
        part = jnp.where(group == 5 + k, second, 0.0)
        for step in (16, 32, 64):
            part = part + pltpu.roll(part, step, 1)
        part = jnp.where(group == line[:8], part, 0.0)
        noise_ref[k : k + 1, :] = jnp.sum(part, axis=0, keepdims=True)


def involution(value, count, step, first):
    pairs = []
    for i in range(first, count):
        j = ((i - first) ^ step) + first
        if j < count:
            pairs.append((i, j))
    return lax.ppermute(value, "space", pairs)


def sum_space(value, count):
    bits = count.bit_length() - 1
    assert 1 << bits == count
    stages = []
    at = 0
    while at < bits:
        width = 2 if at == 1 and bits - at >= 3 else 1
        stages.append([m << at for m in range(1, 1 << width)])
        at += width
    for masks in stages[:-1]:
        got = []
        for m in masks:
            got.append(lax.ppermute(value, "space", [(i, i ^ m) for i in range(count)]))
        value = value + got[0]
        if len(got) == 3:
            value = value + (got[1] + got[2])
    (mask,) = stages[-1]
    got = lax.ppermute(value, "space", [(i, i ^ mask) for i in range(count)])
    return value, got


def call(body, args, outs, scratch):
    vm = pl.BlockSpec(memory_space=pltpu.VMEM)
    sizes = [int(np.prod(a.shape)) * a.dtype.itemsize for a in list(args) + list(outs)]
    sizes += [int(np.prod(a.shape)) * 4 for a in scratch if a.memory_space == pltpu.VMEM]
    return pl.pallas_call(
        body,
        out_shape=tuple(outs),
        in_specs=[vm] * len(args),
        out_specs=(vm,) * len(outs),
        scratch_shapes=scratch,
        compiler_params=pltpu.CompilerParams(vmem_limit_bytes=sum(sizes) + (12 << 20)),
    )(*args)


def shards(raw, shifts, weight, offset, log_var, goal):
    nf = lax.axis_size("frame")
    n_space = lax.axis_size("space")
    fl, band_rows, W = raw.shape
    T = shifts.shape[3]
    channels, _, ws = goal.shape
    G = W // LANES
    F = nf * fl
    nsc = ws // LANES
    inv_pixels = 1.0 / (band_rows * n_space * W // 4)
    rows_out = max(G, 8)

    def from_frame(value, j):
        return lax.ppermute(value, "frame", [(i, (i - j) % nf) for i in range(nf)])

    def pieces(value):
        return [value] + [from_frame(value, j) for j in range(1, nf)]

    shape = jax.ShapeDtypeStruct
    words = -(-2 * fl // 16)
    planes = -(-(2 * nsc + words) // G)
    raw_core = involution(raw, n_space, 1, 0)
    (side,) = call(
        functools.partial(side_kernel, (fl, nsc, T)),
        [shifts, goal],
        [shape((2 * planes, TILE, W), BF16)],
        [pltpu.VMEM((256, LANES), F32), pltpu.VMEM((16 * words, LANES), jnp.int32)],
    )
    near = lax.optimization_barrier(jnp.pad(raw, ((0, fl + planes), (0, 0), (0, 0))))
    near = lax.dynamic_update_slice(near, side[:planes], (2 * fl, 0, 0))
    near = lax.dynamic_update_slice(near, raw_core, (fl, 0, 0))
    far_own = jnp.concatenate([near[: 2 * fl], side[planes:]], axis=0)
    far_own = involution(far_own, n_space, 1, 1)
    nears = pieces(near)
    *tables, big, bigt = call(
        table_kernel,
        [weight],
        [
            shape((256, 256), BF16),
            shape((128, 256), BF16),
            shape((256, 256), BF16),
            shape((256, 128), BF16),
            shape((256, 256), BF16),
            shape((256, 512), BF16),
            shape((256, 512), BF16),
            shape((320, 256), BF16),
            shape((96, 320), BF16),
        ],
        [pltpu.VMEM((6, 40, LANES), F32)],
    )
    small = jnp.concatenate(
        [jnp.exp(log_var), offset, jnp.zeros((6 * LANES - channels,), F32)]
    ).reshape(8, LANES)
    fars = pieces(far_own)
    goals = pieces(goal)
    (site_goals,) = call(
        functools.partial(target_kernel, (nf, nsc)),
        goals,
        [shape((8, channels, W // 2), F32)],
        [pltpu.VMEM((256, LANES), F32)],
    )

    pack, pc, far, moments = call(
        functools.partial(merge_kernel, (nf, fl, G, T, nsc)),
        [*nears, *fars, small, *tables[:4]],
        [
            shape((G, TILE, LANES), F32),
            shape((4 * G + nf * nsc * channels, LANES), BF16),
            shape((4 * G, LANES), F32),
            shape((32 * rows_out, LANES), F32),
        ],
        [
            pltpu.VMEM((F * G, 4 * TILE, LANES), F32),
            pltpu.VMEM((2, F * G, 8, LANES), jnp.int32),
            pltpu.VMEM((2, 256, LANES), F32),
            pltpu.VMEM((2, 256, LANES), F32),
            pltpu.VMEM((20 * rows_out, LANES), F32),
            pltpu.VMEM((2 * F, LANES), jnp.int32),
            pltpu.VMEM((2 * F, LANES), jnp.int32),
            pltpu.SMEM((2 * F, LANES), jnp.int32),
            pltpu.SMEM((2 * F, LANES), jnp.int32),
            pltpu.SemaphoreType.DMA((2,)),
        ],
    )
    pc = involution(pc, n_space, 1, 0)
    (partial,) = call(
        functools.partial(demosaic_kernel, (nf, fl, G, nsc, n_space, inv_pixels)),
        [pack, pc, far, site_goals, moments, *fars, big, bigt, small, *tables[4:]],
        [shape((16, LANES), F32)],
        [
            pltpu.VMEM((2, channels, W // 2), F32),
            pltpu.VMEM((G, 24, LANES), F32),
            pltpu.VMEM((rows_out * TILE, LANES), F32),
            pltpu.VMEM((rows_out * TILE, LANES), F32),
            pltpu.VMEM((rows_out * TILE, LANES), F32),
        ],
    )
    (merged,) = call(functools.partial(store_merged, nf), [pack], [shape((TILE, W // nf), F32)], [])
    grad_weight, grad_bias, grad_noise = call(
        last_sum,
        sum_space(partial, n_space),
        [
            shape((channels, 36), F32),
            shape((1, channels), F32),
            shape((2, LANES), F32),
        ],
        [],
    )
    return merged, grad_weight, grad_bias.reshape(channels), grad_noise.reshape(256)


def solution(mesh):
    placed = (
        P("frame", "space", None),
        P("frame", None, "space", None),
        P(),
        P(),
        P(),
        P(None, "space", "frame"),
    )

    return jax.shard_map(
        shards,
        mesh=mesh,
        in_specs=placed,
        out_specs=(P("space", "frame"), P(), P(), P()),
        check_vma=False,
    )
```
